32 devices in a mesh: seq: 4 (over y, core), rows: 8 (over z, x).
Axes of the slice: x: 2, y: 2, z: 4, core: 2. Of those that a mesh axis runs over, the one named last changes fastest.
Arguments:
- tokens: bfloat16 [8, 1024, 2048], P('rows', 'seq'), may hold values from -6 to 6
- doc_starts: int32 [8, 1024], P('rows', 'seq'), may hold values 0 or 1
- cotangent: bfloat16 [8, 1024, 2048], P('rows', 'seq'), may hold values from -6 to 6
- norm_first: bfloat16 [2048], replicated, may hold values from 0.5 to 1.5
- norm_second: bfloat16 [2048], replicated, may hold values from 0.5 to 1.5
- w_query: bfloat16 [2048, 2048], P('rows'), may hold values from -0.125 to 0.125
- w_key: bfloat16 [2048, 512], P('rows'), may hold values from -0.125 to 0.125
- w_value: bfloat16 [2048, 512], P('rows'), may hold values from -0.125 to 0.125
- w_out: bfloat16 [2048, 2048], P('rows'), may hold values from -0.75 to 0.75
- w_gate_up: bfloat16 [2, 2048, 8192], P(None, None, 'rows'), may hold values from -0.125 to 0.125
- w_down: bfloat16 [8192, 2048], P('rows'), may hold values from -0.0625 to 0.0625
- query_in: bfloat16 [2048, 8], replicated, may hold values from -0.125 to 0.125
- query_out: bfloat16 [8, 2048], replicated, may hold values from -1 to 1
- key_in: bfloat16 [2048, 8], replicated, may hold values from -0.125 to 0.125
- key_out: bfloat16 [8, 512], replicated, may hold values from -1 to 1
- value_in: bfloat16 [2048, 8], replicated, may hold values from -0.125 to 0.125
- value_out: bfloat16 [8, 512], replicated, may hold values from -1 to 1
- proj_in: bfloat16 [2048, 8], replicated, may hold values from -0.75 to 0.75
- proj_out: bfloat16 [8, 2048], replicated, may hold values from -1 to 1
- map_query: bfloat16 [32, 64, 64], replicated, may hold values from -0.75 to 0.75
- map_key: bfloat16 [8, 64, 64], replicated, may hold values from -0.75 to 0.75
- window_logit: float32 [32], replicated, may hold values from -1 to 3
Outputs:
- block_out: bfloat16 [8, 1024, 2048], P('rows', 'seq')
- grad_tokens: float32 [8, 1024, 2048], P('rows', 'seq')
- grad_norm_first: float32 [2048], P('seq')
- grad_norm_second: float32 [2048], P('seq')
- grad_query_in: float32 [2048, 8], P('seq')
- grad_query_out: float32 [8, 2048], P(None, 'seq')
- grad_key_in: float32 [2048, 8], P('seq')
- grad_key_out: float32 [8, 512], P(None, 'seq')
- grad_value_in: float32 [2048, 8], P('seq')
- grad_value_out: float32 [8, 512], P(None, 'seq')
- grad_proj_in: float32 [2048, 8], P('seq')
- grad_proj_out: float32 [8, 2048], P(None, 'seq')
- grad_map_query: float32 [32, 64, 64], P('seq')
- grad_map_key: float32 [8, 64, 64], P(None, 'seq')
- grad_window_logit: float32 [32], P('seq')
The draws below stay inside these ranges and needn't reach their ends.
All inputs are finite; a program needn't handle non-finite values. No bound on the sum of `doc_starts` on one device may be relied on, other than what follows from the above.
Results may differ from the reference program's by a relative error of at most 0.025.
Values may be sent and summed in bfloat16 or wider, within the bound.
No kernel may reach another device: no remote copies, remote signals or barrier semaphores. Data moves between devices by JAX's collectives and lax.ppermute only.
A program may use at most 448 MiB of HBM per device.

```python
import jax
import jax.numpy as jnp
from jax import lax

D = 2048
HEADS = 32
KV_HEADS = 8
HEAD = 64
FF = 8192
RANK = 8
WINDOW = 64
TOK_DEV = 256
KVD = 512
LEN = 1024
NROWS = 8


def place_ends(values, rng, low, largest):
    extent = values.shape
    index_at = [jax.random.randint(jax.random.fold_in(rng, axis), (), 0, extent[axis]) for axis in range(len(extent))]
    values = values.at[tuple(index_at)].set(low)
    longest = extent.index(max(extent))
    index_at[longest] = (index_at[longest] + 1) % extent[longest]
    return values.at[tuple(index_at)].set(largest)


def block_levels(rng, shape, pieces, least, top_value):
    level = 1.0
    for dim, shards_of in pieces:
        steps = jax.random.uniform(jax.random.fold_in(jax.random.fold_in(rng, 6), dim), (shards_of,), jnp.float32, least / len(pieces), top_value / len(pieces))
        level = level * jnp.repeat(jnp.exp(steps), shape[dim] // shards_of).reshape((-1,) + (1,) * (len(shape) - 1 - dim))
    return level


def scatter_about(key, shape, spread, most, pieces=(), kind=jnp.bfloat16):
    entries = jax.random.normal(key, shape, jnp.float32) * spread
    if len(pieces) > 0:
        entries = block_levels(key, shape, pieces, -0.22, 0.18) * entries
    return jnp.clip(entries, min=-most, max=most).astype(kind)


def setup_inputs(seed: int = 0) -> dict:
    key_of = jax.random.split(jax.random.key(seed), 23)
    return {
        "tokens": scatter_about(key_of[0], (NROWS, LEN, D), 1.0, 6.0, ((0, 8), (1, 4))),
        "doc_starts": place_ends((jax.random.randint(key_of[1], (NROWS, LEN), 0, TOK_DEV * 4) < 1).astype(jnp.int32), jax.random.fold_in(key_of[1], 1), 0, 1),
        "cotangent": scatter_about(key_of[2], (NROWS, LEN, D), 1.0, 6.0, ((0, 8), (1, 4))),
        "norm_first": jnp.clip(1.0 + 0.1 * jax.random.normal(key_of[3], (D,), jnp.float32), 0.5, 1.5).astype(jnp.bfloat16),
        "norm_second": jnp.clip(1.0 + 0.1 * jax.random.normal(key_of[4], (D,), jnp.float32), 0.5, 1.5).astype(jnp.bfloat16),
        "w_query": scatter_about(key_of[5], (D, D), D ** -0.5, 0.125, ((0, 8),)),
        "w_key": scatter_about(key_of[6], (D, KVD), D ** -0.5, 0.125, ((0, 8),)),
        "w_value": scatter_about(key_of[7], (D, KVD), D ** -0.5, 0.125, ((0, 8),)),
        "w_out": scatter_about(key_of[8], (D, D), (D // 32) ** -0.5, 0.75, ((0, 8),)),
        "w_gate_up": scatter_about(key_of[9], (2, D, FF), D ** -0.5, 0.125, ((2, 8),)),
        "w_down": scatter_about(key_of[10], (FF, D), FF ** -0.5, 0.0625, ((0, 8),)),
        "query_in": scatter_about(key_of[11], (D, RANK), D ** -0.5, 0.125),
        "query_out": scatter_about(key_of[12], (RANK, D), (4 * RANK) ** -0.5, 1.0),
        "key_in": scatter_about(key_of[13], (D, RANK), D ** -0.5, 0.125),
        "key_out": scatter_about(key_of[14], (RANK, KVD), (4 * RANK) ** -0.5, 1.0),
        "value_in": scatter_about(key_of[15], (D, RANK), D ** -0.5, 0.125),
        "value_out": scatter_about(key_of[16], (RANK, KVD), (4 * RANK) ** -0.5, 1.0),
        "proj_in": scatter_about(key_of[17], (D, RANK), (D // 32) ** -0.5, 0.75),
        "proj_out": scatter_about(key_of[18], (RANK, D), (4 * RANK) ** -0.5, 1.0),
        "map_query": scatter_about(key_of[19], (HEADS, HEAD, HEAD), HEAD ** -0.5, 0.75),
        "map_key": scatter_about(key_of[20], (KV_HEADS, HEAD, HEAD), HEAD ** -0.5, 0.75),
        "window_logit": jnp.clip(jax.random.uniform(key_of[21], (HEADS,), jnp.float32, -1.0, 3.0), -1.0, 3.0),
    }


EPSILON = 1e-05
THETA = 500000.0

@jax.custom_vjp
def low(v):
    return lax.optimization_barrier(v.astype(jnp.bfloat16)).astype(jnp.float32)

@jax.custom_vjp
def low_back(v):
    return v

def low_keep(v):
    return (low(v), None)

def low_pass(kept, grad):
    return (grad,)

def back_keep(v):
    return (v, None)

def back_low(kept, grad):
    return (low(grad),)
low.defvjp(low_keep, low_pass)
low_back.defvjp(back_keep, back_low)

def matmul_high(left, right):
    return jnp.dot(left, right, precision=lax.Precision.HIGHEST)

def root_norm(values, gain):
    return values * lax.rsqrt(lax.optimization_barrier(jnp.mean(values * values, axis=-1, keepdims=True)) + EPSILON) * gain

def rotate(values, places):
    half_width = HEAD // 2
    inverse_freq = jnp.power(THETA, -(jnp.arange(half_width, dtype=jnp.float32) * 2.0 / HEAD))
    angles = places[:, None] * inverse_freq[None, :]
    cosine = jnp.cos(angles)[:, None, :]
    sine = jnp.sin(angles)[:, None, :]
    first = values[..., :half_width]
    second = values[..., half_width:]
    return jnp.concatenate([first * cosine - second * sine, second * cosine + first * sine], axis=-1)

def feature(rolled, maps):
    projected = low_back(jnp.einsum('thd,hde->the', rolled, maps, precision=lax.Precision.HIGHEST))
    return low(jnp.concatenate([jax.nn.softmax(projected, axis=-1), jax.nn.softmax(-projected, axis=-1)], axis=-1))

def attend(queries, keys, values, query_feats, key_feats, doc_ids, mixing):
    length = queries.shape[0]
    groups = HEADS // KV_HEADS
    block_rows = min(512, length)
    highest = lax.Precision.HIGHEST
    key_places = jnp.arange(length, dtype=jnp.int32)
    query_view = queries.reshape(length, KV_HEADS, groups, HEAD)
    feat_view = query_feats.reshape(length, KV_HEADS, groups, 2 * HEAD)
    mix_view = mixing.reshape(KV_HEADS, groups)
    scaling = HEAD ** (-0.5)

    def one_block(offset):
        query_block = lax.dynamic_slice_in_dim(query_view, offset, block_rows, 0)
        feat_block = lax.dynamic_slice_in_dim(feat_view, offset, block_rows, 0)
        block_ids = lax.dynamic_slice_in_dim(doc_ids, offset, block_rows, 0)
        distance = (offset + jnp.arange(block_rows, dtype=jnp.int32))[:, None] - key_places[None, :]
        same_doc = block_ids[:, None] == doc_ids[None, :]
        inside = (same_doc & (distance >= 0) & (distance < WINDOW))[:, None, None, :]
        beyond = (same_doc & (distance >= WINDOW))[:, None, None, :]
        scores = low_back(jnp.einsum('tgrd,jgd->tgrj', query_block, keys, precision=highest) * scaling)
        exp_scores = jnp.where(inside, jnp.exp(scores), 0.0)
        linear_w = jnp.where(beyond, jnp.einsum('tgrf,jgf->tgrj', feat_block, key_feats, precision=highest), 0.0)
        soft_part = low_back(jnp.einsum('tgrj,jgd->tgrd', low(exp_scores), values, precision=highest))
        linear = jnp.einsum('tgrj,jgd->tgrd', linear_w, values, precision=highest)
        totals = lax.optimization_barrier(jnp.sum(exp_scores, axis=-1)) + mix_view * lax.optimization_barrier(jnp.sum(linear_w, axis=-1))
        attended = (soft_part + mix_view[..., None] * linear) / totals[..., None]
        return attended.reshape(block_rows, HEADS * HEAD)
    offsets = jnp.arange(0, length, block_rows, dtype=jnp.int32)
    blocks = lax.map(jax.checkpoint(one_block), offsets)
    return blocks.reshape(length, HEADS * HEAD)

def layer_row(one_row, starts, frozen, trained):
    w_query, w_key, w_value, w_out, w_gate_up, w_down = frozen
    gain_one, gain_two, query_in, query_out, key_in, key_out, value_in, value_out, proj_in, proj_out, map_query, map_key, window_logit = trained
    length = one_row.shape[0]
    places_int = jnp.arange(length, dtype=jnp.int32)
    resets = jnp.where(places_int == 0, 1, starts).astype(jnp.int32)
    doc_ids = jnp.cumsum(resets).astype(jnp.int32)
    places = places_int.astype(jnp.float32)
    inputs = low(root_norm(one_row, gain_one))

    def lowrank(source, full, inner, outer):
        reduced = low(low_back(matmul_high(source, inner)))
        return matmul_high(source, full) + matmul_high(reduced, outer)
    query_raw = low_back(lowrank(inputs, w_query, query_in, query_out)).reshape(length, HEADS, HEAD)
    key_raw = low_back(lowrank(inputs, w_key, key_in, key_out)).reshape(length, KV_HEADS, HEAD)
    values = low(low_back(lowrank(inputs, w_value, value_in, value_out))).reshape(length, KV_HEADS, HEAD)
    queries = low(rotate(query_raw, places))
    keys = low(rotate(key_raw, places))
    query_feats = feature(queries, map_query)
    key_feats = feature(keys, map_key)
    mixing = jax.nn.sigmoid(window_logit)
    merged = low(low_back(attend(queries, keys, values, query_feats, key_feats, doc_ids, mixing)))
    residual = one_row + low_back(lowrank(merged, w_out, proj_in, proj_out))
    second = low(root_norm(residual, gain_two))
    gate_vals = low_back(matmul_high(second, w_gate_up[0]))
    up_vals = low_back(matmul_high(second, w_gate_up[1]))
    activation = low(jax.nn.silu(gate_vals) * up_vals)
    return residual + matmul_high(activation, w_down)

def reference(tokens, doc_starts, cotangent, norm_first, norm_second, w_query, w_key, w_value, w_out, w_gate_up, w_down, query_in, query_out, key_in, key_out, value_in, value_out, proj_in, proj_out, map_query, map_key, window_logit):
    frozen = (w_query.astype(jnp.float32), w_key.astype(jnp.float32), w_value.astype(jnp.float32), w_out.astype(jnp.float32), w_gate_up.astype(jnp.float32), w_down.astype(jnp.float32))
    trained = (norm_first.astype(jnp.float32), norm_second.astype(jnp.float32), query_in.astype(jnp.float32), query_out.astype(jnp.float32), key_in.astype(jnp.float32), key_out.astype(jnp.float32), value_in.astype(jnp.float32), value_out.astype(jnp.float32), proj_in.astype(jnp.float32), proj_out.astype(jnp.float32), map_query.astype(jnp.float32), map_key.astype(jnp.float32), window_logit.astype(jnp.float32))

    def forward(inputs, params):

        def step(carried, pair):
            return (carried, jax.checkpoint(layer_row)(pair[0], pair[1], frozen, params))
        unused, outputs = lax.scan(step, jnp.zeros((), jnp.float32), (inputs, doc_starts))
        return outputs
    outputs, pullback = jax.vjp(forward, tokens.astype(jnp.float32), trained)
    grad_tokens, grads = pullback(cotangent.astype(jnp.float32))
    return (outputs.astype(jnp.bfloat16), grad_tokens, grads[0], grads[1], grads[2], grads[3], grads[4], grads[5], grads[6], grads[7], grads[8], grads[9], grads[10], grads[11], grads[12])
```

```python
import functools

import jax
import jax.numpy as jnp
from jax import lax
from jax.experimental import pallas as pl
from jax.experimental.pallas import tpu as pltpu
from jax.sharding import PartitionSpec as P

D = 2048
HEADS = 32
KV_HEADS = 8
HEAD = 64
WINDOW = 64
KVD = KV_HEADS * HEAD
GROUPS = HEADS // KV_HEADS
QKV = D + 2 * KVD
WIDE = GROUPS * HEAD
FEAT = 2 * HEAD
LOW = 128
STATE = 80
SCALE = HEAD ** (-0.5)

EPSILON = 1e-05
THETA = 500000.0

Z_SIZE = 4
CORES = 2
F32 = jnp.float32
BF16 = jnp.bfloat16


def dot_nn(a, b):
    return jnp.dot(a, b, preferred_element_type=F32)


def dot_nt(a, b):
    return lax.dot_general(a, b, (((1,), (1,)), ((), ())), preferred_element_type=F32)


def dot_tn(a, b):
    return lax.dot_general(a, b, (((0,), (0,)), ((), ())), preferred_element_type=F32)


def lane(shape):
    return lax.broadcasted_iota(jnp.int32, shape, 1)


def row(shape):
    return lax.broadcasted_iota(jnp.int32, shape, 0)


def low_half(shape):
    return lane(shape) % FEAT < HEAD


def turn(x, cosine, sine):
    width = x.shape[1]
    first = lane(x.shape) % HEAD < HEAD // 2
    swapped = jnp.where(
        first, pltpu.roll(x, width - HEAD // 2, 1), pltpu.roll(x, HEAD // 2, 1)
    )
    return x * cosine + swapped * sine


def halves_softmax(u):
    lo = low_half(u.shape)
    top = jnp.where(
        lo,
        jnp.max(jnp.where(lo, u, -jnp.inf), axis=1, keepdims=True),
        jnp.max(jnp.where(lo, -jnp.inf, u), axis=1, keepdims=True),
    )
    e = jnp.exp(u - top)
    total = jnp.where(
        lo,
        jnp.sum(jnp.where(lo, e, 0.0), axis=1, keepdims=True),
        jnp.sum(jnp.where(lo, 0.0, e), axis=1, keepdims=True),
    )
    return e / total


def halves_softmax_back(f, g):
    lo = low_half(f.shape)
    t = f * g
    total = jnp.where(
        lo,
        jnp.sum(jnp.where(lo, t, 0.0), axis=1, keepdims=True),
        jnp.sum(jnp.where(lo, 0.0, t), axis=1, keepdims=True),
    )
    v = f * (g - total)
    return v - pltpu.roll(v, HEAD, 1), t


def pair_features(x, maps):
    u = dot_nn(x, maps)
    return jnp.concatenate(
        [halves_softmax(u[:, :FEAT]), halves_softmax(u[:, FEAT:])], axis=1
    )


def same_head(size):
    shape = (GROUPS * size, WIDE)
    return (row(shape) // size == lane(shape) // HEAD).astype(F32)


def diagonal(tile, mask):
    wide = jnp.concatenate([tile, tile], axis=1)
    return (jnp.concatenate([wide] * GROUPS, axis=0) * mask).astype(BF16)


def diagonal_pair(tile):
    none = jnp.zeros_like(tile)
    return jnp.concatenate(
        [jnp.concatenate([tile, none], axis=1), jnp.concatenate([none, tile], axis=1)], axis=0
    )


def both_halves(kv):
    kv = kv.astype(F32)
    lo = low_half(kv.shape)
    other = pltpu.roll(kv, HEAD, 1)
    return jnp.where(lo, kv, other), jnp.where(lo, other, kv)


def fold_heads(r, mask):
    r = r * mask
    r = r[:64] + r[64:128] + r[128:192] + r[192:]
    r = r[:, :FEAT] + r[:, FEAT:]
    return r + pltpu.roll(r, HEAD, 1)


def fold_pair(r, size):
    return r[:size, :FEAT] + r[size:, FEAT:]


def project_kernel(
    x_ref, low_ref, w_ref, p_ref, cos_ref, sin_ref, maps_ref, survive_ref,
    q_ref, kv_ref, kf_ref, rim_ref, near_ref, full_ref, keys_ref,
):
    n = pl.program_id(0)
    length = x_ref.shape[0]
    q_steps = D // WIDE
    k_steps = KVD // WIDE
    raw = dot_nn(x_ref[...], w_ref[...]) + dot_nn(low_ref[...], p_ref[...])

    @pl.when(n < q_steps)
    def _():
        q_ref[...] = turn(raw, cos_ref[...], sin_ref[...]).astype(BF16)

    for i in range(k_steps):

        @pl.when(n == q_steps + i)
        def _():
            keys = turn(raw, cos_ref[...], sin_ref[...]).astype(BF16)
            keys_ref[i] = keys
            for p in range(WIDE // FEAT):
                at = (i * GROUPS + 2 * p) * FEAT
                feats = pair_features(keys[:, p * FEAT : (p + 1) * FEAT], maps_ref[2 * i + p])
                kf_ref[:, at : at + 2 * FEAT] = feats.astype(BF16)

        @pl.when(n == q_steps + k_steps + i)
        def _():
            survive = survive_ref[...]
            lo = low_half((length, FEAT))
            for h in range(GROUPS):
                p = h // 2
                k2 = keys_ref[i][:, p * FEAT : (p + 1) * FEAT].astype(F32)
                v2 = raw[:, p * FEAT : (p + 1) * FEAT].astype(BF16).astype(F32)
                if h % 2:
                    k2 = pltpu.roll(k2, HEAD, 1)
                    v_low = pltpu.roll(v2, HEAD, 1)
                else:
                    v_low = v2
                    v2 = pltpu.roll(v2, HEAD, 1)
                g = i * GROUPS + h
                at = g * FEAT
                kv_ref[:, at : at + FEAT] = jnp.where(lo, k2, v2).astype(BF16)
                ones = jnp.where(lane((length, FEAT)) < HEAD + 8, 1.0, 0.0)
                v_one = jnp.where(lo, v_low, ones).astype(BF16)
                feats = (kf_ref[:, at : at + FEAT].astype(F32) * survive).astype(BF16)
                cut = length - WINDOW
                head = dot_tn(v_one[:cut], feats[:cut])
                tail = dot_tn(v_one[cut:], feats[cut:])
                near_ref[g] = head[:STATE].astype(BF16)
                full_ref[g] = (head + tail)[:STATE].astype(BF16)

    @pl.when(n == pl.num_programs(0) - 1)
    def _():
        cut = length - WINDOW
        rim_ref[:, : KV_HEADS * FEAT] = kv_ref[cut:, :]
        rim_ref[:, KV_HEADS * FEAT :] = kf_ref[cut:, :]


def project(x, low, w, p, cosine, sine, maps, survive):
    length = x.shape[0]
    steps = QKV // WIDE
    whole = lambda a: pl.BlockSpec(a.shape, lambda n: (0,) * a.ndim)
    q_last = D // WIDE - 1
    shapes = (
        jax.ShapeDtypeStruct((length, D), BF16),
        jax.ShapeDtypeStruct((length, KV_HEADS * FEAT), BF16),
        jax.ShapeDtypeStruct((length, KV_HEADS * FEAT), BF16),
        jax.ShapeDtypeStruct((WINDOW, 2 * KV_HEADS * FEAT), BF16),
        jax.ShapeDtypeStruct((KV_HEADS, STATE, FEAT), BF16),
        jax.ShapeDtypeStruct((KV_HEADS, STATE, FEAT), BF16),
    )
    return pl.pallas_call(
        project_kernel,
        grid=(steps,),
        in_specs=[
            whole(x), whole(low),
            pl.BlockSpec((D, WIDE), lambda n: (0, n)),
            pl.BlockSpec((LOW, WIDE), lambda n: (0, n)),
            whole(cosine), whole(sine), whole(maps), whole(survive),
        ],
        out_specs=[pl.BlockSpec((length, WIDE), lambda n: (0, jnp.minimum(n, q_last)))]
        + [whole(s) for s in shapes[1:]],
        out_shape=shapes,
        scratch_shapes=[pltpu.VMEM((KVD // WIDE, length, WIDE), BF16)],
        compiler_params=pltpu.CompilerParams(vmem_limit_bytes=40 << 20),
        cost_estimate=pl.CostEstimate(
            flops=2 * length * D * QKV, bytes_accessed=2 * D * QKV, transcendentals=0
        ),
        name="project",
    )(x, low, w, p, cosine, sine, maps, survive)


def features_kernel(q_ref, maps_ref, out_ref):
    for p in range(WIDE // FEAT):
        feats = pair_features(q_ref[:, p * FEAT : (p + 1) * FEAT], maps_ref[p])
        out_ref[:, 2 * p * FEAT : 2 * (p + 1) * FEAT] = feats.astype(BF16)


def features(q, maps):
    length = q.shape[0]
    pairs = WIDE // FEAT
    return pl.pallas_call(
        features_kernel,
        grid=(D // WIDE,),
        in_specs=[
            pl.BlockSpec((length, WIDE), lambda g: (0, g)),
            pl.BlockSpec((pairs, FEAT, 2 * FEAT), lambda g: (g, 0, 0)),
        ],
        out_specs=pl.BlockSpec((length, 2 * WIDE), lambda g: (0, g)),
        out_shape=jax.ShapeDtypeStruct((length, 2 * D), BF16),
        cost_estimate=pl.CostEstimate(
            flops=8_000_000_000, bytes_accessed=6 * length * D, transcendentals=2 * length * D
        ),
        name="features",
    )(q, maps)


def key_tiles(kv_ref, kf_ref, rim_kv_ref, rim_kf_ref, mask):
    tiles = []
    for t in range(1 + kv_ref.shape[0] // WINDOW):
        if t == 0:
            kv, kf = rim_kv_ref[...], rim_kf_ref[...]
        else:
            at = (t - 1) * WINDOW
            kv, kf = kv_ref[at : at + WINDOW, :], kf_ref[at : at + WINDOW, :]
        kk, vv = both_halves(kv)
        tiles.append((diagonal(kk, mask * SCALE), diagonal(vv, mask), diagonal_pair(kf)))
    return tiles


def spans(t, length):
    edge = lambda v: min(max(v, 0), length)
    a, b, c = edge((t - 1) * WINDOW), edge(t * WINDOW), edge((t + 1) * WINDOW)
    return (a, b), (b, c), (c, length)


def weights_of(t, tile, q_ref, qf_ref, same, upper, gamma):
    length = q_ref.shape[0]
    (a, b), (_, c), _ = spans(t, length)
    e = jnp.exp(dot_nt(q_ref[a:c, :], tile[0]))
    linear = None
    if b < length:
        linear = gamma * jnp.concatenate(
            [
                dot_nt(qf_ref[b:, 2 * p * FEAT : 2 * (p + 1) * FEAT], tile[2])
                for p in range(GROUPS // 2)
            ],
            axis=1,
        )
    parts = []
    if b > a:
        parts.append(jnp.where(same(a, b) & upper, e[: b - a], 0.0))
    if c > b:
        mixed = jnp.where(upper, linear[: c - b], e[b - a :])
        parts.append(jnp.where(same(b, c), mixed, 0.0))
    if length > c:
        parts.append(jnp.where(same(c, length), linear[c - b :], 0.0))
    return e, jnp.concatenate(parts, axis=0).astype(BF16)


def carried(carry_ref):
    state = carry_ref[0]
    ones = jnp.zeros((HEAD, FEAT), BF16) + state[HEAD : HEAD + 1, :]
    return diagonal_pair(state[:HEAD, :]), diagonal_pair(ones)


def attend_kernel(
    q_ref, qf_ref, kv_ref, kf_ref, rim_kv_ref, rim_kf_ref, carry_ref,
    qdoc_ref, kdoc_ref, fresh_ref, gamma_ref,
    out_ref, att_ref, inv_ref, num_ref, den_ref,
):
    length = q_ref.shape[0]
    mask = same_head(WINDOW)
    ones = mask.astype(BF16)
    gamma = gamma_ref[...]
    shape = (WINDOW, WIDE)
    upper = row(shape) >= lane(shape) % HEAD
    state, state_sum = carried(carry_ref)
    fresh = fresh_ref[...] * gamma
    for p in range(GROUPS // 2):
        feats = qf_ref[:, 2 * p * FEAT : 2 * (p + 1) * FEAT]
        at = slice(p * FEAT, (p + 1) * FEAT)
        num_ref[:, at] = dot_nt(feats, state) * fresh[:, at]
        den_ref[:, at] = dot_nt(feats, state_sum) * fresh[:, at]
    for t, tile in enumerate(key_tiles(kv_ref, kf_ref, rim_kv_ref, rim_kf_ref, mask)):
        a = spans(t, length)[0][0]
        same = lambda i, j, t=t: qdoc_ref[i:j, :] == kdoc_ref[t : t + 1, :]
        _, w = weights_of(t, tile, q_ref, qf_ref, same, upper, gamma)
        num_ref[a:, :] += dot_nn(w, tile[1])
        den_ref[a:, :] += dot_nn(w, ones)
    inv = 1.0 / den_ref[...]
    att = num_ref[...] * inv
    inv_ref[...] = inv
    att_ref[...] = att
    out_ref[...] = att.astype(BF16)


def group_specs(length):
    column = lambda rows, width: pl.BlockSpec((rows, width), lambda g: (0, g))
    whole = lambda rows, width: pl.BlockSpec((rows, width), lambda g: (0, 0))
    return dict(
        q=column(length, WIDE),
        qf=column(length, 2 * WIDE),
        k=column(length, FEAT),
        rim_kv=pl.BlockSpec((WINDOW, FEAT), lambda g: (0, g)),
        rim_kf=pl.BlockSpec((WINDOW, FEAT), lambda g: (0, KV_HEADS + g)),
        state=pl.BlockSpec((1, STATE, FEAT), lambda g: (g, 0, 0)),
        qdoc=whole(length, 1),
        kdoc=whole(8, WIDE),
        gamma=column(1, WIDE),
        wide=whole(length, WIDE),
        maps=pl.BlockSpec((GROUPS // 2, FEAT, 2 * FEAT), lambda g: (g, 0, 0)),
    )


def attend(q, qf, kv, kf, rim, carry, masks):
    length = q.shape[0]
    s = group_specs(length)
    return pl.pallas_call(
        attend_kernel,
        grid=(KV_HEADS,),
        in_specs=[
            s["q"], s["qf"], s["k"], s["k"], s["rim_kv"], s["rim_kf"], s["state"],
            s["qdoc"], s["kdoc"], s["qdoc"], s["gamma"],
        ],
        out_specs=[s["q"]] * 3,
        out_shape=[
            jax.ShapeDtypeStruct((length, D), BF16),
            jax.ShapeDtypeStruct((length, D), F32),
            jax.ShapeDtypeStruct((length, D), F32),
        ],
        scratch_shapes=[pltpu.VMEM((length, WIDE), F32)] * 2,
        compiler_params=pltpu.CompilerParams(vmem_limit_bytes=32 << 20),
        cost_estimate=pl.CostEstimate(
            flops=10_000_000_000, bytes_accessed=16 * length * D, transcendentals=0
        ),
        name="attend",
    )(q, qf, kv, kf, rim, rim, carry, masks["qdoc"], masks["kdoc"], masks["fresh"], masks["gamma"])


def scaled_grads_kernel(
    ga_ref, att_ref, inv_ref, qf_ref, fresh_ref, gamma_ref, g_ref, gd_ref, back_ref
):
    mask = same_head(HEAD)
    ga = ga_ref[...].astype(F32)
    inv = inv_ref[...]
    product = ga * att_ref[...]
    high = product.astype(BF16)
    rest = (product - high.astype(F32)).astype(BF16)
    ones = mask.astype(BF16)
    gd = -(dot_nn(high, ones) + dot_nn(rest, ones)) * inv
    g = ga * inv
    g_ref[...] = g.astype(BF16)
    gd_ref[...] = gd
    fresh = fresh_ref[...] * gamma_ref[...]
    fresh_g = (g * fresh).astype(BF16)
    fresh_gd = (gd * fresh).astype(BF16)
    kv = sums = 0.0
    for p in range(GROUPS // 2):
        feats = qf_ref[:, 2 * p * FEAT : 2 * (p + 1) * FEAT]
        at = slice(p * FEAT, (p + 1) * FEAT)
        kv += fold_pair(dot_tn(fresh_g[:, at], feats), HEAD)
        sums += fold_pair(dot_tn(fresh_gd[:, at], feats), HEAD)
    back_ref[0, :HEAD, :] = kv.astype(BF16)
    back_ref[0, HEAD:, :] = sums[: STATE - HEAD].astype(BF16)


def scaled_grads(ga, att, inv, qf, masks):
    length = ga.shape[0]
    s = group_specs(length)
    return pl.pallas_call(
        scaled_grads_kernel,
        grid=(KV_HEADS,),
        in_specs=[s["q"], s["q"], s["q"], s["qf"], s["qdoc"], s["gamma"]],
        out_specs=[s["q"], s["q"], s["state"]],
        out_shape=[
            jax.ShapeDtypeStruct((length, D), BF16),
            jax.ShapeDtypeStruct((length, D), F32),
            jax.ShapeDtypeStruct((KV_HEADS, STATE, FEAT), BF16),
        ],
        name="scaled_grads",
    )(ga, att, inv, qf, masks["fresh"], masks["gamma"])


def attend_back_kernel(
    q_ref, qf_ref, kv_ref, kf_ref, rim_kv_ref, rim_kf_ref, carry_ref, g_ref, gd_ref,
    qdoc_ref, kdoc_ref, fresh_ref, gamma_ref, maps_ref, cos_ref, sin_ref,
    raw_ref, dkv_ref, dkf_ref, dmap_ref, logit_ref, dq_ref, dqf_ref,
):
    length = q_ref.shape[0]
    mask = same_head(WINDOW)
    gamma = gamma_ref[...]
    shape = (WINDOW, WIDE)
    upper = row(shape) >= lane(shape) % HEAD
    state, state_sum = carried(carry_ref)
    fresh = fresh_ref[...] * gamma
    pairs = range(GROUPS // 2)
    half = lambda p: slice(p * FEAT, (p + 1) * FEAT)
    full = lambda p: slice(2 * p * FEAT, 2 * (p + 1) * FEAT)
    fresh_g = (g_ref[...].astype(F32) * fresh).astype(BF16)
    fresh_gd = (gd_ref[...] * fresh * (1.0 / HEAD)).astype(BF16)
    for p in pairs:
        dqf_ref[:, full(p)] = dot_nn(fresh_g[:, half(p)], state) + dot_nn(
            fresh_gd[:, half(p)], state_sum
        )
    dq_ref[...] = jnp.zeros_like(dq_ref)
    lo = low_half((WINDOW, FEAT))
    for t, tile in enumerate(key_tiles(kv_ref, kf_ref, rim_kv_ref, rim_kf_ref, mask)):
        (a, b), (_, c), _ = spans(t, length)
        same = lambda i, j, t=t: qdoc_ref[i:j, :] == kdoc_ref[t : t + 1, :]
        e, w = weights_of(t, tile, q_ref, qf_ref, same, upper, gamma)
        g = g_ref[a:, :]
        x = dot_nt(g, tile[1]) + gd_ref[a:, :]
        near = x[: c - a] * e
        parts = []
        if b > a:
            parts.append(jnp.where(same(a, b) & upper, near[: b - a], 0.0))
        if c > b:
            parts.append(jnp.where(same(b, c), jnp.where(upper, 0.0, near[b - a :]), 0.0))
        ds = jnp.concatenate(parts, axis=0).astype(BF16)
        dq_ref[a:c, :] += dot_nn(ds, tile[0])
        dk = fold_heads(dot_tn(ds, q_ref[a:c, :]), mask) * SCALE
        dv = fold_heads(dot_tn(w, g), mask)
        at = slice(t * WINDOW, (t + 1) * WINDOW)
        dkv_ref[at, :] = jnp.where(lo, dk, dv)
        if b < length:
            far = x[b - a :] * gamma
            parts = [jnp.where(same(b, c) & upper, far[: c - b], 0.0)]
            if c < length:
                parts.append(jnp.where(same(c, length), far[c - b :], 0.0))
            dl = jnp.concatenate(parts, axis=0).astype(BF16)
            dkf = 0.0
            for p in pairs:
                dqf_ref[b:, full(p)] += dot_nn(dl[:, half(p)], tile[2])
                dkf += fold_pair(dot_tn(dl[:, half(p)], qf_ref[b:, full(p)]), HEAD)
            dkf_ref[at, :] = dkf
        else:
            dkf_ref[at, :] = jnp.zeros((WINDOW, FEAT), F32)
    for p in pairs:
        grads = []
        for h in (2 * p, 2 * p + 1):
            f = qf_ref[:, h * FEAT : (h + 1) * FEAT].astype(F32)
            gu, t = halves_softmax_back(f, dqf_ref[:, h * FEAT : (h + 1) * FEAT])
            grads.append(gu.astype(BF16))
            total = jnp.sum(jnp.sum(t, axis=0, keepdims=True), axis=1, keepdims=True)
            logit_ref[0, h : h + 1, :] = jnp.zeros((1, FEAT), F32) + total
        gu = jnp.concatenate(grads, axis=1)
        dq_ref[:, half(p)] += 0.5 * dot_nt(gu, maps_ref[p])
        dmap = dot_tn(q_ref[:, half(p)], gu)
        dmap_ref[2 * p] = dmap[:HEAD, :FEAT]
        dmap_ref[2 * p + 1] = dmap[HEAD:, FEAT:]
    raw_ref[...] = turn(dq_ref[...], cos_ref[...], -sin_ref[...]).astype(BF16)


def attend_back(q, qf, kv, kf, rim, carry, g, gd, masks, maps):
    length = q.shape[0]
    extended = length + WINDOW
    s = group_specs(length)
    column = pl.BlockSpec((extended, FEAT), lambda g: (0, g))
    return pl.pallas_call(
        attend_back_kernel,
        grid=(KV_HEADS,),
        in_specs=[
            s["q"], s["qf"], s["k"], s["k"], s["rim_kv"], s["rim_kf"], s["state"], s["q"], s["q"],
            s["qdoc"], s["kdoc"], s["qdoc"], s["gamma"], s["maps"], s["wide"], s["wide"],
        ],
        out_specs=[
            s["q"], column, column,
            pl.BlockSpec((GROUPS, HEAD, FEAT), lambda g: (g, 0, 0)),
            pl.BlockSpec((1, 8, FEAT), lambda g: (g, 0, 0)),
        ],
        out_shape=[
            jax.ShapeDtypeStruct((length, D), BF16),
            jax.ShapeDtypeStruct((extended, KV_HEADS * FEAT), F32),
            jax.ShapeDtypeStruct((extended, KV_HEADS * FEAT), F32),
            jax.ShapeDtypeStruct((HEADS, HEAD, FEAT), F32),
            jax.ShapeDtypeStruct((KV_HEADS, 8, FEAT), F32),
        ],
        scratch_shapes=[pltpu.VMEM((length, WIDE), F32), pltpu.VMEM((length, 2 * WIDE), F32)],
        compiler_params=pltpu.CompilerParams(vmem_limit_bytes=32 << 20),
        cost_estimate=pl.CostEstimate(
            flops=30_000_000_000, bytes_accessed=16 * length * D, transcendentals=0
        ),
        name="attend_back",
    )(
        q, qf, kv, kf, rim, rim, carry, g, gd,
        masks["qdoc"], masks["kdoc"], masks["fresh"], masks["gamma"],
        maps, masks["cos"], masks["sin"],
    )


def keys_back_kernel(
    kv_ref, kf_ref, dkv_ref, dkf_ref, rim_kv_ref, rim_kf_ref, near_ref, far_ref, survive_ref,
    maps_ref, cos_ref, sin_ref, rk_ref, rv_ref, dmap_ref,
):
    length = kv_ref.shape[0]
    cut = length - WINDOW
    lo = low_half((length, FEAT))
    survive = survive_ref[...]
    dkv, grads = [], []
    for h in range(2):
        at = slice(h * FEAT, (h + 1) * FEAT)
        kv = kv_ref[:, at].astype(F32)
        kf = kf_ref[:, at]
        v_low = pltpu.roll(kv, HEAD, 1)
        ones = jnp.where(lane((length, FEAT)) == HEAD, 1.0, 0.0)
        v_one = jnp.where(lo, v_low, ones).astype(BF16)[:, :STATE]
        dkf, dv = [], []
        for back, part in ((near_ref, slice(0, cut)), (far_ref, slice(cut, length))):
            state = back[h]
            twice = jnp.concatenate([state[:HEAD], state[:HEAD]], axis=0)
            dkf.append(dot_nn(v_one[part], state))
            dv.append(dot_nt(kf[part], twice))
        rim = jnp.zeros((cut, FEAT), F32)
        dkf = (
            jnp.concatenate(dkf, axis=0) * survive
            + dkf_ref[WINDOW:, at]
            + jnp.concatenate([rim, rim_kf_ref[:, at].astype(F32)], axis=0)
        )
        dv = jnp.concatenate(dv, axis=0) * survive
        total = (
            dkv_ref[WINDOW:, at]
            + jnp.concatenate([rim, rim_kv_ref[:, at].astype(F32)], axis=0)
            + jnp.where(lo, 0.0, dv)
        )
        gu, _ = halves_softmax_back(kf.astype(F32), dkf)
        grads.append(gu.astype(BF16))
        dkv.append(total)
    gu = jnp.concatenate(grads, axis=1)
    keys = jnp.where(lo, kv_ref[:, :FEAT].astype(F32), pltpu.roll(kv_ref[:, FEAT:].astype(F32), HEAD, 1))
    dmap = dot_tn(keys.astype(BF16), gu)
    dmap_ref[0] = dmap[:HEAD, :FEAT]
    dmap_ref[1] = dmap[HEAD:, FEAT:]
    dk = jnp.where(lo, dkv[0], pltpu.roll(dkv[1], HEAD, 1)) + 0.5 * dot_nt(gu, maps_ref[0])
    rk_ref[...] = turn(dk, cos_ref[...], -sin_ref[...]).astype(BF16)
    rv_ref[...] = jnp.where(lo, pltpu.roll(dkv[0], HEAD, 1), dkv[1]).astype(BF16)


def keys_back(kv, kf, dkv, dkf, rim, near, far, masks, maps):
    length = kv.shape[0]
    extended = length + WINDOW
    pairs = KV_HEADS // 2
    column = lambda rows: pl.BlockSpec((rows, 2 * FEAT), lambda g: (0, g))
    state = pl.BlockSpec((2, STATE, FEAT), lambda g: (g, 0, 0))
    narrow = pl.BlockSpec((length, FEAT), lambda g: (0, 0))
    out = pl.BlockSpec((length, FEAT), lambda g: (0, g))
    return pl.pallas_call(
        keys_back_kernel,
        grid=(pairs,),
        in_specs=[
            column(length), column(length), column(extended), column(extended),
            column(WINDOW), pl.BlockSpec((WINDOW, 2 * FEAT), lambda g: (0, pairs + g)),
            state, state, pl.BlockSpec((length, 1), lambda g: (0, 0)),
            pl.BlockSpec((1, FEAT, 2 * FEAT), lambda g: (g, 0, 0)), narrow, narrow,
        ],
        out_specs=[out, out, pl.BlockSpec((2, HEAD, FEAT), lambda g: (g, 0, 0))],
        out_shape=[
            jax.ShapeDtypeStruct((length, KVD), BF16),
            jax.ShapeDtypeStruct((length, KVD), BF16),
            jax.ShapeDtypeStruct((KV_HEADS, HEAD, FEAT), F32),
        ],
        name="keys_back",
    )(
        kv, kf, dkv, dkf, rim, rim, near, far, masks["survive"], maps, masks["cos"], masks["sin"]
    )


class Grid:
    def __init__(self):
        self.seq = lax.axis_size("seq")
        self.rows = lax.axis_size("rows")
        self.zs = Z_SIZE
        self.xs = self.rows // Z_SIZE
        self.ys = self.seq // CORES
        s = lax.axis_index("seq")
        r = lax.axis_index("rows")
        self.y, self.c = s // CORES, s % CORES
        self.z, self.x = r // self.xs, r % self.xs
        self.s, self.r = s, r

    def send(self, value, move):
        route = []
        for s in range(self.seq):
            for r in range(self.rows):
                there = move(s // CORES, s % CORES, r // self.xs, r % self.xs)
                if there is not None:
                    y, c, z, x = there
                    target = (y * CORES + c) * self.rows + z * self.xs + x
                    route.append((s * self.rows + r, target))
        return jax.tree.map(lambda v: lax.ppermute(v, ("seq", "rows"), route), value)

    def along_z(self, value, k):
        return self.send(value, lambda y, c, z, x: (y, c, (z + k) % self.zs, x))

    def along_x(self, value, k):
        return self.send(value, lambda y, c, z, x: (y, c, z, (x + k) % self.xs))

    def along_y(self, value, k):
        return self.send(value, lambda y, c, z, x: ((y + k) % self.ys, c, z, x))

    def flip_z(self, value, bit):
        return self.send(value, lambda y, c, z, x: (y, c, z ^ bit, x))

    def flip_core(self, value):
        return self.send(value, lambda y, c, z, x: (y, 1 - c, z, x))

    def flip_row(self, value, bit):
        def move(y, c, z, x):
            r = (z * self.xs + x) ^ bit
            return (y, c, r // self.xs, r % self.xs)

        return self.send(value, move)

    def along_seq(self, value, k):
        def move(y, c, z, x):
            s = y * CORES + c + k
            return (s // CORES, s % CORES, z, x) if 0 <= s < self.seq else None

        return self.send(value, move)


def after(values, *events):
    return lax.optimization_barrier((values, *events))[0]


def gather_rows(grid, shard):
    half = shard.shape[0] // CORES
    own = lax.dynamic_slice_in_dim(shard, grid.c * half, half, 0)
    pieces = []
    for kz in range(grid.zs):
        from_z = own if kz == 0 else grid.along_z(own, kz)
        for kx in range(grid.xs):
            piece = from_z if kx == 0 else grid.along_x(from_z, kx)
            row = ((grid.z - kz) % grid.zs) * grid.xs + (grid.x - kx) % grid.xs
            pieces.append((piece, (row * CORES + grid.c) * half))
            if kz + kx:
                other = grid.flip_core(piece)
            else:
                other = lax.dynamic_slice_in_dim(shard, (1 - grid.c) * half, half, 0)
            pieces.append((other, (row * CORES + 1 - grid.c) * half))
    return pieces


def assemble(grid, pieces):
    piece = pieces[0][0]
    full = jnp.zeros((piece.shape[0] * len(pieces), piece.shape[1]), piece.dtype)
    for piece, row in pieces:
        full = lax.dynamic_update_slice(full, piece, (row, 0))
    return full


def gather_pair(grid, gate_up, down):
    part = gate_up.shape[2] // grid.seq
    gu = lax.dynamic_slice_in_dim(gate_up, grid.s * part, part, 2)
    dn = lax.dynamic_slice_in_dim(down, grid.s * part, part, 0)
    got = [grid.flip_z((gu, dn), 1)]
    for ky in range(1, grid.ys):
        got.append(grid.along_y(got[0], ky))
    got = got + [grid.flip_core(v) for v in got]
    return (
        jnp.concatenate([v[0] for v in got], axis=2),
        jnp.concatenate([v[1] for v in got], axis=0),
    )


def spread(grid, block):
    near = [block] + [grid.along_x(block, k) for k in range(1, grid.xs)]
    parts = 4
    size = block.shape[0] // parts
    far = [[] for _ in range(grid.xs)]
    for p in range(parts):
        piece = grid.flip_z(block[p * size : (p + 1) * size], 2)
        far[0].append(piece)
        for k in range(1, grid.xs):
            far[k].append(grid.along_x(piece, k))
    return jnp.concatenate(near, axis=0), jnp.concatenate([v for f in far for v in f], axis=0)


def collect(grid, near, far, length):
    parts = 4
    size = length // parts
    total = near[:length]
    for k in range(1, grid.xs):
        total = total + grid.along_x(
            near[k * length : (k + 1) * length].astype(BF16), -k
        ).astype(F32)
    back = []
    for p in range(parts):
        lo = p * size
        piece = far[lo : lo + size]
        for k in range(1, grid.xs):
            piece = piece + grid.along_x(
                far[k * length + lo : k * length + lo + size].astype(BF16), -k
            ).astype(F32)
        back.append(grid.flip_z(piece.astype(BF16), 2).astype(F32))
    return total + jnp.concatenate(back, axis=0)


def total_over_all(grid, values):
    widths = [v.shape[2] for v in values]
    packed = jnp.concatenate([v.astype(BF16) for v in values], axis=2)
    packed = jnp.pad(packed, ((0, 0), (0, 0), (0, -packed.shape[2] % FEAT)))
    packed = packed.reshape(grid.ys, CORES, 8, -1)
    own = lax.dynamic_index_in_dim(packed, grid.c, 1, False)
    other = lax.dynamic_index_in_dim(packed, 1 - grid.c, 1, False)
    both = (own.astype(F32) + grid.flip_core(other).astype(F32)).astype(BF16)
    total = lax.dynamic_index_in_dim(both, grid.y, 0, False).astype(F32)
    for k in range(1, grid.ys):
        part = lax.dynamic_index_in_dim(both, (grid.y + k) % grid.ys, 0, False)
        total = total + grid.along_y(part, k).astype(F32)
    bit = 1
    while bit < grid.rows:
        mine = total.astype(BF16)
        total = mine.astype(F32) + grid.flip_row(mine, bit).astype(F32)
        bit *= 2
    out, at = [], 0
    for w in widths:
        out.append(total[:, at : at + w])
        at += w
    return out


def pair_maps(maps):
    both = jnp.concatenate([maps, -maps], axis=-1)
    both = both.reshape(-1, 2, HEAD, FEAT)
    none = jnp.zeros_like(both[:, 0])
    return jnp.concatenate(
        [
            jnp.concatenate([both[:, 0], none], axis=-1),
            jnp.concatenate([none, both[:, 1]], axis=-1),
        ],
        axis=1,
    )


def adapters(query, key, value, axis):
    if axis == 1:
        joined = jnp.concatenate([query, key, value], axis=1)
        return jnp.pad(joined, ((0, 0), (0, LOW - joined.shape[1])))
    rank = query.shape[0]
    joined = jnp.zeros((LOW, QKV), query.dtype)
    joined = joined.at[:rank, :D].set(query)
    joined = joined.at[rank : 2 * rank, D : D + KVD].set(key)
    return joined.at[2 * rank : 3 * rank, D + KVD :].set(value)


def documents(grid, starts, length):
    resets = lax.all_gather(starts.astype(BF16), "seq", tiled=True).astype(jnp.int32)
    places = jnp.arange(resets.shape[0], dtype=jnp.int32)
    docs = jnp.cumsum(jnp.where(places == 0, 1, resets))
    padded = jnp.concatenate([jnp.full((WINDOW,), -1, jnp.int32), docs])
    extended = lax.dynamic_slice_in_dim(padded, grid.s * length, length + WINDOW, 0)
    own = extended[WINDOW:]
    before = extended[WINDOW - 1]
    last = own[-1]
    ends = docs[length - 1 :: length]
    places = jnp.arange(grid.seq, dtype=jnp.int32)
    tiles = jnp.tile(extended.reshape(-1, 1, WINDOW), (1, GROUPS, 1)).reshape(-1, WIDE)
    masks = dict(
        qdoc=own[:, None],
        kdoc=jnp.pad(tiles, ((0, 8 - tiles.shape[0]), (0, 0))),
        fresh=(own == before).astype(F32)[:, None],
        survive=(own == last).astype(F32)[:, None],
    )
    earlier = ((ends == before) & (places < grid.s)).astype(F32)
    entered = jnp.concatenate([jnp.full((1,), -1, jnp.int32), ends[:-1]])
    later = ((entered == last) & (places > grid.s)).astype(F32)
    pick = lambda v, k: lax.dynamic_index_in_dim(v, jnp.clip(grid.s + k, 0, grid.seq - 1), 0, False)
    former = [pick(earlier, -k) * (grid.s - k >= 0) for k in range(1, grid.seq)]
    latter = [pick(later, k) * (grid.s + k < grid.seq) for k in range(1, grid.seq)]
    return masks, former, latter


def local(
    tokens, doc_starts, cotangent, norm_first, norm_second,
    w_query, w_key, w_value, w_out, w_gate_up, w_down,
    query_in, query_out, key_in, key_out, value_in, value_out, proj_in, proj_out,
    map_query, map_key, window_logit,
):
    grid = Grid()
    length = tokens.shape[1]
    rank = query_in.shape[1]
    hidden = tokens[0].astype(F32)
    grad_out = cotangent[0]
    gain_first = norm_first.astype(F32)
    gain_second = norm_second.astype(F32)

    qkv_shard = jnp.concatenate([w_query, w_key, w_value], axis=1)
    qkv_full = assemble(grid, gather_rows(grid, qkv_shard))
    grad_out, w_out, w_gate_up, w_down = after((grad_out, w_out, w_gate_up, w_down), qkv_full)
    output_full = assemble(grid, gather_rows(grid, w_out))
    pair_gate_up, pair_down = gather_pair(grid, w_gate_up, w_down)
    cot_near, cot_far = spread(grid, grad_out)

    inverse_first = lax.rsqrt(jnp.mean(hidden * hidden, axis=-1, keepdims=True) + EPSILON)
    normed_first = hidden * inverse_first
    inputs = (normed_first * gain_first).astype(BF16)
    masks, former, latter = documents(grid, doc_starts[0], length)
    gamma = jax.nn.sigmoid(window_logit)
    masks["gamma"] = jnp.repeat(gamma, HEAD)[None, :]
    half = HEAD // 2
    inverse_freq = jnp.power(THETA, -(jnp.arange(half, dtype=F32) * 2.0 / HEAD))
    places = (grid.s * length + jnp.arange(length, dtype=jnp.int32)).astype(F32)
    angles = places[:, None] * inverse_freq[None, :]
    sine = jnp.sin(angles)
    masks["cos"] = jnp.tile(jnp.cos(angles), (1, WIDE // half))
    masks["sin"] = jnp.tile(jnp.concatenate([-sine, sine], axis=1), (1, WIDE // HEAD))
    maps_q, maps_k = pair_maps(map_query), pair_maps(map_key)
    qkv_in = adapters(query_in, key_in, value_in, 1)
    qkv_out = adapters(query_out, key_out, value_out, 0)

    low = dot_nn(inputs, qkv_in).astype(BF16)
    queries, kv, kf, rim, near, full = project(
        inputs, low, qkv_full, qkv_out, masks["cos"], masks["sin"], maps_k, masks["survive"]
    )
    rim = grid.along_seq(rim, 1)
    carry = former[0] * grid.along_seq(near, 1).astype(F32)
    for k in range(2, grid.seq):
        carry = carry + former[k - 1] * grid.along_seq(full, k).astype(F32)
    carry = carry.astype(BF16)
    qf = features(queries, maps_q)
    merged, attended, inverse = attend(queries, qf, kv, kf, rim, carry, masks)

    out_low = dot_nn(merged, proj_in).astype(BF16)
    residual = hidden + dot_nn(merged, output_full) + dot_nn(out_low, proj_out)
    inverse_second = lax.rsqrt(jnp.mean(residual * residual, axis=-1, keepdims=True) + EPSILON)
    normed_second = residual * inverse_second
    second_in = (normed_second * gain_second).astype(BF16)
    sides = spread(grid, second_in)
    grad_act = [
        [
            dot_nt(cot, down)
            for down in (w_down, pair_down)
        ]
        for cot in (cot_near, cot_far)
    ]
    mlp_parts, back_parts = [], []
    for side, rows in enumerate(sides):
        mlp_part = back_part = 0.0
        for which, (both, down) in enumerate(((w_gate_up, w_down), (pair_gate_up, pair_down))):
            gate = dot_nn(rows, both[0])
            up = dot_nn(rows, both[1])
            sigmoid_gate = jax.nn.sigmoid(gate)
            silu = gate * sigmoid_gate
            activation = (silu * up).astype(BF16)
            mlp_part = mlp_part + dot_nn(activation, down)
            grads = grad_act[side][which]
            grad_gate = grads * up * sigmoid_gate * (1.0 + gate * (1.0 - sigmoid_gate))
            grad_up = (grads * silu).astype(BF16)
            for grad, full in ((grad_gate.astype(BF16), both[0]), (grad_up, both[1])):
                back_part = back_part + dot_nt(grad, full)
        mlp_parts.append(mlp_part)
        back_parts.append(back_part)
    grad_second = collect(grid, back_parts[0], back_parts[1], length)
    mlp_parts = after(mlp_parts, grad_second)
    mlp_out = collect(grid, mlp_parts[0], mlp_parts[1], length)
    block_out = (residual + mlp_out).astype(BF16)

    def norm_back(grad_normed, normed, inverse_rms, gain):
        scaled = grad_normed * gain
        back = inverse_rms * (scaled - normed * jnp.mean(scaled * normed, axis=-1, keepdims=True))
        return back, jnp.sum(grad_normed * normed, axis=0)

    grad_norm_part, grad_gain_two = norm_back(
        grad_second, normed_second, inverse_second, gain_second
    )
    grad_residual = grad_out.astype(F32) + grad_norm_part
    grad_branch = grad_residual.astype(BF16)
    grad_out_low = dot_nt(grad_branch, proj_out).astype(BF16)
    grad_merged = (dot_nt(grad_branch, output_full) + dot_nt(grad_out_low, proj_in)).astype(BF16)
    grad_proj_out = dot_tn(out_low, grad_branch)
    grad_proj_in = dot_tn(grad_out_low, merged)

    grads, grad_den, back = scaled_grads(grad_merged, attended, inverse, qf, masks)
    far_back = jnp.zeros(back.shape, F32)
    for k in range(2, grid.seq):
        far_back = far_back + latter[k - 1] * grid.along_seq(back, -k).astype(F32)
    near_back = far_back + latter[0] * grid.along_seq(back, -1).astype(F32)
    raw_query, dkv, dkf, dmap_query, dlogit = attend_back(
        queries, qf, kv, kf, rim, carry, grads, grad_den, masks, maps_q
    )
    rim_back = jnp.concatenate([dkv[:WINDOW], dkf[:WINDOW]], axis=1).astype(BF16)
    rim_back = grid.along_seq(rim_back, -1)
    raw_key, raw_value, dmap_key = keys_back(
        kv, kf, dkv, dkf, rim_back, near_back.astype(BF16), far_back.astype(BF16), masks, maps_k
    )
    raw = jnp.concatenate([raw_query, raw_key, raw_value], axis=1)
    grad_low = dot_nt(raw, qkv_out).astype(BF16)
    grad_inputs = dot_nt(raw, qkv_full) + dot_nt(grad_low, qkv_in)
    grad_qkv_out = dot_tn(low, raw)
    grad_qkv_in = dot_tn(grad_low, inputs)
    grad_first_part, grad_gain_one = norm_back(grad_inputs, normed_first, inverse_first, gain_first)
    grad_tokens = grad_residual + grad_first_part
    grad_logit = dlogit[:, :GROUPS, 0].reshape(HEADS) * (1.0 - gamma)

    blocks = lambda v: v.reshape(8, grid.seq, -1).swapaxes(0, 1)
    plain = lambda v: v.reshape(grid.seq, 8, -1)
    outs = (
        blocks(grad_qkv_out[:rank, :D]),
        blocks(grad_qkv_out[rank : 2 * rank, D : D + KVD]),
        blocks(grad_qkv_out[2 * rank : 3 * rank, D + KVD :]),
        blocks(grad_proj_out),
    )
    ins = [blocks(grad_qkv_in[i * rank : (i + 1) * rank]) for i in range(3)]
    ins.append(blocks(grad_proj_in))
    map_q = plain(dmap_query[:, :, :HEAD].reshape(HEADS, -1))
    map_k = dmap_key[:, :, :HEAD].reshape(KV_HEADS, grid.seq, -1).swapaxes(0, 1)
    logit = jnp.pad(grad_logit.reshape(grid.seq, -1, 1), ((0, 0), (0, 8 - HEADS // grid.seq), (0, 0)))
    sums = total_over_all(
        grid, [*outs, *ins, map_q, map_k, plain(grad_gain_one), plain(grad_gain_two), logit]
    )
    outs, ins, (map_q, map_k, gain_one, gain_two, logit) = sums[:4], sums[4:8], sums[8:]
    width = D // grid.seq
    return (
        block_out[None],
        grad_tokens[None],
        gain_one.reshape(width),
        gain_two.reshape(width),
        ins[0].T,
        outs[0],
        ins[1].T,
        outs[1],
        ins[2].T,
        outs[2],
        ins[3].T,
        outs[3],
        map_q.reshape(-1, HEAD, HEAD),
        map_k.reshape(KV_HEADS, -1, HEAD),
        logit[: HEADS // grid.seq, 0],
    )


def solution(mesh):
    placed = (
        P("rows", "seq", None),
        P("rows", "seq"),
        P("rows", "seq", None),
        P(),
        P(),
        P("rows", None),
        P("rows", None),
        P("rows", None),
        P("rows", None),
        P(None, None, "rows"),
        P("rows", None),
        P(),
        P(),
        P(),
        P(),
        P(),
        P(),
        P(),
        P(),
        P(),
        P(),
        P(),
    )
    return jax.shard_map(
        local,
        mesh=mesh,
        in_specs=placed,
        out_specs=(
            P("rows", "seq", None),
            P("rows", "seq", None),
            P("seq"),
            P("seq"),
            P("seq", None),
            P(None, "seq"),
            P("seq", None),
            P(None, "seq"),
            P("seq", None),
            P(None, "seq"),
            P("seq", None),
            P(None, "seq"),
            P("seq", None, None),
            P(None, "seq", None),
            P("seq"),
        ),
        check_vma=False,
    )
```

```python
import functools

import jax
import jax.numpy as jnp
from jax import lax
from jax.experimental import pallas as pl
from jax.experimental.pallas import tpu as pltpu
from jax.sharding import PartitionSpec as P

D = 2048
HEADS = 32
KV_HEADS = 8
HEAD = 64
WINDOW = 64
KVD = KV_HEADS * HEAD
GROUPS = HEADS // KV_HEADS
QKV = D + 2 * KVD
WIDE = GROUPS * HEAD
FEAT = 2 * HEAD
LOW = 128
STATE = 80
HALVES = 2
VMEM_LIMIT = 58 << 20
HALF = D // HALVES
PER_HALF = KV_HEADS // HALVES
SCALE = HEAD ** (-0.5)

EPSILON = 1e-05
THETA = 500000.0

Z_SIZE = 4
NEAR_BIT = 2
FAR_BIT = 1
CORES = 2
F32 = jnp.float32
BF16 = jnp.bfloat16


def dot_nn(a, b):
    return jnp.dot(a, b, preferred_element_type=F32)


def dot_nt(a, b):
    return lax.dot_general(a, b, (((1,), (1,)), ((), ())), preferred_element_type=F32)


def dot_tn(a, b):
    return lax.dot_general(a, b, (((0,), (0,)), ((), ())), preferred_element_type=F32)


def lane(shape):
    return lax.broadcasted_iota(jnp.int32, shape, 1)


def row(shape):
    return lax.broadcasted_iota(jnp.int32, shape, 0)


def low_half(shape):
    return lane(shape) % FEAT < HEAD


def turn(x, cosine, sine):
    width = x.shape[1]
    first = lane(x.shape) % HEAD < HEAD // 2
    swapped = jnp.where(
        first, pltpu.roll(x, width - HEAD // 2, 1), pltpu.roll(x, HEAD // 2, 1)
    )
    return x * cosine + swapped * sine


def halves_softmax(u):
    lo = low_half(u.shape)
    top = jnp.where(
        lo,
        jnp.max(jnp.where(lo, u, -jnp.inf), axis=1, keepdims=True),
        jnp.max(jnp.where(lo, -jnp.inf, u), axis=1, keepdims=True),
    )
    e = jnp.exp(u - top)
    total = jnp.where(
        lo,
        jnp.sum(jnp.where(lo, e, 0.0), axis=1, keepdims=True),
        jnp.sum(jnp.where(lo, 0.0, e), axis=1, keepdims=True),
    )
    return e / total


def halves_softmax_back(f, g):
    lo = low_half(f.shape)
    t = f * g
    total = jnp.where(
        lo,
        jnp.sum(jnp.where(lo, t, 0.0), axis=1, keepdims=True),
        jnp.sum(jnp.where(lo, 0.0, t), axis=1, keepdims=True),
    )
    v = f * (g - total)
    return v - pltpu.roll(v, HEAD, 1), t


def pair_features(x, maps):
    u = dot_nn(x, maps)
    return jnp.concatenate(
        [halves_softmax(u[:, :FEAT]), halves_softmax(u[:, FEAT:])], axis=1
    )


def same_head(size):
    shape = (GROUPS * size, WIDE)
    return (row(shape) // size == lane(shape) // HEAD).astype(F32)


def diagonal(tile, mask):
    wide = jnp.concatenate([tile, tile], axis=1)
    return (jnp.concatenate([wide] * GROUPS, axis=0) * mask).astype(BF16)


def diagonal_pair(tile):
    none = jnp.zeros_like(tile)
    return jnp.concatenate(
        [jnp.concatenate([tile, none], axis=1), jnp.concatenate([none, tile], axis=1)], axis=0
    )


def both_halves(kv):
    kv = kv.astype(F32)
    lo = low_half(kv.shape)
    other = pltpu.roll(kv, HEAD, 1)
    return jnp.where(lo, kv, other), jnp.where(lo, other, kv)


def fold_heads(r, mask):
    r = r * mask
    r = r[:64] + r[64:128] + r[128:192] + r[192:]
    r = r[:, :FEAT] + r[:, FEAT:]
    return r + pltpu.roll(r, HEAD, 1)


def fold_pair(r, size):
    return r[:size, :FEAT] + r[size:, FEAT:]


def whole(a):
    return pl.BlockSpec(a.shape, lambda *_: (0,) * len(a.shape))


ANYWHERE = pl.BlockSpec(memory_space=pl.ANY)
SCALARS = pl.BlockSpec(memory_space=pltpu.SMEM)


class Gathered:
    def __init__(self, blocks, places, size):
        self.blocks, self.places, self.size = blocks, places, size

    def shapes(self):
        return tuple(b.shape[0] // self.size for b in self.blocks)


def start_rows(places, refs, counts, size, target, sem, column=0):
    n = 0
    columns = slice(column, column + target.shape[1])
    for ref, count in zip(refs, counts):
        for i in range(count):
            to = pl.ds(pl.multiple_of(places[n] * size, size), size)
            part = ref.at[i * size : (i + 1) * size, columns]
            pltpu.make_async_copy(part, target.at[to], sem).start()
            n += 1


def wait_rows(target, sem):
    pltpu.make_async_copy(target, target, sem).wait()


def project_kv_kernel(*refs, counts, size):
    n = len(counts)
    places_ref, blocks = refs[0], refs[1 : 1 + n]
    x_ref, low_ref, p_ref, cos_ref, sin_ref, maps_ref, survive_ref = refs[1 + n : 8 + n]
    kv_ref, kf_ref, pack_ref, full_ref, w_ref, sem = refs[8 + n :]
    length = x_ref.shape[0]
    start_rows(places_ref, blocks, counts, size, w_ref, sem, D)
    wait_rows(w_ref, sem)
    survive = survive_ref[...]
    lo = low_half((length, FEAT))
    cut = length - WINDOW
    steps = KVD // WIDE
    part = lambda j: slice(j * WIDE, (j + 1) * WIDE)
    for i in range(steps):
        raw_k, raw_v = (
            dot_nn(x_ref[...], w_ref[:, part(j)]) + dot_nn(low_ref[...], p_ref[:, part(j)])
            for j in (i, steps + i)
        )
        keys = turn(raw_k, cos_ref[...], sin_ref[...]).astype(BF16)
        values = raw_v.astype(BF16).astype(F32)
        for p in range(WIDE // FEAT):
            at = (i * GROUPS + 2 * p) * FEAT
            k2 = keys[:, p * FEAT : (p + 1) * FEAT]
            v2 = values[:, p * FEAT : (p + 1) * FEAT]
            feats = pair_features(k2, maps_ref[2 * i + p])
            kf_ref[:, at : at + 2 * FEAT] = feats.astype(BF16)
            k2 = k2.astype(F32)
            k_other, v_other = pltpu.roll(k2, HEAD, 1), pltpu.roll(v2, HEAD, 1)
            ones = jnp.where(lane((length, FEAT)) < HEAD + 8, 1.0, 0.0)
            for h, kv, v in (
                (0, jnp.where(lo, k2, v_other), v2),
                (1, jnp.where(lo, k_other, v2), v_other),
            ):
                at_h = at + h * FEAT
                kv_ref[:, at_h : at_h + FEAT] = kv.astype(BF16)
                v_one = jnp.where(lo, v, ones).astype(BF16)
                kept = (feats[:, h * FEAT : (h + 1) * FEAT].astype(BF16).astype(F32) * survive)
                kept = kept.astype(BF16)
                head = dot_tn(v_one[:cut], kept[:cut])
                tail = dot_tn(v_one[cut:], kept[cut:])
                at_h = slice(at_h, at_h + FEAT)
                pack_ref[2 * WINDOW :, at_h] = head[:STATE].astype(BF16)
                full_ref[:, at_h] = (head + tail)[:STATE].astype(BF16)
    pack_ref[:WINDOW, :] = kv_ref[cut:, :]
    pack_ref[WINDOW : 2 * WINDOW, :] = kf_ref[cut:, :]


def project_kv(w, x, low, p, cosine, sine, maps, survive):
    length = x.shape[0]
    shapes = (
        jax.ShapeDtypeStruct((length, KV_HEADS * FEAT), BF16),
        jax.ShapeDtypeStruct((length, KV_HEADS * FEAT), BF16),
        jax.ShapeDtypeStruct((2 * WINDOW + STATE, KV_HEADS * FEAT), BF16),
        jax.ShapeDtypeStruct((STATE, KV_HEADS * FEAT), BF16),
    )
    rest = (x, low, p, cosine, sine, maps, survive)
    return pl.pallas_call(
        functools.partial(project_kv_kernel, counts=w.shapes(), size=w.size),
        grid=(1,),
        in_specs=[SCALARS] + [ANYWHERE] * len(w.blocks) + [whole(a) for a in rest],
        out_specs=[whole(v) for v in shapes],
        out_shape=shapes,
        scratch_shapes=[pltpu.VMEM((D, 2 * KVD), BF16), pltpu.SemaphoreType.DMA],
        compiler_params=pltpu.CompilerParams(vmem_limit_bytes=VMEM_LIMIT),
        cost_estimate=pl.CostEstimate(
            flops=4 * length * D * KVD, bytes_accessed=4 * D * KVD, transcendentals=0
        ),
        name="project_kv",
    )(w.places, *w.blocks, *rest)


def project_q_kernel(*refs, counts, size, column):
    n = len(counts)
    places_ref, blocks = refs[0], refs[1 : 1 + n]
    x_ref, low_ref, p_ref, cos_ref, sin_ref, maps_ref, q_ref, qf_ref, w_ref, sem = refs[1 + n :]
    step = pl.program_id(0)

    @pl.when(step == 0)
    def _():
        start_rows(places_ref, blocks, counts, size, w_ref, sem, column)
        wait_rows(w_ref, sem)

    at = pl.ds(pl.multiple_of(step * WIDE, WIDE), WIDE)
    raw = dot_nn(x_ref[...], w_ref[:, at]) + dot_nn(low_ref[...], p_ref[...])
    q = turn(raw, cos_ref[...], sin_ref[...]).astype(BF16)
    q_ref[...] = q
    for p in range(WIDE // FEAT):
        feats = pair_features(q[:, p * FEAT : (p + 1) * FEAT], maps_ref[p])
        qf_ref[:, 2 * p * FEAT : 2 * (p + 1) * FEAT] = feats.astype(BF16)


def project_q(half, w, x, low, p, cosine, sine, maps):
    length = x.shape[0]
    first = half * PER_HALF
    pairs = WIDE // FEAT
    return pl.pallas_call(
        functools.partial(
            project_q_kernel, counts=w.shapes(), size=w.size, column=half * HALF
        ),
        grid=(HALF // WIDE,),
        in_specs=[SCALARS] + [ANYWHERE] * len(w.blocks) + [
            whole(x), whole(low),
            pl.BlockSpec((LOW, WIDE), lambda g: (0, first + g)),
            whole(cosine), whole(sine),
            pl.BlockSpec((pairs, FEAT, 2 * FEAT), lambda g: (first + g, 0, 0)),
        ],
        out_specs=[
            pl.BlockSpec((length, WIDE), lambda g: (0, g)),
            pl.BlockSpec((length, 2 * WIDE), lambda g: (0, g)),
        ],
        out_shape=[
            jax.ShapeDtypeStruct((length, HALF), BF16),
            jax.ShapeDtypeStruct((length, 2 * HALF), BF16),
        ],
        scratch_shapes=[pltpu.VMEM((D, HALF), BF16), pltpu.SemaphoreType.DMA],
        compiler_params=pltpu.CompilerParams(vmem_limit_bytes=VMEM_LIMIT),
        cost_estimate=pl.CostEstimate(
            flops=2 * length * D * HALF, bytes_accessed=2 * D * HALF, transcendentals=0
        ),
        name="project_q",
    )(w.places, *w.blocks, x, low, p, cosine, sine, maps)


def key_tiles(kv_ref, kf_ref, rim_kv_ref, rim_kf_ref, mask):
    tiles = []
    for t in range(1 + kv_ref.shape[0] // WINDOW):
        if t == 0:
            kv, kf = rim_kv_ref[...], rim_kf_ref[...]
        else:
            at = (t - 1) * WINDOW
            kv, kf = kv_ref[at : at + WINDOW, :], kf_ref[at : at + WINDOW, :]
        kk, vv = both_halves(kv)
        tiles.append((diagonal(kk, mask * SCALE), diagonal(vv, mask), diagonal_pair(kf)))
    return tiles


def spans(t, length):
    edge = lambda v: min(max(v, 0), length)
    a, b, c = edge((t - 1) * WINDOW), edge(t * WINDOW), edge((t + 1) * WINDOW)
    return (a, b), (b, c), (c, length)


def weights_of(t, tile, q_ref, qf_ref, same, upper, gamma):
    length = q_ref.shape[0]
    (a, b), (_, c), _ = spans(t, length)
    e = jnp.exp(dot_nt(q_ref[a:c, :], tile[0]))
    linear = None
    if b < length:
        linear = gamma * jnp.concatenate(
            [
                dot_nt(qf_ref[b:, 2 * p * FEAT : 2 * (p + 1) * FEAT], tile[2])
                for p in range(GROUPS // 2)
            ],
            axis=1,
        )
    parts = []
    if b > a:
        parts.append(jnp.where(same(a, b) & upper, e[: b - a], 0.0))
    if c > b:
        mixed = jnp.where(upper, linear[: c - b], e[b - a :])
        parts.append(jnp.where(same(b, c), mixed, 0.0))
    if length > c:
        parts.append(jnp.where(same(c, length), linear[c - b :], 0.0))
    return e, jnp.concatenate(parts, axis=0).astype(BF16)


def carried(carry_ref):
    state = carry_ref[...]
    ones = jnp.zeros((HEAD, FEAT), BF16) + state[HEAD : HEAD + 1, :]
    return diagonal_pair(state[:HEAD, :]), diagonal_pair(ones)


def attend_kernel(
    q_ref, qf_ref, kv_ref, kf_ref, rim_kv_ref, rim_kf_ref, carry_ref,
    qdoc_ref, kdoc_ref, fresh_ref, gamma_ref,
    out_ref, att_ref, inv_ref, num_ref, den_ref,
):
    length = q_ref.shape[0]
    mask = same_head(WINDOW)
    ones = mask.astype(BF16)
    gamma = gamma_ref[...]
    shape = (WINDOW, WIDE)
    upper = row(shape) >= lane(shape) % HEAD
    state, state_sum = carried(carry_ref)
    fresh = fresh_ref[...] * gamma
    for p in range(GROUPS // 2):
        feats = qf_ref[:, 2 * p * FEAT : 2 * (p + 1) * FEAT]
        at = slice(p * FEAT, (p + 1) * FEAT)
        num_ref[:, at] = dot_nt(feats, state) * fresh[:, at]
        den_ref[:, at] = dot_nt(feats, state_sum) * fresh[:, at]
    for t, tile in enumerate(key_tiles(kv_ref, kf_ref, rim_kv_ref, rim_kf_ref, mask)):
        a = spans(t, length)[0][0]
        same = lambda i, j, t=t: qdoc_ref[i:j, :] == kdoc_ref[t : t + 1, :]
        _, w = weights_of(t, tile, q_ref, qf_ref, same, upper, gamma)
        num_ref[a:, :] += dot_nn(w, tile[1])
        den_ref[a:, :] += dot_nn(w, ones)
    inv = 1.0 / den_ref[...]
    att = num_ref[...] * inv
    inv_ref[...] = inv
    att_ref[...] = att
    out_ref[...] = att.astype(BF16)


def group_specs(length, half):
    first = half * PER_HALF
    column = lambda rows, width: pl.BlockSpec((rows, width), lambda g: (0, g))
    shared = lambda rows, width, at: pl.BlockSpec((rows, width), lambda g: (0, at + g))
    fixed = lambda rows, width: pl.BlockSpec((rows, width), lambda g: (0, 0))
    return dict(
        q=column(length, WIDE),
        qf=column(length, 2 * WIDE),
        k=shared(length, FEAT, first),
        rim_kv=shared(WINDOW, FEAT, first),
        rim_kf=pl.BlockSpec((WINDOW, FEAT), lambda g: (1, first + g)),
        state=shared(STATE, FEAT, first),
        back=column(STATE, FEAT),
        qdoc=fixed(length, 1),
        kdoc=fixed(8, WIDE),
        gamma=shared(1, WIDE, first),
        wide=fixed(length, WIDE),
        maps=pl.BlockSpec((GROUPS // 2, FEAT, 2 * FEAT), lambda g: (first + g, 0, 0)),
    )


def attend(half, q, qf, kv, kf, rim, carry, masks):
    length = q.shape[0]
    s = group_specs(length, half)
    return pl.pallas_call(
        attend_kernel,
        grid=(PER_HALF,),
        in_specs=[
            s["q"], s["qf"], s["k"], s["k"], s["rim_kv"], s["rim_kf"], s["state"],
            s["qdoc"], s["kdoc"], s["qdoc"], s["gamma"],
        ],
        out_specs=[s["q"]] * 3,
        out_shape=[
            jax.ShapeDtypeStruct((length, HALF), BF16),
            jax.ShapeDtypeStruct((length, HALF), F32),
            jax.ShapeDtypeStruct((length, HALF), F32),
        ],
        scratch_shapes=[pltpu.VMEM((length, WIDE), F32)] * 2,
        compiler_params=pltpu.CompilerParams(vmem_limit_bytes=VMEM_LIMIT),
        cost_estimate=pl.CostEstimate(
            flops=5_000_000_000, bytes_accessed=8 * length * D, transcendentals=0
        ),
        name="attend",
    )(q, qf, kv, kf, rim, rim, carry, masks["qdoc"], masks["kdoc"], masks["fresh"], masks["gamma"])


def scaled_grads_kernel(
    ga_ref, att_ref, inv_ref, qf_ref, fresh_ref, gamma_ref, g_ref, gd_ref, back_ref
):
    mask = same_head(HEAD)
    ga = ga_ref[...].astype(F32)
    inv = inv_ref[...]
    product = ga * att_ref[...]
    high = product.astype(BF16)
    rest = (product - high.astype(F32)).astype(BF16)
    ones = mask.astype(BF16)
    gd = -(dot_nn(high, ones) + dot_nn(rest, ones)) * inv
    g = ga * inv
    g_ref[...] = g.astype(BF16)
    gd_ref[...] = gd
    fresh = fresh_ref[...] * gamma_ref[...]
    fresh_g = (g * fresh).astype(BF16)
    fresh_gd = (gd * fresh).astype(BF16)
    kv = sums = 0.0
    for p in range(GROUPS // 2):
        feats = qf_ref[:, 2 * p * FEAT : 2 * (p + 1) * FEAT]
        at = slice(p * FEAT, (p + 1) * FEAT)
        kv += fold_pair(dot_tn(fresh_g[:, at], feats), HEAD)
        sums += fold_pair(dot_tn(fresh_gd[:, at], feats), HEAD)
    back_ref[:HEAD, :] = kv.astype(BF16)
    back_ref[HEAD:, :] = sums[: STATE - HEAD].astype(BF16)


def scaled_grads(half, ga, att, inv, qf, masks):
    length = ga.shape[0]
    s = group_specs(length, half)
    return pl.pallas_call(
        scaled_grads_kernel,
        grid=(PER_HALF,),
        in_specs=[s["q"], s["q"], s["q"], s["qf"], s["qdoc"], s["gamma"]],
        out_specs=[s["q"], s["q"], s["back"]],
        out_shape=[
            jax.ShapeDtypeStruct((length, HALF), BF16),
            jax.ShapeDtypeStruct((length, HALF), F32),
            jax.ShapeDtypeStruct((STATE, PER_HALF * FEAT), BF16),
        ],
        compiler_params=pltpu.CompilerParams(vmem_limit_bytes=VMEM_LIMIT),
        name="scaled_grads",
    )(ga, att, inv, qf, masks["fresh"], masks["gamma"])


def attend_back_kernel(
    q_ref, qf_ref, kv_ref, kf_ref, rim_kv_ref, rim_kf_ref, carry_ref, g_ref, gd_ref,
    qdoc_ref, kdoc_ref, fresh_ref, gamma_ref, maps_ref, cos_ref, sin_ref,
    raw_ref, dkv_ref, dkf_ref, rim_ref, dmap_ref, logit_ref, dq_ref, dqf_ref,
):
    length = q_ref.shape[0]
    mask = same_head(WINDOW)
    gamma = gamma_ref[...]
    shape = (WINDOW, WIDE)
    upper = row(shape) >= lane(shape) % HEAD
    state, state_sum = carried(carry_ref)
    fresh = fresh_ref[...] * gamma
    pairs = range(GROUPS // 2)
    half = lambda p: slice(p * FEAT, (p + 1) * FEAT)
    full = lambda p: slice(2 * p * FEAT, 2 * (p + 1) * FEAT)
    fresh_g = (g_ref[...].astype(F32) * fresh).astype(BF16)
    fresh_gd = (gd_ref[...] * fresh * (1.0 / HEAD)).astype(BF16)
    for p in pairs:
        dqf_ref[:, full(p)] = dot_nn(fresh_g[:, half(p)], state) + dot_nn(
            fresh_gd[:, half(p)], state_sum
        )
    dq_ref[...] = jnp.zeros_like(dq_ref)
    lo = low_half((WINDOW, FEAT))
    for t, tile in enumerate(key_tiles(kv_ref, kf_ref, rim_kv_ref, rim_kf_ref, mask)):
        (a, b), (_, c), _ = spans(t, length)
        same = lambda i, j, t=t: qdoc_ref[i:j, :] == kdoc_ref[t : t + 1, :]
        e, w = weights_of(t, tile, q_ref, qf_ref, same, upper, gamma)
        g = g_ref[a:, :]
        x = dot_nt(g, tile[1]) + gd_ref[a:, :]
        near = x[: c - a] * e
        parts = []
        if b > a:
            parts.append(jnp.where(same(a, b) & upper, near[: b - a], 0.0))
        if c > b:
            parts.append(jnp.where(same(b, c), jnp.where(upper, 0.0, near[b - a :]), 0.0))
        ds = jnp.concatenate(parts, axis=0).astype(BF16)
        dq_ref[a:c, :] += dot_nn(ds, tile[0])
        dk = fold_heads(dot_tn(ds, q_ref[a:c, :]), mask) * SCALE
        dv = fold_heads(dot_tn(w, g), mask)
        at = slice((t - 1) * WINDOW, t * WINDOW)
        dkv = jnp.where(lo, dk, dv)
        if t:
            dkv_ref[at, :] = dkv
        else:
            rim_ref[:WINDOW, :] = dkv.astype(BF16)
        if b < length:
            far = x[b - a :] * gamma
            parts = [jnp.where(same(b, c) & upper, far[: c - b], 0.0)]
            if c < length:
                parts.append(jnp.where(same(c, length), far[c - b :], 0.0))
            dl = jnp.concatenate(parts, axis=0).astype(BF16)
            dkf = 0.0
            for p in pairs:
                dqf_ref[b:, full(p)] += dot_nn(dl[:, half(p)], tile[2])
                dkf += fold_pair(dot_tn(dl[:, half(p)], qf_ref[b:, full(p)]), HEAD)
            if t:
                dkf_ref[at, :] = dkf
            else:
                rim_ref[WINDOW:, :] = dkf.astype(BF16)
        else:
            dkf_ref[at, :] = jnp.zeros((WINDOW, FEAT), F32)
    for p in pairs:
        grads = []
        for h in (2 * p, 2 * p + 1):
            f = qf_ref[:, h * FEAT : (h + 1) * FEAT].astype(F32)
            gu, t = halves_softmax_back(f, dqf_ref[:, h * FEAT : (h + 1) * FEAT])
            grads.append(gu.astype(BF16))
            total = jnp.sum(jnp.sum(t, axis=0, keepdims=True), axis=1, keepdims=True)
            logit_ref[0, h : h + 1, :] = jnp.zeros((1, FEAT), F32) + total
        gu = jnp.concatenate(grads, axis=1)
        dq_ref[:, half(p)] += 0.5 * dot_nt(gu, maps_ref[p])
        dmap = dot_tn(q_ref[:, half(p)], gu)
        dmap_ref[2 * p] = dmap[:HEAD, :FEAT]
        dmap_ref[2 * p + 1] = dmap[HEAD:, FEAT:]
    raw_ref[...] = turn(dq_ref[...], cos_ref[...], -sin_ref[...]).astype(BF16)


def attend_back(half, q, qf, kv, kf, rim, carry, g, gd, masks, maps):
    length = q.shape[0]
    s = group_specs(length, half)
    column = lambda rows: pl.BlockSpec((rows, FEAT), lambda g: (0, g))
    return pl.pallas_call(
        attend_back_kernel,
        grid=(PER_HALF,),
        in_specs=[
            s["q"], s["qf"], s["k"], s["k"], s["rim_kv"], s["rim_kf"], s["state"], s["q"], s["q"],
            s["qdoc"], s["kdoc"], s["qdoc"], s["gamma"], s["maps"], s["wide"], s["wide"],
        ],
        out_specs=[
            s["q"], column(length), column(length), column(2 * WINDOW),
            pl.BlockSpec((GROUPS, HEAD, FEAT), lambda g: (g, 0, 0)),
            pl.BlockSpec((1, 8, FEAT), lambda g: (g, 0, 0)),
        ],
        out_shape=[
            jax.ShapeDtypeStruct((length, HALF), BF16),
            jax.ShapeDtypeStruct((length, PER_HALF * FEAT), F32),
            jax.ShapeDtypeStruct((length, PER_HALF * FEAT), F32),
            jax.ShapeDtypeStruct((2 * WINDOW, PER_HALF * FEAT), BF16),
            jax.ShapeDtypeStruct((HEADS // HALVES, HEAD, FEAT), F32),
            jax.ShapeDtypeStruct((PER_HALF, 8, FEAT), F32),
        ],
        scratch_shapes=[pltpu.VMEM((length, WIDE), F32), pltpu.VMEM((length, 2 * WIDE), F32)],
        compiler_params=pltpu.CompilerParams(vmem_limit_bytes=VMEM_LIMIT),
        cost_estimate=pl.CostEstimate(
            flops=15_000_000_000, bytes_accessed=8 * length * D, transcendentals=0
        ),
        name="attend_back",
    )(
        q, qf, kv, kf, rim, rim, carry, g, gd,
        masks["qdoc"], masks["kdoc"], masks["fresh"], masks["gamma"],
        maps, masks["cos"], masks["sin"],
    )


def keys_back_kernel(
    kv_ref, kf_ref, dkv_ref, dkf_ref, rim_kv_ref, rim_kf_ref, near_ref, far_ref, survive_ref,
    maps_ref, cos_ref, sin_ref, rk_ref, rv_ref, dmap_ref,
):
    length = kv_ref.shape[0]
    cut = length - WINDOW
    lo = low_half((length, FEAT))
    survive = survive_ref[...]
    dkv, grads = [], []
    for h in range(2):
        at = slice(h * FEAT, (h + 1) * FEAT)
        kv = kv_ref[:, at].astype(F32)
        kf = kf_ref[:, at]
        v_low = pltpu.roll(kv, HEAD, 1)
        ones = jnp.where(lane((length, FEAT)) == HEAD, 1.0, 0.0)
        v_one = jnp.where(lo, v_low, ones).astype(BF16)[:, :STATE]
        dkf, dv = [], []
        for back, part in ((near_ref, slice(0, cut)), (far_ref, slice(cut, length))):
            state = back[:, at]
            twice = jnp.concatenate([state[:HEAD], state[:HEAD]], axis=0)
            dkf.append(dot_nn(v_one[part], state))
            dv.append(dot_nt(kf[part], twice))
        rim = jnp.zeros((cut, FEAT), F32)
        dkf = (
            jnp.concatenate(dkf, axis=0) * survive
            + dkf_ref[:, at]
            + jnp.concatenate([rim, rim_kf_ref[:, at].astype(F32)], axis=0)
        )
        dv = jnp.concatenate(dv, axis=0) * survive
        total = (
            dkv_ref[:, at]
            + jnp.concatenate([rim, rim_kv_ref[:, at].astype(F32)], axis=0)
            + jnp.where(lo, 0.0, dv)
        )
        gu, _ = halves_softmax_back(kf.astype(F32), dkf)
        grads.append(gu.astype(BF16))
        dkv.append(total)
    gu = jnp.concatenate(grads, axis=1)
    keys = jnp.where(lo, kv_ref[:, :FEAT].astype(F32), pltpu.roll(kv_ref[:, FEAT:].astype(F32), HEAD, 1))
    dmap = dot_tn(keys.astype(BF16), gu)
    dmap_ref[0] = dmap[:HEAD, :FEAT]
    dmap_ref[1] = dmap[HEAD:, FEAT:]
    dk = jnp.where(lo, dkv[0], pltpu.roll(dkv[1], HEAD, 1)) + 0.5 * dot_nt(gu, maps_ref[0])
    rk_ref[...] = turn(dk, cos_ref[...], -sin_ref[...]).astype(BF16)
    rv_ref[...] = jnp.where(lo, pltpu.roll(dkv[0], HEAD, 1), dkv[1]).astype(BF16)


def keys_back(half, kv, kf, dkv, dkf, rim, near, far, masks, maps):
    length = kv.shape[0]
    pairs = PER_HALF // 2
    first = half * pairs
    column = lambda rows: pl.BlockSpec((rows, 2 * FEAT), lambda g: (0, g))
    shared = pl.BlockSpec((length, 2 * FEAT), lambda g: (0, first + g))
    state = pl.BlockSpec((STATE, 2 * FEAT), lambda g: (0, first + g))
    narrow = pl.BlockSpec((length, FEAT), lambda g: (0, 0))
    out = pl.BlockSpec((length, FEAT), lambda g: (0, g))
    return pl.pallas_call(
        keys_back_kernel,
        grid=(pairs,),
        in_specs=[
            shared, shared, column(length), column(length),
            column(WINDOW), pl.BlockSpec((WINDOW, 2 * FEAT), lambda g: (1, g)),
            state, state, pl.BlockSpec((length, 1), lambda g: (0, 0)),
            pl.BlockSpec((1, FEAT, 2 * FEAT), lambda g: (first + g, 0, 0)), narrow, narrow,
        ],
        out_specs=[out, out, pl.BlockSpec((2, HEAD, FEAT), lambda g: (g, 0, 0))],
        out_shape=[
            jax.ShapeDtypeStruct((length, KVD // HALVES), BF16),
            jax.ShapeDtypeStruct((length, KVD // HALVES), BF16),
            jax.ShapeDtypeStruct((PER_HALF, HEAD, FEAT), F32),
        ],
        compiler_params=pltpu.CompilerParams(vmem_limit_bytes=VMEM_LIMIT),
        name="keys_back",
    )(
        kv, kf, dkv, dkf, rim, rim, near, far, masks["survive"], maps, masks["cos"], masks["sin"]
    )


def out_project_kernel(*refs, counts, size):
    n = len(counts)
    places, blocks, refs = refs[0], refs[1 : 1 + n], refs[1 + n :]
    m0, m1, hidden, proj_in, proj_out, gain = refs[:6]
    residual, second, low, inverse, w, sem = refs[6:]
    start_rows(places, blocks, counts, size, w, sem)
    reduced = dot_nn(m0[...], proj_in[:HALF, :]) + dot_nn(m1[...], proj_in[HALF:, :])
    reduced = reduced.astype(BF16)
    low[...] = reduced
    wait_rows(w, sem)
    squares = 0.0
    for j in range(D // WIDE):
        at = slice(j * WIDE, (j + 1) * WIDE)
        sums = (
            hidden[:, at].astype(F32)
            + dot_nn(m0[...], w[:HALF, at])
            + dot_nn(m1[...], w[HALF:, at])
            + dot_nn(reduced, proj_out[:, at])
        )
        residual[:, at] = sums
        squares = squares + jnp.sum(sums * sums, axis=1, keepdims=True)
    inv = lax.rsqrt(squares * (1.0 / D) + EPSILON)
    inverse[...] = jnp.zeros(inverse.shape, F32) + inv
    second[...] = (residual[...] * inv * gain[...]).astype(BF16)


def out_project(w, merged, hidden, proj_in, proj_out, gain):
    length = hidden.shape[0]
    shapes = (
        jax.ShapeDtypeStruct((length, D), F32),
        jax.ShapeDtypeStruct((length, D), BF16),
        jax.ShapeDtypeStruct((length, LOW), BF16),
        jax.ShapeDtypeStruct((length, LOW), F32),
    )
    rest = (*merged, hidden, proj_in, proj_out, gain)
    return pl.pallas_call(
        functools.partial(out_project_kernel, counts=w.shapes(), size=w.size),
        grid=(1,),
        in_specs=[SCALARS] + [ANYWHERE] * len(w.blocks) + [whole(a) for a in rest],
        out_specs=[whole(v) for v in shapes],
        out_shape=shapes,
        scratch_shapes=[pltpu.VMEM((D, D), BF16), pltpu.SemaphoreType.DMA],
        compiler_params=pltpu.CompilerParams(vmem_limit_bytes=VMEM_LIMIT),
        cost_estimate=pl.CostEstimate(
            flops=2 * length * D * D, bytes_accessed=2 * D * D, transcendentals=0
        ),
        name="out_project",
    )(w.places, *w.blocks, *rest)


def branch_back_kernel(*refs, counts, size, extra):
    n = len(counts)
    places, blocks, refs = refs[0], refs[1 : 1 + n], refs[1 + n :]
    sums, refs = refs[:extra], refs[extra:]
    cot, residual, inverse, gain, proj_in, proj_out, m0, m1, low = refs[:9]
    grad_residual, g0, g1, grad_gain, grad_in, grad_out, w, sem = refs[9:]
    start_rows(places, blocks, counts, size, w, sem)
    total = sums[0][...].astype(F32)
    for v in sums[1:]:
        total = total + v[...].astype(F32)
    inv = inverse[:, :1]
    normed = residual[...] * inv
    product = total * normed
    grad_gain[...] = jnp.sum(product, axis=0, keepdims=True)
    scaled = total * gain[...]
    mean = jnp.sum(scaled * normed, axis=1, keepdims=True) * (1.0 / D)
    grad = cot[...].astype(F32) + inv * (scaled - normed * mean)
    grad_residual[...] = grad
    branch = grad.astype(BF16)
    grad_low = dot_nt(branch, proj_out[...]).astype(BF16)
    grad_out[...] = dot_tn(low[...], branch)
    for i, m in enumerate((m0, m1)):
        grad_in[:, i * HALF : (i + 1) * HALF] = dot_tn(grad_low, m[...])
    wait_rows(w, sem)
    for j in range(D // WIDE):
        at = slice(j * WIDE, (j + 1) * WIDE)
        i, col = j // (HALF // WIDE), (j % (HALF // WIDE)) * WIDE
        back = dot_nt(grad_low, proj_in[at, :]) + dot_nt(branch, w[at, :])
        (g0, g1)[i][:, col : col + WIDE] = back.astype(BF16)


def branch_back(w, sums, cot, residual, inverse, gain, proj_in, proj_out, merged, low):
    length = cot.shape[0]
    shapes = (
        jax.ShapeDtypeStruct((length, D), F32),
        jax.ShapeDtypeStruct((length, HALF), BF16),
        jax.ShapeDtypeStruct((length, HALF), BF16),
        jax.ShapeDtypeStruct((1, D), F32),
        jax.ShapeDtypeStruct((LOW, D), F32),
        jax.ShapeDtypeStruct((LOW, D), F32),
    )
    rest = (*sums, cot, residual, inverse, gain, proj_in, proj_out, *merged, low)
    return pl.pallas_call(
        functools.partial(
            branch_back_kernel, counts=w.shapes(), size=w.size, extra=len(sums)
        ),
        grid=(1,),
        in_specs=[SCALARS] + [ANYWHERE] * len(w.blocks) + [whole(a) for a in rest],
        out_specs=[whole(v) for v in shapes],
        out_shape=shapes,
        scratch_shapes=[pltpu.VMEM((D, D), BF16), pltpu.SemaphoreType.DMA],
        compiler_params=pltpu.CompilerParams(vmem_limit_bytes=VMEM_LIMIT),
        cost_estimate=pl.CostEstimate(
            flops=2 * length * D * D, bytes_accessed=2 * D * D, transcendentals=0
        ),
        name="branch_back",
    )(w.places, *w.blocks, *rest)


def inputs_back_kernel(*refs, counts, size):
    n = len(counts)
    places, blocks, refs = refs[0], refs[1 : 1 + n], refs[1 + n :]
    raws, refs = refs[:6], refs[6:]
    p_in, p_out, low, x, hidden, gain, grad_residual = refs[:7]
    grad_tokens, grad_gain, grad_in, grad_out, w, raw, back, sem = refs[7:]
    start_rows(places, blocks, counts, size, w, sem)
    at = 0
    for r in raws:
        raw[:, at : at + r.shape[1]] = r[...]
        at += r.shape[1]
    grad_low = dot_nt(raw[...], p_out[...]).astype(BF16)
    grad_out[...] = dot_tn(low[...], raw[...])
    grad_in[...] = dot_tn(grad_low, x[...])
    wait_rows(w, sem)
    values = hidden[...].astype(F32)
    inv = lax.rsqrt(jnp.sum(values * values, axis=1, keepdims=True) * (1.0 / D) + EPSILON)
    mean = 0.0
    for j in range(D // WIDE):
        at = slice(j * WIDE, (j + 1) * WIDE)
        part = dot_nt(grad_low, p_in[at, :]) + dot_nt(raw[...], w[at, :])
        normed = hidden[:, at].astype(F32) * inv
        product = part * normed
        grad_gain[:, at] = jnp.sum(product, axis=0, keepdims=True)
        mean = mean + jnp.sum(product * gain[:, at], axis=1, keepdims=True)
        back[:, at] = part
    mean = mean * (1.0 / D)
    grad_tokens[...] = grad_residual[...] + inv * (
        back[...] * gain[...] - values * inv * mean
    )


def inputs_back(w, raws, p_in, p_out, low, x, hidden, gain, grad_residual):
    length = x.shape[0]
    shapes = (
        jax.ShapeDtypeStruct((length, D), F32),
        jax.ShapeDtypeStruct((1, D), F32),
        jax.ShapeDtypeStruct((LOW, D), F32),
        jax.ShapeDtypeStruct((LOW, QKV), F32),
    )
    rest = (*raws, p_in, p_out, low, x, hidden, gain, grad_residual)
    return pl.pallas_call(
        functools.partial(inputs_back_kernel, counts=w.shapes(), size=w.size),
        grid=(1,),
        in_specs=[SCALARS] + [ANYWHERE] * len(w.blocks) + [whole(a) for a in rest],
        out_specs=[whole(v) for v in shapes],
        out_shape=shapes,
        scratch_shapes=[
            pltpu.VMEM((D, QKV), BF16),
            pltpu.VMEM((length, QKV), BF16),
            pltpu.VMEM((length, D), F32),
            pltpu.SemaphoreType.DMA,
        ],
        compiler_params=pltpu.CompilerParams(vmem_limit_bytes=VMEM_LIMIT),
        cost_estimate=pl.CostEstimate(
            flops=2 * length * D * QKV, bytes_accessed=2 * D * QKV, transcendentals=0
        ),
        name="inputs_back",
    )(w.places, *w.blocks, *rest)


def mlp_kernel(places_ref, *refs, rows, parts, tile):
    n = len(rows[0]) + len(rows[1])
    tokens, refs = refs[:n], refs[n:]
    own_gu, own_dn = refs[:2]
    pair_gu, pair_dn, refs = refs[2 : 2 + parts], refs[2 + parts : 2 + 2 * parts], refs[2 + 2 * parts :]
    out_ref, back_ref, h, c, gu, dn, out, back, row_sem, gu_sem, dn_sem = refs
    step, steps = pl.program_id(0), pl.num_programs(0)
    own_tiles = own_gu.shape[2] // tile
    width = D // parts

    def fetch(i, slot):
        @pl.when(i < own_tiles)
        def _():
            at = pl.ds(pl.multiple_of(i * tile, tile), tile)
            pltpu.make_async_copy(own_gu.at[:, :, at], gu.at[slot], gu_sem.at[slot]).start()
            pltpu.make_async_copy(own_dn.at[at, :], dn.at[slot], dn_sem.at[slot]).start()

        @pl.when(i >= own_tiles)
        def _():
            at = pl.ds(pl.multiple_of((i - own_tiles) * tile, tile), tile)
            for k in range(parts):
                there = pl.ds(pl.multiple_of(places_ref[k] * width, width), width)
                pltpu.make_async_copy(
                    pair_gu[k].at[:, :, at], gu.at[slot, :, there, :], gu_sem.at[slot]
                ).start()
                pltpu.make_async_copy(
                    pair_dn[k].at[at, :], dn.at[slot, :, there], dn_sem.at[slot]
                ).start()

    @pl.when(step == 0)
    def _():
        fetch(step, 0)
        copies = []
        for target, sizes in zip((h, c), rows):
            at = 0
            for size in sizes:
                i = len(copies)
                there = target.at[at : at + size]
                copies.append(pltpu.make_async_copy(tokens[i], there, row_sem.at[i]))
                at += size
        for copy in copies:
            copy.start()
        out[...] = jnp.zeros_like(out)
        back[...] = jnp.zeros_like(back)
        for copy in copies:
            copy.wait()

    slot = step % 2

    @pl.when(step + 1 < steps)
    def _():
        fetch(step + 1, 1 - slot)

    pltpu.make_async_copy(own_gu.at[:, :, pl.ds(0, tile)], gu.at[slot], gu_sem.at[slot]).wait()
    pltpu.make_async_copy(own_dn.at[pl.ds(0, tile), :], dn.at[slot], dn_sem.at[slot]).wait()
    w_gate, w_up, w_down = gu.at[slot, 0], gu.at[slot, 1], dn.at[slot]
    gate = dot_nn(h[...], w_gate[...])
    up = dot_nn(h[...], w_up[...])
    grad = dot_nt(c[...], w_down[...])
    sig = jax.nn.sigmoid(gate)
    silu = gate * sig
    act = (silu * up).astype(BF16)
    grad_gate = (grad * up * sig * (1.0 + gate * (1.0 - sig))).astype(BF16)
    grad_up = (grad * silu).astype(BF16)
    out[...] += dot_nn(act, w_down[...])
    back[...] += dot_nt(grad_gate, w_gate[...]) + dot_nt(grad_up, w_up[...])

    @pl.when(step == steps - 1)
    def _():
        out_ref[...] = out[...].astype(BF16)
        back_ref[...] = back[...].astype(BF16)


def mlp(second, cot, own_gu, own_dn, pair, places):
    rows = tuple(v.shape[0] for v in second), tuple(v.shape[0] for v in cot)
    total = sum(rows[0])
    hidden = own_gu.shape[2]
    tile = min(256, hidden)
    parts = len(pair)
    anywhere = pl.BlockSpec(memory_space=pl.ANY)
    whole = pl.BlockSpec((total, D), lambda i, p: (0, 0))
    return pl.pallas_call(
        functools.partial(mlp_kernel, rows=rows, parts=parts, tile=tile),
        grid_spec=pltpu.PrefetchScalarGridSpec(
            num_scalar_prefetch=1,
            grid=(2 * hidden // tile,),
            in_specs=[anywhere] * (len(second) + len(cot) + 2 + 2 * parts),
            out_specs=[whole, whole],
            scratch_shapes=[
                pltpu.VMEM((total, D), BF16),
                pltpu.VMEM((total, D), BF16),
                pltpu.VMEM((2, 2, D, tile), BF16),
                pltpu.VMEM((2, tile, D), BF16),
                pltpu.VMEM((total, D), F32),
                pltpu.VMEM((total, D), F32),
                pltpu.SemaphoreType.DMA((len(second) + len(cot),)),
                pltpu.SemaphoreType.DMA((2,)),
                pltpu.SemaphoreType.DMA((2,)),
            ],
        ),
        out_shape=[jax.ShapeDtypeStruct((total, D), BF16)] * 2,
        compiler_params=pltpu.CompilerParams(vmem_limit_bytes=VMEM_LIMIT),
        cost_estimate=pl.CostEstimate(
            flops=12 * total * D * hidden * 2, bytes_accessed=12 * D * hidden, transcendentals=0
        ),
        name="mlp",
    )(places, *second, *cot, own_gu, own_dn, *[p[0] for p in pair], *[p[1] for p in pair])


class Grid:
    def __init__(self):
        self.seq = lax.axis_size("seq")
        self.rows = lax.axis_size("rows")
        self.zs = Z_SIZE
        self.xs = self.rows // Z_SIZE
        self.ys = self.seq // CORES
        s = lax.axis_index("seq")
        r = lax.axis_index("rows")
        self.y, self.c = s // CORES, s % CORES
        self.z, self.x = r // self.xs, r % self.xs
        self.s, self.r = s, r

    def send(self, value, move):
        route = []
        for s in range(self.seq):
            for r in range(self.rows):
                there = move(s // CORES, s % CORES, r // self.xs, r % self.xs)
                if there is not None:
                    y, c, z, x = there
                    target = (y * CORES + c) * self.rows + z * self.xs + x
                    route.append((s * self.rows + r, target))
        return jax.tree.map(lambda v: lax.ppermute(v, ("seq", "rows"), route), value)

    def along_z(self, value, k):
        return self.send(value, lambda y, c, z, x: (y, c, (z + k) % self.zs, x))

    def along_x(self, value, k):
        return self.send(value, lambda y, c, z, x: (y, c, z, (x + k) % self.xs))

    def along_y(self, value, k):
        return self.send(value, lambda y, c, z, x: ((y + k) % self.ys, c, z, x))

    def flip_z(self, value, bit):
        return self.send(value, lambda y, c, z, x: (y, c, z ^ bit, x))

    def flip_core(self, value):
        return self.send(value, lambda y, c, z, x: (y, 1 - c, z, x))

    def flip_row(self, value, bit):
        def move(y, c, z, x):
            r = (z * self.xs + x) ^ bit
            return (y, c, r // self.xs, r % self.xs)

        return self.send(value, move)

    def along_seq(self, value, k):
        def move(y, c, z, x):
            s = y * CORES + c + k
            return (s // CORES, s % CORES, z, x) if 0 <= s < self.seq else None

        return self.send(value, move)


def after(values, *events):
    return lax.optimization_barrier((values, *events))[0]


class Gather:
    def __init__(self, grid, shard):
        self.grid = grid
        self.size = shard.shape[0] // grid.seq
        self.own = lax.dynamic_slice_in_dim(shard, grid.s * self.size, self.size, 0)

    def over_z(self):
        grid = self.grid
        pieces = [self.own] + [grid.along_z(self.own, k) for k in range(1, grid.zs)]
        half = grid.zs // 2
        self.halves = [jnp.concatenate(pieces[:half]), jnp.concatenate(pieces[half:])]

    def first(self):
        grid = self.grid
        a, b = self.halves
        self.moved = [
            [grid.along_x(a, k) for k in range(1, grid.xs)],
            [grid.along_y(b, k) for k in range(1, grid.ys)],
        ]

    def second(self):
        grid = self.grid
        a, b = (jnp.concatenate([h, *m]) for h, m in zip(self.halves, self.moved))
        self.blocks = [a, b]
        self.last = [grid.along_y(a, k) for k in range(1, grid.ys)]
        self.last += [grid.along_x(b, k) for k in range(1, grid.xs)]

    def cores(self):
        self.over = [self.grid.flip_core(b) for b in self.blocks]

    def result(self):
        grid = self.grid
        blocks = self.blocks + self.last
        blocks = blocks + self.over + [grid.flip_core(b) for b in self.last]
        places = []
        kzs = range(grid.zs // 2), range(grid.zs // 2, grid.zs)
        a = [(kx, 0, kz) for kx in range(grid.xs) for kz in kzs[0]]
        b = [(0, ky, kz) for ky in range(grid.ys) for kz in kzs[1]]
        moves = a + b
        for k in range(1, grid.ys):
            moves = moves + [(kx, k, kz) for kx, _, kz in a]
        for k in range(1, grid.xs):
            moves = moves + [(k, ky, kz) for _, ky, kz in b]
        for core in range(CORES):
            c = (grid.c + core) % CORES
            for kx, ky, kz in moves:
                z, x, y = (grid.z - kz) % grid.zs, (grid.x - kx) % grid.xs, (grid.y - ky) % grid.ys
                places.append((z * grid.xs + x) * grid.seq + y * CORES + c)
        return Gathered(blocks, jnp.stack(places).astype(jnp.int32), self.size)


class Pair:
    def __init__(self, grid, gate_up, down):
        self.grid = grid
        part = D // grid.seq
        self.gu = lax.dynamic_slice_in_dim(gate_up, grid.s * part, part, 1)
        self.dn = lax.dynamic_slice_in_dim(down, grid.s * part, part, 1)

    def gate_up_z(self):
        self.gu = [self.grid.flip_z(self.gu, FAR_BIT)]

    def down_z(self):
        self.dn = [self.grid.flip_z(self.dn, FAR_BIT)]

    def gate_up_y(self):
        self.gu += [self.grid.along_y(self.gu[0], k) for k in range(1, self.grid.ys)]

    def down_y(self):
        self.dn += [self.grid.along_y(self.dn[0], k) for k in range(1, self.grid.ys)]

    def result(self):
        grid = self.grid
        gus = self.gu + [grid.flip_core(v) for v in self.gu]
        dns = self.dn + [grid.flip_core(v) for v in self.dn]
        places = [grid.s] + [(grid.y - k) % grid.ys * CORES + grid.c for k in range(1, grid.ys)]
        places = places + [p + 1 - 2 * grid.c for p in places]
        return list(zip(gus, dns)), jnp.stack(places).astype(jnp.int32)


def spread_near(grid, block):
    return [block] + [grid.along_x(block, k) for k in range(1, grid.xs)]


def spread_far(grid, block, parts):
    size = block.shape[0] // parts
    pieces = [grid.flip_z(block[p * size : (p + 1) * size], NEAR_BIT) for p in range(parts)]
    return pieces, lambda pieces: list(pieces) + [
        grid.along_x(piece, k) for k in range(1, grid.xs) for piece in pieces
    ]


def collect(grid, near, far, length, parts):
    size = length // parts
    terms = [near[:length]]
    send = []
    for p in range(parts):
        lo = p * size
        total = far[lo : lo + size]
        for k in range(1, grid.xs):
            other = grid.along_x(far[k * length + lo : k * length + lo + size], -k)
            total = (total.astype(F32) + other.astype(F32)).astype(BF16)
        send.append(total)
    for k in range(1, grid.xs):
        terms.append(grid.along_x(near[k * length : (k + 1) * length], -k))
    return terms, send


def total_over_all(grid, values):
    widths = [v.shape[2] for v in values]
    packed = jnp.concatenate([v.astype(BF16) for v in values], axis=2)
    packed = jnp.pad(packed, ((0, 0), (0, 0), (0, -packed.shape[2] % FEAT)))
    packed = packed.reshape(grid.ys, CORES, 8, -1)
    own = lax.dynamic_index_in_dim(packed, grid.c, 1, False)
    other = lax.dynamic_index_in_dim(packed, 1 - grid.c, 1, False)
    both = (own.astype(F32) + grid.flip_core(other).astype(F32)).astype(BF16)
    total = lax.dynamic_index_in_dim(both, grid.y, 0, False).astype(F32)
    for k in range(1, grid.ys):
        part = lax.dynamic_index_in_dim(both, (grid.y + k) % grid.ys, 0, False)
        total = total + grid.along_y(part, k).astype(F32)
    bit = 1
    while bit < grid.rows:
        mine = total.astype(BF16)
        total = mine.astype(F32) + grid.flip_row(mine, bit).astype(F32)
        bit *= 2
    out, at = [], 0
    for w in widths:
        out.append(total[:, at : at + w])
        at += w
    return out


def pair_maps(maps):
    both = jnp.concatenate([maps, -maps], axis=-1)
    both = both.reshape(-1, 2, HEAD, FEAT)
    none = jnp.zeros_like(both[:, 0])
    return jnp.concatenate(
        [
            jnp.concatenate([both[:, 0], none], axis=-1),
            jnp.concatenate([none, both[:, 1]], axis=-1),
        ],
        axis=1,
    )


def adapters(query, key, value, axis):
    if axis == 1:
        joined = jnp.concatenate([query, key, value], axis=1)
        return jnp.pad(joined, ((0, 0), (0, LOW - joined.shape[1])))
    rank = query.shape[0]
    joined = jnp.zeros((LOW, QKV), query.dtype)
    joined = joined.at[:rank, :D].set(query)
    joined = joined.at[rank : 2 * rank, D : D + KVD].set(key)
    return joined.at[2 * rank : 3 * rank, D + KVD :].set(value)


def documents(grid, starts, length):
    own = starts.astype(BF16)
    other = grid.flip_core(own)
    chip = jnp.where(grid.c == 0, jnp.concatenate([own, other]), jnp.concatenate([other, own]))
    resets = jnp.zeros((grid.ys, chip.shape[0]), BF16)
    resets = lax.dynamic_update_slice(resets, chip[None], (grid.y, 0))
    for k in range(1, grid.ys):
        got = grid.along_y(chip, k)
        resets = lax.dynamic_update_slice(resets, got[None], ((grid.y - k) % grid.ys, 0))
    heard = resets
    resets = resets.reshape(-1).astype(jnp.int32)
    places = jnp.arange(resets.shape[0], dtype=jnp.int32)
    docs = jnp.cumsum(jnp.where(places == 0, 1, resets))
    padded = jnp.concatenate([jnp.full((WINDOW,), -1, jnp.int32), docs])
    extended = lax.dynamic_slice_in_dim(padded, grid.s * length, length + WINDOW, 0)
    own = extended[WINDOW:]
    before = extended[WINDOW - 1]
    last = own[-1]
    ends = docs[length - 1 :: length]
    places = jnp.arange(grid.seq, dtype=jnp.int32)
    tiles = jnp.tile(extended.reshape(-1, 1, WINDOW), (1, GROUPS, 1)).reshape(-1, WIDE)
    masks = dict(
        qdoc=own[:, None],
        kdoc=jnp.pad(tiles, ((0, 8 - tiles.shape[0]), (0, 0))),
        fresh=(own == before).astype(F32)[:, None],
        survive=(own == last).astype(F32)[:, None],
    )
    earlier = ((ends == before) & (places < grid.s)).astype(F32)
    entered = jnp.concatenate([jnp.full((1,), -1, jnp.int32), ends[:-1]])
    later = ((entered == last) & (places > grid.s)).astype(F32)
    pick = lambda v, k: lax.dynamic_index_in_dim(v, jnp.clip(grid.s + k, 0, grid.seq - 1), 0, False)
    former = [pick(earlier, -k) * (grid.s - k >= 0) for k in range(1, grid.seq)]
    latter = [pick(later, k) * (grid.s + k < grid.seq) for k in range(1, grid.seq)]
    return masks, former, latter, heard


def local(
    tokens, doc_starts, cotangent, norm_first, norm_second,
    w_query, w_key, w_value, w_out, w_gate_up, w_down,
    query_in, query_out, key_in, key_out, value_in, value_out, proj_in, proj_out,
    map_query, map_key, window_logit,
):
    grid = Grid()
    length = tokens.shape[1]
    rank = query_in.shape[1]
    hidden = tokens[0]
    grad_out = cotangent[0]
    gain_first = norm_first.astype(F32)[None, :]
    gain_second = norm_second.astype(F32)[None, :]

    masks, former, latter, heard = documents(grid, doc_starts[0], length)
    qkv = Gather(grid, jnp.concatenate([w_query, w_key, w_value], axis=1))
    out = Gather(grid, w_out)
    pair = Pair(grid, w_gate_up, w_down)
    cot_near = spread_near(grid, grad_out)
    qkv.over_z()

    values = hidden.astype(F32)
    inverse_first = lax.rsqrt(jnp.mean(values * values, axis=-1, keepdims=True) + EPSILON)
    inputs = (values * inverse_first * gain_first).astype(BF16)
    gamma = jax.nn.sigmoid(window_logit)
    masks["gamma"] = jnp.repeat(gamma, HEAD)[None, :]
    half = HEAD // 2
    inverse_freq = jnp.power(THETA, -(jnp.arange(half, dtype=F32) * 2.0 / HEAD))
    places = (grid.s * length + jnp.arange(length, dtype=jnp.int32)).astype(F32)
    angles = places[:, None] * inverse_freq[None, :]
    sine = jnp.sin(angles)
    masks["cos"] = jnp.tile(jnp.cos(angles), (1, WIDE // half))
    masks["sin"] = jnp.tile(jnp.concatenate([-sine, sine], axis=1), (1, WIDE // HEAD))
    maps_q, maps_k = pair_maps(map_query), pair_maps(map_key)
    qkv_in = adapters(query_in, key_in, value_in, 1)
    qkv_out = adapters(query_out, key_out, value_out, 0)
    o_in = jnp.pad(proj_in, ((0, 0), (0, LOW - rank)))
    o_out = jnp.pad(proj_out, ((0, LOW - rank), (0, 0)))
    low = dot_nn(inputs, qkv_in).astype(BF16)

    cot_near, qkv.halves, heard, pair.gu = after((cot_near, qkv.halves, heard, pair.gu))
    qkv.first()
    pair.gate_up_z()
    ready = (masks, former, latter, maps_q, maps_k, qkv_in, qkv_out, o_in, o_out, inputs, low)
    qkv.moved, ready = after((qkv.moved, ready))
    masks, former, latter, maps_q, maps_k, qkv_in, qkv_out, o_in, o_out, inputs, low = ready
    cosine, sine = masks["cos"], masks["sin"]
    qkv.second()
    qkv.cores()
    qkv.last, qkv.over, out.own, pair.gu = after((qkv.last, qkv.over, out.own, pair.gu))
    w_qkv = qkv.result()
    out.over_z()
    kv, kf, pack, full = project_kv(
        w_qkv, inputs, low, qkv_out[:, D:], cosine, sine, maps_k, masks["survive"]
    )
    rim = grid.along_seq(pack, 1)
    carry = former[0] * rim[2 * WINDOW :].astype(F32)
    for k in range(2, grid.seq):
        carry = carry + former[k - 1] * grid.along_seq(full, k).astype(F32)
    carry = carry.astype(BF16)
    first = project_q(0, w_qkv, inputs, low, qkv_out, cosine, sine, maps_q)
    rim, carry, first, out.halves, pair.gu, pair.dn, grad_out = after(
        (rim, carry, first, out.halves, pair.gu, pair.dn, grad_out)
    )
    out.first()
    out.second()
    out.cores()
    pair.gate_up_y()
    pair.down_z()
    cot_far, relay = spread_far(grid, grad_out, 1)
    queries, merged, attended, inverse = [], [], [], []
    for i in range(HALVES):
        q, qf = project_q(i, w_qkv, inputs, low, qkv_out, cosine, sine, maps_q) if i else first
        queries.append((q, qf))
        block = attend(i, q, qf, kv, kf, rim, carry, masks)
        merged.append(block[0])
        attended.append(block[1])
        inverse.append(block[2])

    merged, out.last, cot_far, pair.dn = after((merged, out.last, cot_far, pair.dn))
    w_o = out.result()
    pair.down_y()
    cot_far = relay(cot_far)
    pair, pair_places = pair.result()
    residual, second_in, out_low, inverse_second = out_project(
        w_o, merged, hidden, o_in, o_out, gain_second
    )
    near = spread_near(grid, second_in)
    far, relay = spread_far(grid, second_in, 2)
    far = relay(after(far, near))
    near_out, near_grad = mlp(near, cot_near, w_gate_up, w_down, pair, pair_places)
    far, near_out, near_grad = after((far, near_out, near_grad))
    far_out, far_grad = mlp(far, cot_far, w_gate_up, w_down, pair, pair_places)
    terms, send = collect(grid, near_grad, far_grad, length, 2)
    near_out, far_out = after((near_out, far_out), send)
    terms.append(jnp.concatenate([grid.flip_z(v, NEAR_BIT) for v in send], axis=0))

    grad_residual, *grad_merged, grad_gain_two, grad_proj_in, grad_proj_out = branch_back(
        w_o, terms, grad_out, residual, inverse_second, gain_second, o_in, o_out, merged, out_low
    )
    scaled = [
        scaled_grads(i, grad_merged[i], attended[i], inverse[i], queries[i][1], masks)
        for i in range(HALVES)
    ]
    back = jnp.concatenate([v[2] for v in scaled], axis=1)
    far_back = jnp.zeros(back.shape, F32)
    for k in range(2, grid.seq):
        far_back = far_back + latter[k - 1] * grid.along_seq(back, -k).astype(F32)
    near_back = far_back + latter[0] * grid.along_seq(back, -1).astype(F32)
    near_back, far_back = near_back.astype(BF16), far_back.astype(BF16)
    out_terms, send = collect(grid, near_out, far_out, length, 1)
    scaled, out_terms, send = after((scaled, out_terms, send))
    out_terms += [grid.flip_z(v, NEAR_BIT) for v in send]
    backs = [
        attend_back(i, *queries[i], kv, kf, rim, carry, *scaled[i][:2], masks, maps_q)
        for i in range(HALVES)
    ]
    raw_query = [v[0] for v in backs]
    rim_back = [grid.along_seq(v[3], -1) for v in backs]
    rim_back, out_terms = after((rim_back, out_terms))
    block_out = residual
    for term in out_terms:
        block_out = block_out + term.astype(F32)
    block_out = block_out.astype(BF16)
    raw_key, raw_value, dmap_key = [], [], []
    for i, (_, dkv, dkf, *_) in enumerate(backs):
        k, v, m = keys_back(
            i, kv, kf, dkv, dkf, rim_back[i], near_back, far_back, masks, maps_k
        )
        raw_key.append(k)
        raw_value.append(v)
        dmap_key.append(m)
    dmap_query = jnp.concatenate([v[4] for v in backs], axis=0)
    dmap_key = jnp.concatenate(dmap_key, axis=0)
    dlogit = jnp.concatenate([v[5] for v in backs], axis=0)
    grad_tokens, grad_gain_one, grad_qkv_in, grad_qkv_out = inputs_back(
        w_qkv, [*raw_query, *raw_key, *raw_value], qkv_in, qkv_out, low, inputs,
        hidden, gain_first, grad_residual,
    )
    grad_logit = dlogit[:, :GROUPS, 0].reshape(HEADS) * (1.0 - gamma)
    grad_proj_in, grad_proj_out = grad_proj_in[:rank], grad_proj_out[:rank]

    blocks = lambda v: v.reshape(8, grid.seq, -1).swapaxes(0, 1)
    plain = lambda v: v.reshape(grid.seq, 8, -1)
    outs = (
        blocks(grad_qkv_out[:rank, :D]),
        blocks(grad_qkv_out[rank : 2 * rank, D : D + KVD]),
        blocks(grad_qkv_out[2 * rank : 3 * rank, D + KVD :]),
        blocks(grad_proj_out),
    )
    ins = [blocks(grad_qkv_in[i * rank : (i + 1) * rank]) for i in range(3)]
    ins.append(blocks(grad_proj_in))
    map_q = plain(dmap_query[:, :, :HEAD].reshape(HEADS, -1))
    map_k = dmap_key[:, :, :HEAD].reshape(KV_HEADS, grid.seq, -1).swapaxes(0, 1)
    logit = jnp.pad(grad_logit.reshape(grid.seq, -1, 1), ((0, 0), (0, 8 - HEADS // grid.seq), (0, 0)))
    sums = total_over_all(
        grid, [*outs, *ins, map_q, map_k, plain(grad_gain_one), plain(grad_gain_two), logit]
    )
    outs, ins, (map_q, map_k, gain_one, gain_two, logit) = sums[:4], sums[4:8], sums[8:]
    width = D // grid.seq
    return (
        block_out[None],
        grad_tokens[None],
        gain_one.reshape(width),
        gain_two.reshape(width),
        ins[0].T,
        outs[0],
        ins[1].T,
        outs[1],
        ins[2].T,
        outs[2],
        ins[3].T,
        outs[3],
        map_q.reshape(-1, HEAD, HEAD),
        map_k.reshape(KV_HEADS, -1, HEAD),
        logit[: HEADS // grid.seq, 0],
    )


def solution(mesh):
    placed = (
        P("rows", "seq", None),
        P("rows", "seq"),
        P("rows", "seq", None),
        P(),
        P(),
        P("rows", None),
        P("rows", None),
        P("rows", None),
        P("rows", None),
        P(None, None, "rows"),
        P("rows", None),
        P(),
        P(),
        P(),
        P(),
        P(),
        P(),
        P(),
        P(),
        P(),
        P(),
        P(),
    )
    return jax.shard_map(
        local,
        mesh=mesh,
        in_specs=placed,
        out_specs=(
            P("rows", "seq", None),
            P("rows", "seq", None),
            P("seq"),
            P("seq"),
            P("seq", None),
            P(None, "seq"),
            P("seq", None),
            P(None, "seq"),
            P("seq", None),
            P(None, "seq"),
            P("seq", None),
            P(None, "seq"),
            P("seq", None, None),
            P(None, "seq", None),
            P("seq"),
        ),
        check_vma=False,
    )
```

```python
import functools

import jax
import jax.numpy as jnp
from jax import lax
from jax.experimental import pallas as pl
from jax.experimental.pallas import tpu as pltpu
from jax.sharding import PartitionSpec as P

D = 2048
HEADS = 32
KV_HEADS = 8
HEAD = 64
WINDOW = 64
KVD = KV_HEADS * HEAD
GROUPS = HEADS // KV_HEADS
QKV = D + 2 * KVD
WIDE = GROUPS * HEAD
FEAT = 2 * HEAD
LOW = 128
STATE = 80
HALVES = 2
VMEM_LIMIT = 58 << 20
HALF = D // HALVES
PER_HALF = KV_HEADS // HALVES
SCALE = HEAD ** (-0.5)

EPSILON = 1e-05
THETA = 500000.0

Z_SIZE = 4
NEAR_BIT = 2
FAR_BIT = 1
CORES = 2
F32 = jnp.float32
BF16 = jnp.bfloat16


def dot_nn(a, b):
    return jnp.dot(a, b, preferred_element_type=F32)


def dot_nt(a, b):
    return lax.dot_general(a, b, (((1,), (1,)), ((), ())), preferred_element_type=F32)


def dot_tn(a, b):
    return lax.dot_general(a, b, (((0,), (0,)), ((), ())), preferred_element_type=F32)


def lane(shape):
    return lax.broadcasted_iota(jnp.int32, shape, 1)


def row(shape):
    return lax.broadcasted_iota(jnp.int32, shape, 0)


def low_half(shape):
    return lane(shape) % FEAT < HEAD


def turn(x, cosine, sine):
    width = x.shape[1]
    first = lane(x.shape) % HEAD < HEAD // 2
    swapped = jnp.where(
        first, pltpu.roll(x, width - HEAD // 2, 1), pltpu.roll(x, HEAD // 2, 1)
    )
    return x * cosine + swapped * sine


def halves_softmax(u):
    lo = low_half(u.shape)
    top = jnp.where(
        lo,
        jnp.max(jnp.where(lo, u, -jnp.inf), axis=1, keepdims=True),
        jnp.max(jnp.where(lo, -jnp.inf, u), axis=1, keepdims=True),
    )
    e = jnp.exp(u - top)
    total = jnp.where(
        lo,
        jnp.sum(jnp.where(lo, e, 0.0), axis=1, keepdims=True),
        jnp.sum(jnp.where(lo, 0.0, e), axis=1, keepdims=True),
    )
    return e / total


def halves_softmax_back(f, g):
    lo = low_half(f.shape)
    t = f * g
    total = jnp.where(
        lo,
        jnp.sum(jnp.where(lo, t, 0.0), axis=1, keepdims=True),
        jnp.sum(jnp.where(lo, 0.0, t), axis=1, keepdims=True),
    )
    v = f * (g - total)
    return v - pltpu.roll(v, HEAD, 1), t


def pair_features(x, maps):
    u = dot_nn(x, maps)
    return jnp.concatenate(
        [halves_softmax(u[:, :FEAT]), halves_softmax(u[:, FEAT:])], axis=1
    )


def same_head(size):
    shape = (GROUPS * size, WIDE)
    return (row(shape) // size == lane(shape) // HEAD).astype(F32)


def diagonal(tile, mask):
    wide = jnp.concatenate([tile, tile], axis=1)
    return (jnp.concatenate([wide] * GROUPS, axis=0) * mask).astype(BF16)


def diagonal_pair(tile):
    none = jnp.zeros_like(tile)
    return jnp.concatenate(
        [jnp.concatenate([tile, none], axis=1), jnp.concatenate([none, tile], axis=1)], axis=0
    )


def both_halves(kv):
    kv = kv.astype(F32)
    lo = low_half(kv.shape)
    other = pltpu.roll(kv, HEAD, 1)
    return jnp.where(lo, kv, other), jnp.where(lo, other, kv)


def fold_heads(r, mask):
    r = r * mask
    r = r[:64] + r[64:128] + r[128:192] + r[192:]
    r = r[:, :FEAT] + r[:, FEAT:]
    return r + pltpu.roll(r, HEAD, 1)


def fold_pair(r, size):
    return r[:size, :FEAT] + r[size:, FEAT:]


def whole(a):
    return pl.BlockSpec(a.shape, lambda *_: (0,) * len(a.shape))


ANYWHERE = pl.BlockSpec(memory_space=pl.ANY)
SCALARS = pl.BlockSpec(memory_space=pltpu.SMEM)


class Gathered:
    def __init__(self, blocks, places, size):
        self.blocks, self.places, self.size = blocks, places, size

    def shapes(self):
        return tuple(b.shape[0] // self.size for b in self.blocks)


def start_rows(places, refs, counts, size, target, sem, column=0):
    n = 0
    columns = slice(column, column + target.shape[1])
    for ref, count in zip(refs, counts):
        for i in range(count):
            to = pl.ds(pl.multiple_of(places[n] * size, size), size)
            part = ref.at[i * size : (i + 1) * size, columns]
            pltpu.make_async_copy(part, target.at[to], sem).start()
            n += 1


def wait_rows(target, sem):
    pltpu.make_async_copy(target, target, sem).wait()


def project_kv_kernel(*refs, counts, size):
    n = len(counts)
    places_ref, blocks = refs[0], refs[1 : 1 + n]
    x_ref, low_ref, p_ref, cos_ref, sin_ref, maps_ref, survive_ref = refs[1 + n : 8 + n]
    kv_ref, kf_ref, pack_ref, full_ref, w_ref, sem = refs[8 + n :]
    length = x_ref.shape[0]
    start_rows(places_ref, blocks, counts, size, w_ref, sem, D)
    wait_rows(w_ref, sem)
    survive = survive_ref[...]
    lo = low_half((length, FEAT))
    cut = length - WINDOW
    steps = KVD // WIDE
    part = lambda j: slice(j * WIDE, (j + 1) * WIDE)
    for i in range(steps):
        raw_k, raw_v = (
            dot_nn(x_ref[...], w_ref[:, part(j)]) + dot_nn(low_ref[...], p_ref[:, part(j)])
            for j in (i, steps + i)
        )
        keys = turn(raw_k, cos_ref[...], sin_ref[...]).astype(BF16)
        values = raw_v.astype(BF16).astype(F32)
        for p in range(WIDE // FEAT):
            at = (i * GROUPS + 2 * p) * FEAT
            k2 = keys[:, p * FEAT : (p + 1) * FEAT]
            v2 = values[:, p * FEAT : (p + 1) * FEAT]
            feats = pair_features(k2, maps_ref[2 * i + p])
            kf_ref[:, at : at + 2 * FEAT] = feats.astype(BF16)
            k2 = k2.astype(F32)
            k_other, v_other = pltpu.roll(k2, HEAD, 1), pltpu.roll(v2, HEAD, 1)
            ones = jnp.where(lane((length, FEAT)) < HEAD + 8, 1.0, 0.0)
            for h, kv, v in (
                (0, jnp.where(lo, k2, v_other), v2),
                (1, jnp.where(lo, k_other, v2), v_other),
            ):
                at_h = at + h * FEAT
                kv_ref[:, at_h : at_h + FEAT] = kv.astype(BF16)
                v_one = jnp.where(lo, v, ones).astype(BF16)
                kept = (feats[:, h * FEAT : (h + 1) * FEAT].astype(BF16).astype(F32) * survive)
                kept = kept.astype(BF16)
                head = dot_tn(v_one[:cut], kept[:cut])
                tail = dot_tn(v_one[cut:], kept[cut:])
                at_h = slice(at_h, at_h + FEAT)
                pack_ref[2 * WINDOW :, at_h] = head[:STATE].astype(BF16)
                full_ref[:, at_h] = (head + tail)[:STATE].astype(BF16)
    pack_ref[:WINDOW, :] = kv_ref[cut:, :]
    pack_ref[WINDOW : 2 * WINDOW, :] = kf_ref[cut:, :]


def project_kv(w, x, low, p, cosine, sine, maps, survive):
    length = x.shape[0]
    shapes = (
        jax.ShapeDtypeStruct((length, KV_HEADS * FEAT), BF16),
        jax.ShapeDtypeStruct((length, KV_HEADS * FEAT), BF16),
        jax.ShapeDtypeStruct((2 * WINDOW + STATE, KV_HEADS * FEAT), BF16),
        jax.ShapeDtypeStruct((STATE, KV_HEADS * FEAT), BF16),
    )
    rest = (x, low, p, cosine, sine, maps, survive)
    return pl.pallas_call(
        functools.partial(project_kv_kernel, counts=w.shapes(), size=w.size),
        grid=(1,),
        in_specs=[SCALARS] + [ANYWHERE] * len(w.blocks) + [whole(a) for a in rest],
        out_specs=[whole(v) for v in shapes],
        out_shape=shapes,
        scratch_shapes=[pltpu.VMEM((D, 2 * KVD), BF16), pltpu.SemaphoreType.DMA],
        compiler_params=pltpu.CompilerParams(vmem_limit_bytes=VMEM_LIMIT),
        cost_estimate=pl.CostEstimate(
            flops=4 * length * D * KVD, bytes_accessed=4 * D * KVD, transcendentals=0
        ),
        name="project_kv",
    )(w.places, *w.blocks, *rest)


def project_q_kernel(*refs, counts, size, column):
    n = len(counts)
    places_ref, blocks = refs[0], refs[1 : 1 + n]
    x_ref, low_ref, p_ref, cos_ref, sin_ref, maps_ref, q_ref, qf_ref, w_ref, sem = refs[1 + n :]
    step = pl.program_id(0)

    @pl.when(step == 0)
    def _():
        start_rows(places_ref, blocks, counts, size, w_ref, sem, column)
        wait_rows(w_ref, sem)

    at = pl.ds(pl.multiple_of(step * WIDE, WIDE), WIDE)
    raw = dot_nn(x_ref[...], w_ref[:, at]) + dot_nn(low_ref[...], p_ref[...])
    q = turn(raw, cos_ref[...], sin_ref[...]).astype(BF16)
    q_ref[...] = q
    for p in range(WIDE // FEAT):
        feats = pair_features(q[:, p * FEAT : (p + 1) * FEAT], maps_ref[p])
        qf_ref[:, 2 * p * FEAT : 2 * (p + 1) * FEAT] = feats.astype(BF16)


def project_q(half, w, x, low, p, cosine, sine, maps):
    length = x.shape[0]
    first = half * PER_HALF
    pairs = WIDE // FEAT
    return pl.pallas_call(
        functools.partial(
            project_q_kernel, counts=w.shapes(), size=w.size, column=half * HALF
        ),
        grid=(HALF // WIDE,),
        in_specs=[SCALARS] + [ANYWHERE] * len(w.blocks) + [
            whole(x), whole(low),
            pl.BlockSpec((LOW, WIDE), lambda g: (0, first + g)),
            whole(cosine), whole(sine),
            pl.BlockSpec((pairs, FEAT, 2 * FEAT), lambda g: (first + g, 0, 0)),
        ],
        out_specs=[
            pl.BlockSpec((length, WIDE), lambda g: (0, g)),
            pl.BlockSpec((length, 2 * WIDE), lambda g: (0, g)),
        ],
        out_shape=[
            jax.ShapeDtypeStruct((length, HALF), BF16),
            jax.ShapeDtypeStruct((length, 2 * HALF), BF16),
        ],
        scratch_shapes=[pltpu.VMEM((D, HALF), BF16), pltpu.SemaphoreType.DMA],
        compiler_params=pltpu.CompilerParams(vmem_limit_bytes=VMEM_LIMIT),
        cost_estimate=pl.CostEstimate(
            flops=2 * length * D * HALF, bytes_accessed=2 * D * HALF, transcendentals=0
        ),
        name="project_q",
    )(w.places, *w.blocks, x, low, p, cosine, sine, maps)


def key_tiles(kv_ref, kf_ref, rim_kv_ref, rim_kf_ref, mask):
    tiles = []
    for t in range(1 + kv_ref.shape[0] // WINDOW):
        if t == 0:
            kv, kf = rim_kv_ref[...], rim_kf_ref[...]
        else:
            at = (t - 1) * WINDOW
            kv, kf = kv_ref[at : at + WINDOW, :], kf_ref[at : at + WINDOW, :]
        kk, vv = both_halves(kv)
        tiles.append((diagonal(kk, mask * SCALE), diagonal(vv, mask), diagonal_pair(kf)))
    return tiles


def spans(t, length):
    edge = lambda v: min(max(v, 0), length)
    a, b, c = edge((t - 1) * WINDOW), edge(t * WINDOW), edge((t + 1) * WINDOW)
    return (a, b), (b, c), (c, length)


def weights_of(t, tile, q_ref, qf_ref, same, upper, gamma):
    length = q_ref.shape[0]
    (a, b), (_, c), _ = spans(t, length)
    e = jnp.exp(dot_nt(q_ref[a:c, :], tile[0]))
    linear = None
    if b < length:
        linear = gamma * jnp.concatenate(
            [
                dot_nt(qf_ref[b:, 2 * p * FEAT : 2 * (p + 1) * FEAT], tile[2])
                for p in range(GROUPS // 2)
            ],
            axis=1,
        )
    parts = []
    if b > a:
        parts.append(jnp.where(same(a, b) & upper, e[: b - a], 0.0))
    if c > b:
        mixed = jnp.where(upper, linear[: c - b], e[b - a :])
        parts.append(jnp.where(same(b, c), mixed, 0.0))
    if length > c:
        parts.append(jnp.where(same(c, length), linear[c - b :], 0.0))
    return e, jnp.concatenate(parts, axis=0).astype(BF16)


def carried(carry_ref):
    state = carry_ref[...]
    ones = jnp.zeros((HEAD, FEAT), BF16) + state[HEAD : HEAD + 1, :]
    return diagonal_pair(state[:HEAD, :]), diagonal_pair(ones)


def attend_kernel(
    q_ref, qf_ref, kv_ref, kf_ref, rim_kv_ref, rim_kf_ref, carry_ref,
    qdoc_ref, kdoc_ref, fresh_ref, gamma_ref,
    out_ref, att_ref, inv_ref, num_ref, den_ref,
):
    length = q_ref.shape[0]
    mask = same_head(WINDOW)
    ones = mask.astype(BF16)
    gamma = gamma_ref[...]
    shape = (WINDOW, WIDE)
    upper = row(shape) >= lane(shape) % HEAD
    state, state_sum = carried(carry_ref)
    fresh = fresh_ref[...] * gamma
    for p in range(GROUPS // 2):
        feats = qf_ref[:, 2 * p * FEAT : 2 * (p + 1) * FEAT]
        at = slice(p * FEAT, (p + 1) * FEAT)
        num_ref[:, at] = dot_nt(feats, state) * fresh[:, at]
        den_ref[:, at] = dot_nt(feats, state_sum) * fresh[:, at]
    for t, tile in enumerate(key_tiles(kv_ref, kf_ref, rim_kv_ref, rim_kf_ref, mask)):
        a = spans(t, length)[0][0]
        same = lambda i, j, t=t: qdoc_ref[i:j, :] == kdoc_ref[t : t + 1, :]
        _, w = weights_of(t, tile, q_ref, qf_ref, same, upper, gamma)
        num_ref[a:, :] += dot_nn(w, tile[1])
        den_ref[a:, :] += dot_nn(w, ones)
    inv = 1.0 / den_ref[...]
    att = num_ref[...] * inv
    inv_ref[...] = inv
    att_ref[...] = att
    out_ref[...] = att.astype(BF16)


def group_specs(length, half):
    first = half * PER_HALF
    column = lambda rows, width: pl.BlockSpec((rows, width), lambda g: (0, g))
    shared = lambda rows, width, at: pl.BlockSpec((rows, width), lambda g: (0, at + g))
    fixed = lambda rows, width: pl.BlockSpec((rows, width), lambda g: (0, 0))
    return dict(
        q=column(length, WIDE),
        qf=column(length, 2 * WIDE),
        k=shared(length, FEAT, first),
        rim_kv=shared(WINDOW, FEAT, first),
        rim_kf=pl.BlockSpec((WINDOW, FEAT), lambda g: (1, first + g)),
        state=shared(STATE, FEAT, first),
        back=column(STATE, FEAT),
        qdoc=fixed(length, 1),
        kdoc=fixed(8, WIDE),
        gamma=shared(1, WIDE, first),
        wide=fixed(length, WIDE),
        maps=pl.BlockSpec((GROUPS // 2, FEAT, 2 * FEAT), lambda g: (first + g, 0, 0)),
    )


def attend(half, q, qf, kv, kf, rim, carry, masks):
    length = q.shape[0]
    s = group_specs(length, half)
    return pl.pallas_call(
        attend_kernel,
        grid=(PER_HALF,),
        in_specs=[
            s["q"], s["qf"], s["k"], s["k"], s["rim_kv"], s["rim_kf"], s["state"],
            s["qdoc"], s["kdoc"], s["qdoc"], s["gamma"],
        ],
        out_specs=[s["q"]] * 3,
        out_shape=[
            jax.ShapeDtypeStruct((length, HALF), BF16),
            jax.ShapeDtypeStruct((length, HALF), F32),
            jax.ShapeDtypeStruct((length, HALF), F32),
        ],
        scratch_shapes=[pltpu.VMEM((length, WIDE), F32)] * 2,
        compiler_params=pltpu.CompilerParams(vmem_limit_bytes=VMEM_LIMIT),
        cost_estimate=pl.CostEstimate(
            flops=5_000_000_000, bytes_accessed=8 * length * D, transcendentals=0
        ),
        name="attend",
    )(q, qf, kv, kf, rim, rim, carry, masks["qdoc"], masks["kdoc"], masks["fresh"], masks["gamma"])


def scaled_grads_kernel(
    ga_ref, att_ref, inv_ref, qf_ref, fresh_ref, gamma_ref, g_ref, gd_ref, back_ref
):
    mask = same_head(HEAD)
    ga = ga_ref[...].astype(F32)
    inv = inv_ref[...]
    product = ga * att_ref[...]
    high = product.astype(BF16)
    rest = (product - high.astype(F32)).astype(BF16)
    ones = mask.astype(BF16)
    gd = -(dot_nn(high, ones) + dot_nn(rest, ones)) * inv
    g = ga * inv
    g_ref[...] = g.astype(BF16)
    gd_ref[...] = gd
    fresh = fresh_ref[...] * gamma_ref[...]
    fresh_g = (g * fresh).astype(BF16)
    fresh_gd = (gd * fresh).astype(BF16)
    kv = sums = 0.0
    for p in range(GROUPS // 2):
        feats = qf_ref[:, 2 * p * FEAT : 2 * (p + 1) * FEAT]
        at = slice(p * FEAT, (p + 1) * FEAT)
        kv += fold_pair(dot_tn(fresh_g[:, at], feats), HEAD)
        sums += fold_pair(dot_tn(fresh_gd[:, at], feats), HEAD)
    back_ref[:HEAD, :] = kv.astype(BF16)
    back_ref[HEAD:, :] = sums[: STATE - HEAD].astype(BF16)


def scaled_grads(half, ga, att, inv, qf, masks):
    length = ga.shape[0]
    s = group_specs(length, half)
    return pl.pallas_call(
        scaled_grads_kernel,
        grid=(PER_HALF,),
        in_specs=[s["q"], s["q"], s["q"], s["qf"], s["qdoc"], s["gamma"]],
        out_specs=[s["q"], s["q"], s["back"]],
        out_shape=[
            jax.ShapeDtypeStruct((length, HALF), BF16),
            jax.ShapeDtypeStruct((length, HALF), F32),
            jax.ShapeDtypeStruct((STATE, PER_HALF * FEAT), BF16),
        ],
        compiler_params=pltpu.CompilerParams(vmem_limit_bytes=VMEM_LIMIT),
        name="scaled_grads",
    )(ga, att, inv, qf, masks["fresh"], masks["gamma"])


def attend_back_kernel(
    q_ref, qf_ref, kv_ref, kf_ref, rim_kv_ref, rim_kf_ref, carry_ref, g_ref, gd_ref,
    qdoc_ref, kdoc_ref, fresh_ref, gamma_ref, maps_ref, cos_ref, sin_ref,
    raw_ref, dkv_ref, dkf_ref, rim_ref, dmap_ref, logit_ref, dq_ref, dqf_ref,
):
    length = q_ref.shape[0]
    mask = same_head(WINDOW)
    gamma = gamma_ref[...]
    shape = (WINDOW, WIDE)
    upper = row(shape) >= lane(shape) % HEAD
    state, state_sum = carried(carry_ref)
    fresh = fresh_ref[...] * gamma
    pairs = range(GROUPS // 2)
    half = lambda p: slice(p * FEAT, (p + 1) * FEAT)
    full = lambda p: slice(2 * p * FEAT, 2 * (p + 1) * FEAT)
    fresh_g = (g_ref[...].astype(F32) * fresh).astype(BF16)
    fresh_gd = (gd_ref[...] * fresh * (1.0 / HEAD)).astype(BF16)
    for p in pairs:
        dqf_ref[:, full(p)] = dot_nn(fresh_g[:, half(p)], state) + dot_nn(
            fresh_gd[:, half(p)], state_sum
        )
    dq_ref[...] = jnp.zeros_like(dq_ref)
    lo = low_half((WINDOW, FEAT))
    for t, tile in enumerate(key_tiles(kv_ref, kf_ref, rim_kv_ref, rim_kf_ref, mask)):
        (a, b), (_, c), _ = spans(t, length)
        same = lambda i, j, t=t: qdoc_ref[i:j, :] == kdoc_ref[t : t + 1, :]
        e, w = weights_of(t, tile, q_ref, qf_ref, same, upper, gamma)
        g = g_ref[a:, :]
        x = dot_nt(g, tile[1]) + gd_ref[a:, :]
        near = x[: c - a] * e
        parts = []
        if b > a:
            parts.append(jnp.where(same(a, b) & upper, near[: b - a], 0.0))
        if c > b:
            parts.append(jnp.where(same(b, c), jnp.where(upper, 0.0, near[b - a :]), 0.0))
        ds = jnp.concatenate(parts, axis=0).astype(BF16)
        dq_ref[a:c, :] += dot_nn(ds, tile[0])
        dk = fold_heads(dot_tn(ds, q_ref[a:c, :]), mask) * SCALE
        dv = fold_heads(dot_tn(w, g), mask)
        at = slice((t - 1) * WINDOW, t * WINDOW)
        dkv = jnp.where(lo, dk, dv)
        if t:
            dkv_ref[at, :] = dkv
        else:
            rim_ref[:WINDOW, :] = dkv.astype(BF16)
        if b < length:
            far = x[b - a :] * gamma
            parts = [jnp.where(same(b, c) & upper, far[: c - b], 0.0)]
            if c < length:
                parts.append(jnp.where(same(c, length), far[c - b :], 0.0))
            dl = jnp.concatenate(parts, axis=0).astype(BF16)
            dkf = 0.0
            for p in pairs:
                dqf_ref[b:, full(p)] += dot_nn(dl[:, half(p)], tile[2])
                dkf += fold_pair(dot_tn(dl[:, half(p)], qf_ref[b:, full(p)]), HEAD)
            if t:
                dkf_ref[at, :] = dkf
            else:
                rim_ref[WINDOW:, :] = dkf.astype(BF16)
        else:
            dkf_ref[at, :] = jnp.zeros((WINDOW, FEAT), F32)
    for p in pairs:
        grads = []
        for h in (2 * p, 2 * p + 1):
            f = qf_ref[:, h * FEAT : (h + 1) * FEAT].astype(F32)
            gu, t = halves_softmax_back(f, dqf_ref[:, h * FEAT : (h + 1) * FEAT])
            grads.append(gu.astype(BF16))
            total = jnp.sum(jnp.sum(t, axis=0, keepdims=True), axis=1, keepdims=True)
            logit_ref[0, h : h + 1, :] = jnp.zeros((1, FEAT), F32) + total
        gu = jnp.concatenate(grads, axis=1)
        dq_ref[:, half(p)] += 0.5 * dot_nt(gu, maps_ref[p])
        dmap = dot_tn(q_ref[:, half(p)], gu)
        dmap_ref[2 * p] = dmap[:HEAD, :FEAT]
        dmap_ref[2 * p + 1] = dmap[HEAD:, FEAT:]
    raw_ref[...] = turn(dq_ref[...], cos_ref[...], -sin_ref[...]).astype(BF16)


def attend_back(half, q, qf, kv, kf, rim, carry, g, gd, masks, maps):
    length = q.shape[0]
    s = group_specs(length, half)
    column = lambda rows: pl.BlockSpec((rows, FEAT), lambda g: (0, g))
    return pl.pallas_call(
        attend_back_kernel,
        grid=(PER_HALF,),
        in_specs=[
            s["q"], s["qf"], s["k"], s["k"], s["rim_kv"], s["rim_kf"], s["state"], s["q"], s["q"],
            s["qdoc"], s["kdoc"], s["qdoc"], s["gamma"], s["maps"], s["wide"], s["wide"],
        ],
        out_specs=[
            s["q"], column(length), column(length), column(2 * WINDOW),
            pl.BlockSpec((GROUPS, HEAD, FEAT), lambda g: (g, 0, 0)),
            pl.BlockSpec((1, 8, FEAT), lambda g: (g, 0, 0)),
        ],
        out_shape=[
            jax.ShapeDtypeStruct((length, HALF), BF16),
            jax.ShapeDtypeStruct((length, PER_HALF * FEAT), F32),
            jax.ShapeDtypeStruct((length, PER_HALF * FEAT), F32),
            jax.ShapeDtypeStruct((2 * WINDOW, PER_HALF * FEAT), BF16),
            jax.ShapeDtypeStruct((HEADS // HALVES, HEAD, FEAT), F32),
            jax.ShapeDtypeStruct((PER_HALF, 8, FEAT), F32),
        ],
        scratch_shapes=[pltpu.VMEM((length, WIDE), F32), pltpu.VMEM((length, 2 * WIDE), F32)],
        compiler_params=pltpu.CompilerParams(vmem_limit_bytes=VMEM_LIMIT),
        cost_estimate=pl.CostEstimate(
            flops=15_000_000_000, bytes_accessed=8 * length * D, transcendentals=0
        ),
        name="attend_back",
    )(
        q, qf, kv, kf, rim, rim, carry, g, gd,
        masks["qdoc"], masks["kdoc"], masks["fresh"], masks["gamma"],
        maps, masks["cos"], masks["sin"],
    )


def keys_back_kernel(
    kv_ref, kf_ref, dkv_ref, dkf_ref, rim_kv_ref, rim_kf_ref, near_ref, far_ref, survive_ref,
    maps_ref, cos_ref, sin_ref, rk_ref, rv_ref, dmap_ref,
):
    length = kv_ref.shape[0]
    cut = length - WINDOW
    lo = low_half((length, FEAT))
    survive = survive_ref[...]
    dkv, grads = [], []
    for h in range(2):
        at = slice(h * FEAT, (h + 1) * FEAT)
        kv = kv_ref[:, at].astype(F32)
        kf = kf_ref[:, at]
        v_low = pltpu.roll(kv, HEAD, 1)
        ones = jnp.where(lane((length, FEAT)) == HEAD, 1.0, 0.0)
        v_one = jnp.where(lo, v_low, ones).astype(BF16)[:, :STATE]
        dkf, dv = [], []
        for back, part in ((near_ref, slice(0, cut)), (far_ref, slice(cut, length))):
            state = back[:, at]
            twice = jnp.concatenate([state[:HEAD], state[:HEAD]], axis=0)
            dkf.append(dot_nn(v_one[part], state))
            dv.append(dot_nt(kf[part], twice))
        rim = jnp.zeros((cut, FEAT), F32)
        dkf = (
            jnp.concatenate(dkf, axis=0) * survive
            + dkf_ref[:, at]
            + jnp.concatenate([rim, rim_kf_ref[:, at].astype(F32)], axis=0)
        )
        dv = jnp.concatenate(dv, axis=0) * survive
        total = (
            dkv_ref[:, at]
            + jnp.concatenate([rim, rim_kv_ref[:, at].astype(F32)], axis=0)
            + jnp.where(lo, 0.0, dv)
        )
        gu, _ = halves_softmax_back(kf.astype(F32), dkf)
        grads.append(gu.astype(BF16))
        dkv.append(total)
    gu = jnp.concatenate(grads, axis=1)
    keys = jnp.where(lo, kv_ref[:, :FEAT].astype(F32), pltpu.roll(kv_ref[:, FEAT:].astype(F32), HEAD, 1))
    dmap = dot_tn(keys.astype(BF16), gu)
    dmap_ref[0] = dmap[:HEAD, :FEAT]
    dmap_ref[1] = dmap[HEAD:, FEAT:]
    dk = jnp.where(lo, dkv[0], pltpu.roll(dkv[1], HEAD, 1)) + 0.5 * dot_nt(gu, maps_ref[0])
    rk_ref[...] = turn(dk, cos_ref[...], -sin_ref[...]).astype(BF16)
    rv_ref[...] = jnp.where(lo, pltpu.roll(dkv[0], HEAD, 1), dkv[1]).astype(BF16)


def keys_back(half, kv, kf, dkv, dkf, rim, near, far, masks, maps):
    length = kv.shape[0]
    pairs = PER_HALF // 2
    first = half * pairs
    column = lambda rows: pl.BlockSpec((rows, 2 * FEAT), lambda g: (0, g))
    shared = pl.BlockSpec((length, 2 * FEAT), lambda g: (0, first + g))
    state = pl.BlockSpec((STATE, 2 * FEAT), lambda g: (0, first + g))
    narrow = pl.BlockSpec((length, FEAT), lambda g: (0, 0))
    out = pl.BlockSpec((length, FEAT), lambda g: (0, g))
    return pl.pallas_call(
        keys_back_kernel,
        grid=(pairs,),
        in_specs=[
            shared, shared, column(length), column(length),
            column(WINDOW), pl.BlockSpec((WINDOW, 2 * FEAT), lambda g: (1, g)),
            state, state, pl.BlockSpec((length, 1), lambda g: (0, 0)),
            pl.BlockSpec((1, FEAT, 2 * FEAT), lambda g: (first + g, 0, 0)), narrow, narrow,
        ],
        out_specs=[out, out, pl.BlockSpec((2, HEAD, FEAT), lambda g: (g, 0, 0))],
        out_shape=[
            jax.ShapeDtypeStruct((length, KVD // HALVES), BF16),
            jax.ShapeDtypeStruct((length, KVD // HALVES), BF16),
            jax.ShapeDtypeStruct((PER_HALF, HEAD, FEAT), F32),
        ],
        compiler_params=pltpu.CompilerParams(vmem_limit_bytes=VMEM_LIMIT),
        name="keys_back",
    )(
        kv, kf, dkv, dkf, rim, rim, near, far, masks["survive"], maps, masks["cos"], masks["sin"]
    )


def out_project_kernel(*refs, counts, size):
    n = len(counts)
    places, blocks, refs = refs[0], refs[1 : 1 + n], refs[1 + n :]
    m0, m1, hidden, proj_in, proj_out, gain = refs[:6]
    residual, second, low, inverse, w, sem = refs[6:]
    start_rows(places, blocks, counts, size, w, sem)
    reduced = dot_nn(m0[...], proj_in[:HALF, :]) + dot_nn(m1[...], proj_in[HALF:, :])
    reduced = reduced.astype(BF16)
    low[...] = reduced
    wait_rows(w, sem)
    squares = 0.0
    for j in range(D // WIDE):
        at = slice(j * WIDE, (j + 1) * WIDE)
        sums = (
            hidden[:, at].astype(F32)
            + dot_nn(m0[...], w[:HALF, at])
            + dot_nn(m1[...], w[HALF:, at])
            + dot_nn(reduced, proj_out[:, at])
        )
        residual[:, at] = sums
        squares = squares + jnp.sum(sums * sums, axis=1, keepdims=True)
    inv = lax.rsqrt(squares * (1.0 / D) + EPSILON)
    inverse[...] = jnp.zeros(inverse.shape, F32) + inv
    second[...] = (residual[...] * inv * gain[...]).astype(BF16)


def out_project(w, merged, hidden, proj_in, proj_out, gain):
    length = hidden.shape[0]
    shapes = (
        jax.ShapeDtypeStruct((length, D), F32),
        jax.ShapeDtypeStruct((length, D), BF16),
        jax.ShapeDtypeStruct((length, LOW), BF16),
        jax.ShapeDtypeStruct((length, LOW), F32),
    )
    rest = (*merged, hidden, proj_in, proj_out, gain)
    return pl.pallas_call(
        functools.partial(out_project_kernel, counts=w.shapes(), size=w.size),
        grid=(1,),
        in_specs=[SCALARS] + [ANYWHERE] * len(w.blocks) + [whole(a) for a in rest],
        out_specs=[whole(v) for v in shapes],
        out_shape=shapes,
        scratch_shapes=[pltpu.VMEM((D, D), BF16), pltpu.SemaphoreType.DMA],
        compiler_params=pltpu.CompilerParams(vmem_limit_bytes=VMEM_LIMIT),
        cost_estimate=pl.CostEstimate(
            flops=2 * length * D * D, bytes_accessed=2 * D * D, transcendentals=0
        ),
        name="out_project",
    )(w.places, *w.blocks, *rest)


def branch_back_kernel(*refs, counts, size, extra):
    n = len(counts)
    places, blocks, refs = refs[0], refs[1 : 1 + n], refs[1 + n :]
    sums, refs = refs[:extra], refs[extra:]
    cot, residual, inverse, gain, proj_in, proj_out, m0, m1, low = refs[:9]
    grad_residual, g0, g1, grad_gain, grad_in, grad_out, w, sem = refs[9:]
    start_rows(places, blocks, counts, size, w, sem)
    total = sums[0][...].astype(F32)
    for v in sums[1:]:
        total = total + v[...].astype(F32)
    inv = inverse[:, :1]
    normed = residual[...] * inv
    product = total * normed
    grad_gain[...] = jnp.sum(product, axis=0, keepdims=True)
    scaled = total * gain[...]
    mean = jnp.sum(scaled * normed, axis=1, keepdims=True) * (1.0 / D)
    grad = cot[...].astype(F32) + inv * (scaled - normed * mean)
    grad_residual[...] = grad
    branch = grad.astype(BF16)
    grad_low = dot_nt(branch, proj_out[...]).astype(BF16)
    grad_out[...] = dot_tn(low[...], branch)
    for i, m in enumerate((m0, m1)):
        grad_in[:, i * HALF : (i + 1) * HALF] = dot_tn(grad_low, m[...])
    wait_rows(w, sem)
    for j in range(D // WIDE):
        at = slice(j * WIDE, (j + 1) * WIDE)
        i, col = j // (HALF // WIDE), (j % (HALF // WIDE)) * WIDE
        back = dot_nt(grad_low, proj_in[at, :]) + dot_nt(branch, w[at, :])
        (g0, g1)[i][:, col : col + WIDE] = back.astype(BF16)


def branch_back(w, sums, cot, residual, inverse, gain, proj_in, proj_out, merged, low):
    length = cot.shape[0]
    shapes = (
        jax.ShapeDtypeStruct((length, D), F32),
        jax.ShapeDtypeStruct((length, HALF), BF16),
        jax.ShapeDtypeStruct((length, HALF), BF16),
        jax.ShapeDtypeStruct((1, D), F32),
        jax.ShapeDtypeStruct((LOW, D), F32),
        jax.ShapeDtypeStruct((LOW, D), F32),
    )
    rest = (*sums, cot, residual, inverse, gain, proj_in, proj_out, *merged, low)
    return pl.pallas_call(
        functools.partial(
            branch_back_kernel, counts=w.shapes(), size=w.size, extra=len(sums)
        ),
        grid=(1,),
        in_specs=[SCALARS] + [ANYWHERE] * len(w.blocks) + [whole(a) for a in rest],
        out_specs=[whole(v) for v in shapes],
        out_shape=shapes,
        scratch_shapes=[pltpu.VMEM((D, D), BF16), pltpu.SemaphoreType.DMA],
        compiler_params=pltpu.CompilerParams(vmem_limit_bytes=VMEM_LIMIT),
        cost_estimate=pl.CostEstimate(
            flops=2 * length * D * D, bytes_accessed=2 * D * D, transcendentals=0
        ),
        name="branch_back",
    )(w.places, *w.blocks, *rest)


def inputs_back_kernel(*refs, counts, size):
    n = len(counts)
    places, blocks, refs = refs[0], refs[1 : 1 + n], refs[1 + n :]
    raws, refs = refs[:6], refs[6:]
    p_in, p_out, low, x, hidden, gain, grad_residual = refs[:7]
    grad_tokens, grad_gain, grad_in, grad_out, w, raw, back, sem = refs[7:]
    start_rows(places, blocks, counts, size, w, sem)
    at = 0
    for r in raws:
        raw[:, at : at + r.shape[1]] = r[...]
        at += r.shape[1]
    grad_low = dot_nt(raw[...], p_out[...]).astype(BF16)
    grad_out[...] = dot_tn(low[...], raw[...])
    grad_in[...] = dot_tn(grad_low, x[...])
    wait_rows(w, sem)
    values = hidden[...].astype(F32)
    inv = lax.rsqrt(jnp.sum(values * values, axis=1, keepdims=True) * (1.0 / D) + EPSILON)
    mean = 0.0
    for j in range(D // WIDE):
        at = slice(j * WIDE, (j + 1) * WIDE)
        part = dot_nt(grad_low, p_in[at, :]) + dot_nt(raw[...], w[at, :])
        normed = hidden[:, at].astype(F32) * inv
        product = part * normed
        grad_gain[:, at] = jnp.sum(product, axis=0, keepdims=True)
        mean = mean + jnp.sum(product * gain[:, at], axis=1, keepdims=True)
        back[:, at] = part
    mean = mean * (1.0 / D)
    grad_tokens[...] = grad_residual[...] + inv * (
        back[...] * gain[...] - values * inv * mean
    )


def inputs_back(w, raws, p_in, p_out, low, x, hidden, gain, grad_residual):
    length = x.shape[0]
    shapes = (
        jax.ShapeDtypeStruct((length, D), F32),
        jax.ShapeDtypeStruct((1, D), F32),
        jax.ShapeDtypeStruct((LOW, D), F32),
        jax.ShapeDtypeStruct((LOW, QKV), F32),
    )
    rest = (*raws, p_in, p_out, low, x, hidden, gain, grad_residual)
    return pl.pallas_call(
        functools.partial(inputs_back_kernel, counts=w.shapes(), size=w.size),
        grid=(1,),
        in_specs=[SCALARS] + [ANYWHERE] * len(w.blocks) + [whole(a) for a in rest],
        out_specs=[whole(v) for v in shapes],
        out_shape=shapes,
        scratch_shapes=[
            pltpu.VMEM((D, QKV), BF16),
            pltpu.VMEM((length, QKV), BF16),
            pltpu.VMEM((length, D), F32),
            pltpu.SemaphoreType.DMA,
        ],
        compiler_params=pltpu.CompilerParams(vmem_limit_bytes=VMEM_LIMIT),
        cost_estimate=pl.CostEstimate(
            flops=2 * length * D * QKV, bytes_accessed=2 * D * QKV, transcendentals=0
        ),
        name="inputs_back",
    )(w.places, *w.blocks, *rest)


def mlp_kernel(place_ref, *refs, rows, paired, tile, own, carried_in):
    n = len(rows[0]) + len(rows[1])
    tokens, refs = refs[:n], refs[n:]
    own_gu, own_dn = refs[:2]
    pair, refs = (refs[2], refs[3:]) if paired else (None, refs[2:])
    sums, refs = (refs[:2], refs[2:]) if carried_in else (None, refs)
    out_ref, back_ref, h, c, gu, dn, out, back, row_sem, gu_sem, dn_sem = refs
    step, steps = pl.program_id(0), pl.num_programs(0)
    own_tiles = own_gu.shape[2] // tile if own else 0

    def fetch(n, slot):
        @pl.when(n < own_tiles)
        def _():
            at = pl.ds(pl.multiple_of(n * tile, tile), tile)
            pltpu.make_async_copy(own_gu.at[:, :, at], gu.at[slot], gu_sem.at[slot]).start()
            pltpu.make_async_copy(own_dn.at[at, :], dn.at[slot], dn_sem.at[slot]).start()

        if not paired:
            return

        @pl.when(n >= own_tiles)
        def _():
            first = (n - own_tiles) * tile
            at = pl.ds(pl.multiple_of(first, tile), tile)
            width = pair.shape[1] // 3
            row = pl.ds(pl.multiple_of(2 * width + first % width, tile), tile)
            column = pl.ds(pl.multiple_of(first // width * width, width), width)
            for k in range(D // width):
                part = pair.at[2 * k + place_ref[0]]
                there = slice(k * width, (k + 1) * width)
                for i in range(2):
                    pltpu.make_async_copy(
                        part.at[i * width : (i + 1) * width, at],
                        gu.at[slot, i, there, :],
                        gu_sem.at[slot],
                    ).start()
                pltpu.make_async_copy(
                    part.at[row, column], dn.at[slot, :, there], dn_sem.at[slot]
                ).start()

    @pl.when(step == 0)
    def _():
        fetch(step, 0)
        copies = []
        for target, sizes in zip((h, c), rows):
            at = 0
            for size in sizes:
                i = len(copies)
                there = target.at[at : at + size]
                copies.append(pltpu.make_async_copy(tokens[i], there, row_sem.at[i]))
                at += size
        for copy in copies:
            copy.start()
        if carried_in:
            for i, target in enumerate((out, back)):
                copies.append(pltpu.make_async_copy(sums[i], target, row_sem.at[len(copies)]))
                copies[-1].start()
        else:
            out[...] = jnp.zeros_like(out)
            back[...] = jnp.zeros_like(back)
        for copy in copies:
            copy.wait()

    slot = step % 2

    @pl.when(step + 1 < steps)
    def _():
        fetch(step + 1, 1 - slot)

    pltpu.make_async_copy(own_gu.at[:, :, pl.ds(0, tile)], gu.at[slot], gu_sem.at[slot]).wait()
    pltpu.make_async_copy(own_dn.at[pl.ds(0, tile), :], dn.at[slot], dn_sem.at[slot]).wait()
    w_gate, w_up, w_down = gu.at[slot, 0], gu.at[slot, 1], dn.at[slot]
    gate = dot_nn(h[...], w_gate[...])
    up = dot_nn(h[...], w_up[...])
    grad = dot_nt(c[...], w_down[...])
    sig = jax.nn.sigmoid(gate)
    silu = gate * sig
    act = (silu * up).astype(BF16)
    grad_gate = (grad * up * sig * (1.0 + gate * (1.0 - sig))).astype(BF16)
    grad_up = (grad * silu).astype(BF16)
    out[...] += dot_nn(act, w_down[...])
    back[...] += dot_nt(grad_gate, w_gate[...]) + dot_nt(grad_up, w_up[...])

    @pl.when(step == steps - 1)
    def _():
        out_ref[...] = out[...].astype(out_ref.dtype)
        back_ref[...] = back[...].astype(back_ref.dtype)


def mlp(second, cot, own_gu, own_dn, pair=None, place=None, own=True, sums=()):
    rows = tuple(v.shape[0] for v in second), tuple(v.shape[0] for v in cot)
    total = sum(rows[0])
    hidden = own_gu.shape[2]
    tile = min(256, hidden)
    shards = own + (pair is not None)
    kind = F32 if pair is None else BF16
    if pair is None:
        place = jnp.zeros((1,), jnp.int32)
    block = pl.BlockSpec((total, D), lambda i, p: (0, 0))
    arrays = (*second, *cot, own_gu, own_dn, *(() if pair is None else (pair,)), *sums)
    return pl.pallas_call(
        functools.partial(
            mlp_kernel,
            rows=rows,
            paired=pair is not None,
            tile=tile,
            own=own,
            carried_in=bool(sums),
        ),
        grid_spec=pltpu.PrefetchScalarGridSpec(
            num_scalar_prefetch=1,
            grid=(shards * hidden // tile,),
            in_specs=[ANYWHERE] * len(arrays),
            out_specs=[block, block],
            scratch_shapes=[
                pltpu.VMEM((total, D), BF16),
                pltpu.VMEM((total, D), BF16),
                pltpu.VMEM((2, 2, D, tile), BF16),
                pltpu.VMEM((2, tile, D), BF16),
                pltpu.VMEM((total, D), F32),
                pltpu.VMEM((total, D), F32),
                pltpu.SemaphoreType.DMA((len(second) + len(cot) + len(sums),)),
                pltpu.SemaphoreType.DMA((2,)),
                pltpu.SemaphoreType.DMA((2,)),
            ],
        ),
        out_shape=[jax.ShapeDtypeStruct((total, D), kind)] * 2,
        compiler_params=pltpu.CompilerParams(vmem_limit_bytes=VMEM_LIMIT),
        cost_estimate=pl.CostEstimate(
            flops=12 * total * D * hidden * shards,
            bytes_accessed=6 * D * hidden * shards,
            transcendentals=0,
        ),
        name="mlp",
    )(place, *arrays)


class Grid:
    def __init__(self):
        self.seq = lax.axis_size("seq")
        self.rows = lax.axis_size("rows")
        self.zs = Z_SIZE
        self.xs = self.rows // Z_SIZE
        self.ys = self.seq // CORES
        s = lax.axis_index("seq")
        r = lax.axis_index("rows")
        self.y, self.c = s // CORES, s % CORES
        self.z, self.x = r // self.xs, r % self.xs
        self.s, self.r = s, r

    def send(self, value, move):
        route = []
        for s in range(self.seq):
            for r in range(self.rows):
                there = move(s // CORES, s % CORES, r // self.xs, r % self.xs)
                if there is not None:
                    y, c, z, x = there
                    target = (y * CORES + c) * self.rows + z * self.xs + x
                    route.append((s * self.rows + r, target))
        return jax.tree.map(lambda v: lax.ppermute(v, ("seq", "rows"), route), value)

    def along_z(self, value, k):
        return self.send(value, lambda y, c, z, x: (y, c, (z + k) % self.zs, x))

    def along_x(self, value, k):
        return self.send(value, lambda y, c, z, x: (y, c, z, (x + k) % self.xs))

    def along_y(self, value, k):
        return self.send(value, lambda y, c, z, x: ((y + k) % self.ys, c, z, x))

    def flip_z(self, value, bit):
        return self.send(value, lambda y, c, z, x: (y, c, z ^ bit, x))

    def flip_core(self, value):
        return self.send(value, lambda y, c, z, x: (y, 1 - c, z, x))

    def flip_x(self, value, bit):
        return self.send(value, lambda y, c, z, x: (y, c, z, x ^ bit))

    def flip_seq(self, value, bit):
        def move(y, c, z, x):
            s = (y * CORES + c) ^ bit
            return (s // CORES, s % CORES, z, x)

        return self.send(value, move)

    def along_seq(self, value, k):
        def move(y, c, z, x):
            s = y * CORES + c + k
            return (s // CORES, s % CORES, z, x) if 0 <= s < self.seq else None

        return self.send(value, move)


def after(values, *events):
    return lax.optimization_barrier((values, *events))[0]


class Gather:
    def __init__(self, grid, shard):
        self.grid = grid
        self.size = shard.shape[0] // grid.seq
        self.own = lax.dynamic_slice_in_dim(shard, grid.s * self.size, self.size, 0)

    def over_z(self):
        grid = self.grid
        pieces = [self.own] + [grid.along_z(self.own, k) for k in range(1, grid.zs)]
        half = grid.zs // 2
        self.halves = [jnp.concatenate(pieces[:half]), jnp.concatenate(pieces[half:])]

    def first(self):
        grid = self.grid
        a, b = self.halves
        self.moved = [
            [grid.along_x(a, k) for k in range(1, grid.xs)],
            [grid.along_y(b, k) for k in range(1, grid.ys)],
        ]

    def second(self):
        grid = self.grid
        a, b = (jnp.concatenate([h, *m]) for h, m in zip(self.halves, self.moved))
        self.blocks = [a, b]
        self.last = [grid.along_y(a, k) for k in range(1, grid.ys)]
        self.last += [grid.along_x(b, k) for k in range(1, grid.xs)]

    def cores(self):
        self.over = [self.grid.flip_core(b) for b in self.blocks]

    def result(self):
        grid = self.grid
        blocks = self.blocks + self.last
        blocks = blocks + self.over + [grid.flip_core(b) for b in self.last]
        places = []
        kzs = range(grid.zs // 2), range(grid.zs // 2, grid.zs)
        a = [(kx, 0, kz) for kx in range(grid.xs) for kz in kzs[0]]
        b = [(0, ky, kz) for ky in range(grid.ys) for kz in kzs[1]]
        moves = a + b
        for k in range(1, grid.ys):
            moves = moves + [(kx, k, kz) for kx, _, kz in a]
        for k in range(1, grid.xs):
            moves = moves + [(k, ky, kz) for _, ky, kz in b]
        for core in range(CORES):
            c = (grid.c + core) % CORES
            for kx, ky, kz in moves:
                z, x, y = (grid.z - kz) % grid.zs, (grid.x - kx) % grid.xs, (grid.y - ky) % grid.ys
                places.append((z * grid.xs + x) * grid.seq + y * CORES + c)
        return Gathered(blocks, jnp.stack(places).astype(jnp.int32), self.size)


def pair_part(grid, gate_up, down):
    part = D // grid.seq
    hidden = down.shape[0]
    size = (1, part, hidden)
    gu = [lax.dynamic_slice(gate_up, (i, grid.s * part, 0), size)[0] for i in range(2)]
    dn = lax.dynamic_slice_in_dim(down, grid.s * part, part, 1)
    dn = jnp.concatenate([dn[i : i + part] for i in range(0, hidden, part)], axis=1)
    return jnp.concatenate([*gu, dn], axis=0)


def gather_pair(grid, part):
    groups = []
    for z in range(0, grid.zs, 2):
        for x in range(grid.xs):
            rows = [(z + i) * grid.xs + x for i in range(2)]
            groups.append([s * grid.rows + r for s in range(grid.seq) for r in rows])
    parts = lax.all_gather(part, ("seq", "rows"), axis_index_groups=groups)
    return parts, (1 - grid.z % 2).reshape(1).astype(jnp.int32)


def spread_near(grid, block):
    return [block] + [grid.along_x(block, k) for k in range(1, grid.xs)]


def spread_far(grid, block, parts):
    size = block.shape[0] // parts
    return [grid.flip_z(block[p * size : (p + 1) * size], NEAR_BIT) for p in range(parts)]


def relay(grid, pieces):
    moved = [grid.along_x(piece, k) for k in range(1, grid.xs) for piece in pieces]
    return list(pieces) + moved


def collect_near(grid, near, length):
    blocks = [near[k * length : (k + 1) * length] for k in range(grid.xs)]
    return [blocks[0]] + [grid.along_x(blocks[k], -k) for k in range(1, grid.xs)]


def collect_far(grid, far, length, parts):
    size = length // parts
    send, total = [], None
    for p in range(parts):
        lo = p * size
        far = after(far, total)
        total = far[lo : lo + size]
        for k in range(1, grid.xs):
            other = grid.along_x(far[k * length + lo : k * length + lo + size], -k)
            total = (total.astype(F32) + other.astype(F32)).astype(BF16)
        send.append(total)
    return send


def total_over_all(grid, values):
    widths = [v.shape[2] for v in values]
    packed = jnp.concatenate([v.astype(BF16) for v in values], axis=2)
    packed = jnp.pad(packed, ((0, 0), (0, 0), (0, -packed.shape[2] % FEAT)))
    chunk = lambda i: lax.dynamic_index_in_dim(packed, i, 0, False)
    total = chunk(grid.s).astype(F32)
    for k in range(1, grid.seq):
        total = total + grid.flip_seq(chunk(grid.s ^ k), k).astype(F32)
    for flip, count in ((grid.flip_z, grid.zs), (grid.flip_x, grid.xs)):
        mine = total.astype(BF16)
        terms = [mine.astype(F32)] + [flip(mine, k).astype(F32) for k in range(1, count)]
        while len(terms) > 1:
            terms = [a + b for a, b in zip(terms[::2], terms[1::2])]
        total = terms[0]
    out, at = [], 0
    for w in widths:
        out.append(total[:, at : at + w])
        at += w
    return out


def pair_maps(maps):
    both = jnp.concatenate([maps, -maps], axis=-1)
    both = both.reshape(-1, 2, HEAD, FEAT)
    none = jnp.zeros_like(both[:, 0])
    return jnp.concatenate(
        [
            jnp.concatenate([both[:, 0], none], axis=-1),
            jnp.concatenate([none, both[:, 1]], axis=-1),
        ],
        axis=1,
    )


def adapters(query, key, value, axis):
    if axis == 1:
        joined = jnp.concatenate([query, key, value], axis=1)
        return jnp.pad(joined, ((0, 0), (0, LOW - joined.shape[1])))
    rank = query.shape[0]
    joined = jnp.zeros((LOW, QKV), query.dtype)
    joined = joined.at[:rank, :D].set(query)
    joined = joined.at[rank : 2 * rank, D : D + KVD].set(key)
    return joined.at[2 * rank : 3 * rank, D + KVD :].set(value)


def documents(grid, starts, length):
    own = starts.astype(BF16)
    other = grid.flip_core(own)
    chip = jnp.where(grid.c == 0, jnp.concatenate([own, other]), jnp.concatenate([other, own]))
    resets = jnp.zeros((grid.ys, chip.shape[0]), BF16)
    resets = lax.dynamic_update_slice(resets, chip[None], (grid.y, 0))
    for k in range(1, grid.ys):
        got = grid.along_y(chip, k)
        resets = lax.dynamic_update_slice(resets, got[None], ((grid.y - k) % grid.ys, 0))
    heard = resets
    resets = resets.reshape(-1).astype(jnp.int32)
    places = jnp.arange(resets.shape[0], dtype=jnp.int32)
    docs = jnp.cumsum(jnp.where(places == 0, 1, resets))
    padded = jnp.concatenate([jnp.full((WINDOW,), -1, jnp.int32), docs])
    extended = lax.dynamic_slice_in_dim(padded, grid.s * length, length + WINDOW, 0)
    own = extended[WINDOW:]
    before = extended[WINDOW - 1]
    last = own[-1]
    ends = docs[length - 1 :: length]
    places = jnp.arange(grid.seq, dtype=jnp.int32)
    tiles = jnp.tile(extended.reshape(-1, 1, WINDOW), (1, GROUPS, 1)).reshape(-1, WIDE)
    masks = dict(
        qdoc=own[:, None],
        kdoc=jnp.pad(tiles, ((0, 8 - tiles.shape[0]), (0, 0))),
        fresh=(own == before).astype(F32)[:, None],
        survive=(own == last).astype(F32)[:, None],
    )
    earlier = ((ends == before) & (places < grid.s)).astype(F32)
    entered = jnp.concatenate([jnp.full((1,), -1, jnp.int32), ends[:-1]])
    later = ((entered == last) & (places > grid.s)).astype(F32)
    pick = lambda v, k: lax.dynamic_index_in_dim(v, jnp.clip(grid.s + k, 0, grid.seq - 1), 0, False)
    former = [pick(earlier, -k) * (grid.s - k >= 0) for k in range(1, grid.seq)]
    latter = [pick(later, k) * (grid.s + k < grid.seq) for k in range(1, grid.seq)]
    return masks, former, latter, heard


def local(
    tokens, doc_starts, cotangent, norm_first, norm_second,
    w_query, w_key, w_value, w_out, w_gate_up, w_down,
    query_in, query_out, key_in, key_out, value_in, value_out, proj_in, proj_out,
    map_query, map_key, window_logit,
):
    grid = Grid()
    length = tokens.shape[1]
    rank = query_in.shape[1]
    hidden = tokens[0]
    grad_out = cotangent[0]
    gain_first = norm_first.astype(F32)[None, :]
    gain_second = norm_second.astype(F32)[None, :]

    masks, former, latter, heard = documents(grid, doc_starts[0], length)
    qkv = Gather(grid, jnp.concatenate([w_query, w_key, w_value], axis=1))
    out = Gather(grid, w_out)
    cot_near = spread_near(grid, grad_out)
    qkv.over_z()

    values = hidden.astype(F32)
    inverse_first = lax.rsqrt(jnp.mean(values * values, axis=-1, keepdims=True) + EPSILON)
    inputs = (values * inverse_first * gain_first).astype(BF16)
    gamma = jax.nn.sigmoid(window_logit)
    masks["gamma"] = jnp.repeat(gamma, HEAD)[None, :]
    half = HEAD // 2
    inverse_freq = jnp.power(THETA, -(jnp.arange(half, dtype=F32) * 2.0 / HEAD))
    places = (grid.s * length + jnp.arange(length, dtype=jnp.int32)).astype(F32)
    angles = places[:, None] * inverse_freq[None, :]
    sine = jnp.sin(angles)
    masks["cos"] = jnp.tile(jnp.cos(angles), (1, WIDE // half))
    masks["sin"] = jnp.tile(jnp.concatenate([-sine, sine], axis=1), (1, WIDE // HEAD))
    maps_q, maps_k = pair_maps(map_query), pair_maps(map_key)
    qkv_in = adapters(query_in, key_in, value_in, 1)
    qkv_out = adapters(query_out, key_out, value_out, 0)
    o_in = jnp.pad(proj_in, ((0, 0), (0, LOW - rank)))
    o_out = jnp.pad(proj_out, ((0, LOW - rank), (0, 0)))
    low = dot_nn(inputs, qkv_in).astype(BF16)

    cot_near, qkv.halves, heard, out.own = after((cot_near, qkv.halves, heard, out.own))
    qkv.first()
    out.over_z()
    ready = (masks, former, latter, maps_q, maps_k, qkv_in, qkv_out, o_in, o_out, inputs, low)
    mine = w_gate_up, w_down
    qkv.moved, out.halves, ready, mine, grad_out = after(
        (qkv.moved, out.halves, ready, mine, grad_out)
    )
    pair = pair_part(grid, *mine)
    masks, former, latter, maps_q, maps_k, qkv_in, qkv_out, o_in, o_out, inputs, low = ready
    cosine, sine = masks["cos"], masks["sin"]
    qkv.second()
    qkv.cores()
    half = length // 2
    cot_far = spread_far(grid, grad_out[:half], 1)
    late = grad_out[half:]
    qkv.last, qkv.over, out.halves, cot_far, late, pair = after(
        (qkv.last, qkv.over, out.halves, cot_far, late, pair)
    )
    pair = gather_pair(grid, pair)
    w_qkv = qkv.result()
    out.first()
    kv, kf, pack, full = project_kv(
        w_qkv, inputs, low, qkv_out[:, D:], cosine, sine, maps_k, masks["survive"]
    )
    kv, kf, pack, full, out.moved = after((kv, kf, pack, full, out.moved))
    rim = grid.along_seq(pack, 1)
    fulls = [grid.along_seq(full, k) for k in range(2, grid.seq)]
    out.second()
    queries = [
        project_q(i, w_qkv, inputs, low, qkv_out, cosine, sine, maps_q) for i in range(HALVES)
    ]
    rim, fulls, queries, out.blocks, out.last, late = after(
        (rim, fulls, queries, out.blocks, out.last, late)
    )
    out.cores()
    w_o = out.result()
    cot_far += spread_far(grid, late, 1)
    carry = former[0] * rim[2 * WINDOW :].astype(F32)
    for w, full in zip(former[1:], fulls):
        carry = carry + w * full.astype(F32)
    carry = carry.astype(BF16)
    merged, attended, inverse = [], [], []
    for i in range(HALVES):
        block = attend(i, *queries[i], kv, kf, rim, carry, masks)
        merged.append(block[0])
        attended.append(block[1])
        inverse.append(block[2])
    merged, w_o.blocks, cot_far = after((merged, w_o.blocks, cot_far))
    moved = relay(grid, cot_far[:1])[1:]
    residual, second_in, out_low, inverse_second = out_project(
        w_o, merged, hidden, o_in, o_out, gain_second
    )
    second_in, moved = after((second_in, moved))
    near = spread_near(grid, second_in)
    far = spread_far(grid, second_in[:half], 1)
    near, far, late, cot_far = after((near, far, second_in[half:], cot_far))
    others = relay(grid, cot_far[1:])[1:]
    cot_far = cot_far + [v for pieces in zip(moved, others) for v in pieces]
    far += spread_far(grid, late, 1)
    moved = relay(grid, far[:1])[1:]
    sums = mlp(near, cot_near, w_gate_up, w_down)
    sums, far, moved = after((sums, far, moved))
    others = relay(grid, far[1:])[1:]
    far = far + [v for pieces in zip(moved, others) for v in pieces]
    shard = w_gate_up, w_down, *pair
    near_out, near_grad = mlp(near, cot_near, *shard, own=False, sums=sums)
    far, near_out, near_grad = after((far, near_out, near_grad))
    far_out, far_grad = mlp(far, cot_far, *shard)
    terms = collect_near(grid, near_grad, length)
    far_grad, terms = after((far_grad, terms))
    send = collect_far(grid, far_grad, length, 2)
    near_out, far_out = after((near_out, far_out), send)
    terms.append(jnp.concatenate([grid.flip_z(v, NEAR_BIT) for v in send], axis=0))

    grad_residual, *grad_merged, grad_gain_two, grad_proj_in, grad_proj_out = branch_back(
        w_o, terms, grad_out, residual, inverse_second, gain_second, o_in, o_out, merged, out_low
    )
    scaled = [
        scaled_grads(i, grad_merged[i], attended[i], inverse[i], queries[i][1], masks)
        for i in range(HALVES)
    ]
    back = jnp.concatenate([v[2] for v in scaled], axis=1)
    far_back = jnp.zeros(back.shape, F32)
    for k in range(2, grid.seq):
        far_back = far_back + latter[k - 1] * grid.along_seq(back, -k).astype(F32)
    near_back = far_back + latter[0] * grid.along_seq(back, -1).astype(F32)
    near_back, far_back = near_back.astype(BF16), far_back.astype(BF16)
    out_terms = collect_near(grid, near_out, length)
    send = collect_far(grid, far_out, length, 1)
    scaled, out_terms, send = after((scaled, out_terms, send))
    out_terms += [grid.flip_z(v, NEAR_BIT) for v in send]
    backs = []
    for i in range(HALVES):
        backs.append(
            attend_back(i, *queries[i], kv, kf, rim, carry, *scaled[i][:2], masks, maps_q)
        )
    raw_query = [v[0] for v in backs]
    rim_back = [grid.along_seq(v[3], -1) for v in backs]
    raw_key, raw_value, dmap_key = [], [], []
    for i, (_, dkv, dkf, *_) in enumerate(backs):
        k, v, m = keys_back(
            i, kv, kf, dkv, dkf, rim_back[i], near_back, far_back, masks, maps_k
        )
        raw_key.append(k)
        raw_value.append(v)
        dmap_key.append(m)
    raw_key, out_terms = after((raw_key, out_terms))
    block_out = residual
    for term in out_terms:
        block_out = block_out + term.astype(F32)
    block_out = block_out.astype(BF16)
    dmap_query = jnp.concatenate([v[4] for v in backs], axis=0)
    dmap_key = jnp.concatenate(dmap_key, axis=0)
    dlogit = jnp.concatenate([v[5] for v in backs], axis=0)
    grad_tokens, grad_gain_one, grad_qkv_in, grad_qkv_out = inputs_back(
        w_qkv, [*raw_query, *raw_key, *raw_value], qkv_in, qkv_out, low, inputs,
        hidden, gain_first, grad_residual,
    )
    grad_logit = dlogit[:, :GROUPS, 0].reshape(HEADS) * (1.0 - gamma)
    grad_proj_in, grad_proj_out = grad_proj_in[:rank], grad_proj_out[:rank]

    blocks = lambda v: v.reshape(8, grid.seq, -1).swapaxes(0, 1)
    plain = lambda v: v.reshape(grid.seq, 8, -1)
    outs = (
        blocks(grad_qkv_out[:rank, :D]),
        blocks(grad_qkv_out[rank : 2 * rank, D : D + KVD]),
        blocks(grad_qkv_out[2 * rank : 3 * rank, D + KVD :]),
        blocks(grad_proj_out),
    )
    ins = [blocks(grad_qkv_in[i * rank : (i + 1) * rank]) for i in range(3)]
    ins.append(blocks(grad_proj_in))
    map_q = plain(dmap_query[:, :, :HEAD].reshape(HEADS, -1))
    map_k = dmap_key[:, :, :HEAD].reshape(KV_HEADS, grid.seq, -1).swapaxes(0, 1)
    logit = jnp.pad(grad_logit.reshape(grid.seq, -1, 1), ((0, 0), (0, 8 - HEADS // grid.seq), (0, 0)))
    sums = total_over_all(
        grid, [*outs, *ins, map_q, map_k, plain(grad_gain_one), plain(grad_gain_two), logit]
    )
    outs, ins, (map_q, map_k, gain_one, gain_two, logit) = sums[:4], sums[4:8], sums[8:]
    width = D // grid.seq
    return (
        block_out[None],
        grad_tokens[None],
        gain_one.reshape(width),
        gain_two.reshape(width),
        ins[0].T,
        outs[0],
        ins[1].T,
        outs[1],
        ins[2].T,
        outs[2],
        ins[3].T,
        outs[3],
        map_q.reshape(-1, HEAD, HEAD),
        map_k.reshape(KV_HEADS, -1, HEAD),
        logit[: HEADS // grid.seq, 0],
    )


def solution(mesh):
    placed = (
        P("rows", "seq", None),
        P("rows", "seq"),
        P("rows", "seq", None),
        P(),
        P(),
        P("rows", None),
        P("rows", None),
        P("rows", None),
        P("rows", None),
        P(None, None, "rows"),
        P("rows", None),
        P(),
        P(),
        P(),
        P(),
        P(),
        P(),
        P(),
        P(),
        P(),
        P(),
        P(),
    )
    return jax.shard_map(
        local,
        mesh=mesh,
        in_specs=placed,
        out_specs=(
            P("rows", "seq", None),
            P("rows", "seq", None),
            P("seq"),
            P("seq"),
            P("seq", None),
            P(None, "seq"),
            P("seq", None),
            P(None, "seq"),
            P("seq", None),
            P(None, "seq"),
            P("seq", None),
            P(None, "seq"),
            P("seq", None, None),
            P(None, "seq", None),
            P("seq"),
        ),
        check_vma=False,
    )
```

```python
import functools

import jax
import jax.numpy as jnp
from jax import lax
from jax.experimental import pallas as pl
from jax.experimental.pallas import tpu as pltpu
from jax.sharding import PartitionSpec as P

D = 2048
HEADS = 32
KV_HEADS = 8
HEAD = 64
WINDOW = 64
KVD = KV_HEADS * HEAD
GROUPS = HEADS // KV_HEADS
QKV = D + 2 * KVD
WIDE = GROUPS * HEAD
FEAT = 2 * HEAD
LOW = 128
STATE = 80
HALVES = 2
VMEM_LIMIT = 58 << 20
HALF = D // HALVES
PER_HALF = KV_HEADS // HALVES
SCALE = HEAD ** (-0.5)

EPSILON = 1e-05
THETA = 500000.0

Z_SIZE = 4
NEAR_BIT = 2
FAR_BIT = 1
CORES = 2
F32 = jnp.float32
BF16 = jnp.bfloat16


def dot_nn(a, b):
    return jnp.dot(a, b, preferred_element_type=F32)


def dot_nt(a, b):
    return lax.dot_general(a, b, (((1,), (1,)), ((), ())), preferred_element_type=F32)


def dot_tn(a, b):
    return lax.dot_general(a, b, (((0,), (0,)), ((), ())), preferred_element_type=F32)


def lane(shape):
    return lax.broadcasted_iota(jnp.int32, shape, 1)


def row(shape):
    return lax.broadcasted_iota(jnp.int32, shape, 0)


def low_half(shape):
    return lane(shape) % FEAT < HEAD


def turn(x, cosine, sine):
    width = x.shape[1]
    first = lane(x.shape) % HEAD < HEAD // 2
    swapped = jnp.where(
        first, pltpu.roll(x, width - HEAD // 2, 1), pltpu.roll(x, HEAD // 2, 1)
    )
    return x * cosine + swapped * sine


def halves_softmax(u):
    lo = low_half(u.shape)
    top = jnp.where(
        lo,
        jnp.max(jnp.where(lo, u, -jnp.inf), axis=1, keepdims=True),
        jnp.max(jnp.where(lo, -jnp.inf, u), axis=1, keepdims=True),
    )
    e = jnp.exp(u - top)
    total = jnp.where(
        lo,
        jnp.sum(jnp.where(lo, e, 0.0), axis=1, keepdims=True),
        jnp.sum(jnp.where(lo, 0.0, e), axis=1, keepdims=True),
    )
    return e / total


def halves_softmax_back(f, g):
    lo = low_half(f.shape)
    t = f * g
    total = jnp.where(
        lo,
        jnp.sum(jnp.where(lo, t, 0.0), axis=1, keepdims=True),
        jnp.sum(jnp.where(lo, 0.0, t), axis=1, keepdims=True),
    )
    v = f * (g - total)
    return v - pltpu.roll(v, HEAD, 1), t


def pair_features(x, maps):
    u = dot_nn(x, maps)
    return jnp.concatenate(
        [halves_softmax(u[:, :FEAT]), halves_softmax(u[:, FEAT:])], axis=1
    )


def same_head(size):
    shape = (GROUPS * size, WIDE)
    return (row(shape) // size == lane(shape) // HEAD).astype(F32)


def diagonal(tile, mask):
    wide = jnp.concatenate([tile, tile], axis=1)
    return (jnp.concatenate([wide] * GROUPS, axis=0) * mask).astype(BF16)


def diagonal_pair(tile):
    none = jnp.zeros_like(tile)
    return jnp.concatenate(
        [jnp.concatenate([tile, none], axis=1), jnp.concatenate([none, tile], axis=1)], axis=0
    )


def both_halves(kv):
    kv = kv.astype(F32)
    lo = low_half(kv.shape)
    other = pltpu.roll(kv, HEAD, 1)
    return jnp.where(lo, kv, other), jnp.where(lo, other, kv)


def fold_heads(r, mask):
    r = r * mask
    r = r[:64] + r[64:128] + r[128:192] + r[192:]
    r = r[:, :FEAT] + r[:, FEAT:]
    return r + pltpu.roll(r, HEAD, 1)


def fold_pair(r, size):
    return r[:size, :FEAT] + r[size:, FEAT:]


def whole(a):
    return pl.BlockSpec(a.shape, lambda *_: (0,) * len(a.shape))


ANYWHERE = pl.BlockSpec(memory_space=pl.ANY)
SCALARS = pl.BlockSpec(memory_space=pltpu.SMEM)


class Gathered:
    def __init__(self, blocks, places, size):
        self.blocks, self.places, self.size = blocks, places, size

    def shapes(self):
        return tuple(b.shape[0] // self.size for b in self.blocks)


def start_rows(places, refs, counts, size, target, sem, column=0):
    n = 0
    columns = slice(column, column + target.shape[1])
    for ref, count in zip(refs, counts):
        for i in range(count):
            to = pl.ds(pl.multiple_of(places[n] * size, size), size)
            part = ref.at[i * size : (i + 1) * size, columns]
            pltpu.make_async_copy(part, target.at[to], sem).start()
            n += 1


def wait_rows(target, sem):
    pltpu.make_async_copy(target, target, sem).wait()


def project_kv_kernel(*refs, counts, size):
    n = len(counts)
    places_ref, blocks = refs[0], refs[1 : 1 + n]
    x_ref, low_ref, p_ref, cos_ref, sin_ref, maps_ref, survive_ref = refs[1 + n : 8 + n]
    kv_ref, kf_ref, pack_ref, full_ref, w_ref, sem = refs[8 + n :]
    length = x_ref.shape[0]
    start_rows(places_ref, blocks, counts, size, w_ref, sem, D)
    wait_rows(w_ref, sem)
    survive = survive_ref[...]
    lo = low_half((length, FEAT))
    cut = length - WINDOW
    steps = KVD // WIDE
    part = lambda j: slice(j * WIDE, (j + 1) * WIDE)
    for i in range(steps):
        raw_k, raw_v = (
            dot_nn(x_ref[...], w_ref[:, part(j)]) + dot_nn(low_ref[...], p_ref[:, part(j)])
            for j in (i, steps + i)
        )
        keys = turn(raw_k, cos_ref[...], sin_ref[...]).astype(BF16)
        values = raw_v.astype(BF16).astype(F32)
        for p in range(WIDE // FEAT):
            at = (i * GROUPS + 2 * p) * FEAT
            k2 = keys[:, p * FEAT : (p + 1) * FEAT]
            v2 = values[:, p * FEAT : (p + 1) * FEAT]
            feats = pair_features(k2, maps_ref[2 * i + p])
            kf_ref[:, at : at + 2 * FEAT] = feats.astype(BF16)
            k2 = k2.astype(F32)
            k_other, v_other = pltpu.roll(k2, HEAD, 1), pltpu.roll(v2, HEAD, 1)
            ones = jnp.where(lane((length, FEAT)) < HEAD + 8, 1.0, 0.0)
            for h, kv, v in (
                (0, jnp.where(lo, k2, v_other), v2),
                (1, jnp.where(lo, k_other, v2), v_other),
            ):
                at_h = at + h * FEAT
                kv_ref[:, at_h : at_h + FEAT] = kv.astype(BF16)
                v_one = jnp.where(lo, v, ones).astype(BF16)
                kept = (feats[:, h * FEAT : (h + 1) * FEAT].astype(BF16).astype(F32) * survive)
                kept = kept.astype(BF16)
                head = dot_tn(v_one[:cut], kept[:cut])
                tail = dot_tn(v_one[cut:], kept[cut:])
                at_h = slice(at_h, at_h + FEAT)
                pack_ref[2 * WINDOW :, at_h] = head[:STATE].astype(BF16)
                full_ref[:, at_h] = (head + tail)[:STATE].astype(BF16)
    pack_ref[:WINDOW, :] = kv_ref[cut:, :]
    pack_ref[WINDOW : 2 * WINDOW, :] = kf_ref[cut:, :]


def project_kv(w, x, low, p, cosine, sine, maps, survive):
    length = x.shape[0]
    shapes = (
        jax.ShapeDtypeStruct((length, KV_HEADS * FEAT), BF16),
        jax.ShapeDtypeStruct((length, KV_HEADS * FEAT), BF16),
        jax.ShapeDtypeStruct((2 * WINDOW + STATE, KV_HEADS * FEAT), BF16),
        jax.ShapeDtypeStruct((STATE, KV_HEADS * FEAT), BF16),
    )
    rest = (x, low, p, cosine, sine, maps, survive)
    return pl.pallas_call(
        functools.partial(project_kv_kernel, counts=w.shapes(), size=w.size),
        grid=(1,),
        in_specs=[SCALARS] + [ANYWHERE] * len(w.blocks) + [whole(a) for a in rest],
        out_specs=[whole(v) for v in shapes],
        out_shape=shapes,
        scratch_shapes=[pltpu.VMEM((D, 2 * KVD), BF16), pltpu.SemaphoreType.DMA],
        compiler_params=pltpu.CompilerParams(vmem_limit_bytes=VMEM_LIMIT),
        cost_estimate=pl.CostEstimate(
            flops=4 * length * D * KVD, bytes_accessed=4 * D * KVD, transcendentals=0
        ),
        name="project_kv",
    )(w.places, *w.blocks, *rest)


def project_q_kernel(*refs, counts, size, column):
    n = len(counts)
    places_ref, blocks = refs[0], refs[1 : 1 + n]
    x_ref, low_ref, p_ref, cos_ref, sin_ref, maps_ref, q_ref, qf_ref, w_ref, sem = refs[1 + n :]
    step = pl.program_id(0)

    @pl.when(step == 0)
    def _():
        start_rows(places_ref, blocks, counts, size, w_ref, sem, column)
        wait_rows(w_ref, sem)

    at = pl.ds(pl.multiple_of(step * WIDE, WIDE), WIDE)
    raw = dot_nn(x_ref[...], w_ref[:, at]) + dot_nn(low_ref[...], p_ref[...])
    q = turn(raw, cos_ref[...], sin_ref[...]).astype(BF16)
    q_ref[...] = q
    for p in range(WIDE // FEAT):
        feats = pair_features(q[:, p * FEAT : (p + 1) * FEAT], maps_ref[p])
        qf_ref[:, 2 * p * FEAT : 2 * (p + 1) * FEAT] = feats.astype(BF16)


def project_q(half, w, x, low, p, cosine, sine, maps):
    length = x.shape[0]
    first = half * PER_HALF
    pairs = WIDE // FEAT
    return pl.pallas_call(
        functools.partial(
            project_q_kernel, counts=w.shapes(), size=w.size, column=half * HALF
        ),
        grid=(HALF // WIDE,),
        in_specs=[SCALARS] + [ANYWHERE] * len(w.blocks) + [
            whole(x), whole(low),
            pl.BlockSpec((LOW, WIDE), lambda g: (0, first + g)),
            whole(cosine), whole(sine),
            pl.BlockSpec((pairs, FEAT, 2 * FEAT), lambda g: (first + g, 0, 0)),
        ],
        out_specs=[
            pl.BlockSpec((length, WIDE), lambda g: (0, g)),
            pl.BlockSpec((length, 2 * WIDE), lambda g: (0, g)),
        ],
        out_shape=[
            jax.ShapeDtypeStruct((length, HALF), BF16),
            jax.ShapeDtypeStruct((length, 2 * HALF), BF16),
        ],
        scratch_shapes=[pltpu.VMEM((D, HALF), BF16), pltpu.SemaphoreType.DMA],
        compiler_params=pltpu.CompilerParams(vmem_limit_bytes=VMEM_LIMIT),
        cost_estimate=pl.CostEstimate(
            flops=2 * length * D * HALF, bytes_accessed=2 * D * HALF, transcendentals=0
        ),
        name="project_q",
    )(w.places, *w.blocks, x, low, p, cosine, sine, maps)


def key_tiles(kv_ref, kf_ref, rim_kv_ref, rim_kf_ref, mask):
    tiles = []
    for t in range(1 + kv_ref.shape[0] // WINDOW):
        if t == 0:
            kv, kf = rim_kv_ref[...], rim_kf_ref[...]
        else:
            at = (t - 1) * WINDOW
            kv, kf = kv_ref[at : at + WINDOW, :], kf_ref[at : at + WINDOW, :]
        kk, vv = both_halves(kv)
        tiles.append((diagonal(kk, mask * SCALE), diagonal(vv, mask), diagonal_pair(kf)))
    return tiles


def spans(t, length):
    edge = lambda v: min(max(v, 0), length)
    a, b, c = edge((t - 1) * WINDOW), edge(t * WINDOW), edge((t + 1) * WINDOW)
    return (a, b), (b, c), (c, length)


def weights_of(t, tile, q_ref, qf_ref, same, upper, gamma):
    length = q_ref.shape[0]
    (a, b), (_, c), _ = spans(t, length)
    e = jnp.exp(dot_nt(q_ref[a:c, :], tile[0]))
    linear = None
    if b < length:
        linear = gamma * jnp.concatenate(
            [
                dot_nt(qf_ref[b:, 2 * p * FEAT : 2 * (p + 1) * FEAT], tile[2])
                for p in range(GROUPS // 2)
            ],
            axis=1,
        )
    parts = []
    if b > a:
        parts.append(jnp.where(same(a, b) & upper, e[: b - a], 0.0))
    if c > b:
        mixed = jnp.where(upper, linear[: c - b], e[b - a :])
        parts.append(jnp.where(same(b, c), mixed, 0.0))
    if length > c:
        parts.append(jnp.where(same(c, length), linear[c - b :], 0.0))
    return e, jnp.concatenate(parts, axis=0).astype(BF16)


def carried(carry_ref):
    state = carry_ref[...]
    ones = jnp.zeros((HEAD, FEAT), BF16) + state[HEAD : HEAD + 1, :]
    return diagonal_pair(state[:HEAD, :]), diagonal_pair(ones)


def attend_kernel(
    q_ref, qf_ref, kv_ref, kf_ref, rim_kv_ref, rim_kf_ref, carry_ref,
    qdoc_ref, kdoc_ref, fresh_ref, gamma_ref,
    out_ref, att_ref, inv_ref, num_ref, den_ref,
):
    length = q_ref.shape[0]
    mask = same_head(WINDOW)
    ones = mask.astype(BF16)
    gamma = gamma_ref[...]
    shape = (WINDOW, WIDE)
    upper = row(shape) >= lane(shape) % HEAD
    state, state_sum = carried(carry_ref)
    fresh = fresh_ref[...] * gamma
    for p in range(GROUPS // 2):
        feats = qf_ref[:, 2 * p * FEAT : 2 * (p + 1) * FEAT]
        at = slice(p * FEAT, (p + 1) * FEAT)
        num_ref[:, at] = dot_nt(feats, state) * fresh[:, at]
        den_ref[:, at] = dot_nt(feats, state_sum) * fresh[:, at]
    for t, tile in enumerate(key_tiles(kv_ref, kf_ref, rim_kv_ref, rim_kf_ref, mask)):
        a = spans(t, length)[0][0]
        same = lambda i, j, t=t: qdoc_ref[i:j, :] == kdoc_ref[t : t + 1, :]
        _, w = weights_of(t, tile, q_ref, qf_ref, same, upper, gamma)
        num_ref[a:, :] += dot_nn(w, tile[1])
        den_ref[a:, :] += dot_nn(w, ones)
    inv = 1.0 / den_ref[...]
    att = num_ref[...] * inv
    inv_ref[...] = inv
    att_ref[...] = att
    out_ref[...] = att.astype(BF16)


def group_specs(length, half):
    first = half * PER_HALF
    column = lambda rows, width: pl.BlockSpec((rows, width), lambda g: (0, g))
    shared = lambda rows, width, at: pl.BlockSpec((rows, width), lambda g: (0, at + g))
    fixed = lambda rows, width: pl.BlockSpec((rows, width), lambda g: (0, 0))
    return dict(
        q=column(length, WIDE),
        qf=column(length, 2 * WIDE),
        k=shared(length, FEAT, first),
        rim_kv=shared(WINDOW, FEAT, first),
        rim_kf=pl.BlockSpec((WINDOW, FEAT), lambda g: (1, first + g)),
        state=shared(STATE, FEAT, first),
        back=column(STATE, FEAT),
        qdoc=fixed(length, 1),
        kdoc=fixed(8, WIDE),
        gamma=shared(1, WIDE, first),
        wide=fixed(length, WIDE),
        maps=pl.BlockSpec((GROUPS // 2, FEAT, 2 * FEAT), lambda g: (first + g, 0, 0)),
    )


def attend(half, q, qf, kv, kf, rim, carry, masks):
    length = q.shape[0]
    s = group_specs(length, half)
    return pl.pallas_call(
        attend_kernel,
        grid=(PER_HALF,),
        in_specs=[
            s["q"], s["qf"], s["k"], s["k"], s["rim_kv"], s["rim_kf"], s["state"],
            s["qdoc"], s["kdoc"], s["qdoc"], s["gamma"],
        ],
        out_specs=[s["q"]] * 3,
        out_shape=[
            jax.ShapeDtypeStruct((length, HALF), BF16),
            jax.ShapeDtypeStruct((length, HALF), F32),
            jax.ShapeDtypeStruct((length, HALF), F32),
        ],
        scratch_shapes=[pltpu.VMEM((length, WIDE), F32)] * 2,
        compiler_params=pltpu.CompilerParams(vmem_limit_bytes=VMEM_LIMIT),
        cost_estimate=pl.CostEstimate(
            flops=5_000_000_000, bytes_accessed=8 * length * D, transcendentals=0
        ),
        name="attend",
    )(q, qf, kv, kf, rim, rim, carry, masks["qdoc"], masks["kdoc"], masks["fresh"], masks["gamma"])


def scaled_grads_kernel(
    ga_ref, att_ref, inv_ref, qf_ref, fresh_ref, gamma_ref, g_ref, gd_ref, back_ref
):
    mask = same_head(HEAD)
    ga = ga_ref[...].astype(F32)
    inv = inv_ref[...]
    product = ga * att_ref[...]
    high = product.astype(BF16)
    rest = (product - high.astype(F32)).astype(BF16)
    ones = mask.astype(BF16)
    gd = -(dot_nn(high, ones) + dot_nn(rest, ones)) * inv
    g = ga * inv
    g_ref[...] = g.astype(BF16)
    gd_ref[...] = gd
    fresh = fresh_ref[...] * gamma_ref[...]
    fresh_g = (g * fresh).astype(BF16)
    fresh_gd = (gd * fresh).astype(BF16)
    kv = sums = 0.0
    for p in range(GROUPS // 2):
        feats = qf_ref[:, 2 * p * FEAT : 2 * (p + 1) * FEAT]
        at = slice(p * FEAT, (p + 1) * FEAT)
        kv += fold_pair(dot_tn(fresh_g[:, at], feats), HEAD)
        sums += fold_pair(dot_tn(fresh_gd[:, at], feats), HEAD)
    back_ref[:HEAD, :] = kv.astype(BF16)
    back_ref[HEAD:, :] = sums[: STATE - HEAD].astype(BF16)


def scaled_grads(half, ga, att, inv, qf, masks):
    length = ga.shape[0]
    s = group_specs(length, half)
    return pl.pallas_call(
        scaled_grads_kernel,
        grid=(PER_HALF,),
        in_specs=[s["q"], s["q"], s["q"], s["qf"], s["qdoc"], s["gamma"]],
        out_specs=[s["q"], s["q"], s["back"]],
        out_shape=[
            jax.ShapeDtypeStruct((length, HALF), BF16),
            jax.ShapeDtypeStruct((length, HALF), F32),
            jax.ShapeDtypeStruct((STATE, PER_HALF * FEAT), BF16),
        ],
        compiler_params=pltpu.CompilerParams(vmem_limit_bytes=VMEM_LIMIT),
        name="scaled_grads",
    )(ga, att, inv, qf, masks["fresh"], masks["gamma"])


def attend_back_kernel(
    q_ref, qf_ref, kv_ref, kf_ref, rim_kv_ref, rim_kf_ref, carry_ref, g_ref, gd_ref,
    qdoc_ref, kdoc_ref, fresh_ref, gamma_ref, maps_ref, cos_ref, sin_ref,
    raw_ref, dkv_ref, dkf_ref, rim_ref, dmap_ref, logit_ref, dq_ref, dqf_ref,
):
    length = q_ref.shape[0]
    mask = same_head(WINDOW)
    gamma = gamma_ref[...]
    shape = (WINDOW, WIDE)
    upper = row(shape) >= lane(shape) % HEAD
    state, state_sum = carried(carry_ref)
    fresh = fresh_ref[...] * gamma
    pairs = range(GROUPS // 2)
    half = lambda p: slice(p * FEAT, (p + 1) * FEAT)
    full = lambda p: slice(2 * p * FEAT, 2 * (p + 1) * FEAT)
    fresh_g = (g_ref[...].astype(F32) * fresh).astype(BF16)
    fresh_gd = (gd_ref[...] * fresh * (1.0 / HEAD)).astype(BF16)
    for p in pairs:
        dqf_ref[:, full(p)] = dot_nn(fresh_g[:, half(p)], state) + dot_nn(
            fresh_gd[:, half(p)], state_sum
        )
    dq_ref[...] = jnp.zeros_like(dq_ref)
    lo = low_half((WINDOW, FEAT))
    for t, tile in enumerate(key_tiles(kv_ref, kf_ref, rim_kv_ref, rim_kf_ref, mask)):
        (a, b), (_, c), _ = spans(t, length)
        same = lambda i, j, t=t: qdoc_ref[i:j, :] == kdoc_ref[t : t + 1, :]
        e, w = weights_of(t, tile, q_ref, qf_ref, same, upper, gamma)
        g = g_ref[a:, :]
        x = dot_nt(g, tile[1]) + gd_ref[a:, :]
        near = x[: c - a] * e
        parts = []
        if b > a:
            parts.append(jnp.where(same(a, b) & upper, near[: b - a], 0.0))
        if c > b:
            parts.append(jnp.where(same(b, c), jnp.where(upper, 0.0, near[b - a :]), 0.0))
        ds = jnp.concatenate(parts, axis=0).astype(BF16)
        dq_ref[a:c, :] += dot_nn(ds, tile[0])
        dk = fold_heads(dot_tn(ds, q_ref[a:c, :]), mask) * SCALE
        dv = fold_heads(dot_tn(w, g), mask)
        at = slice((t - 1) * WINDOW, t * WINDOW)
        dkv = jnp.where(lo, dk, dv)
        if t:
            dkv_ref[at, :] = dkv
        else:
            rim_ref[:WINDOW, :] = dkv.astype(BF16)
        if b < length:
            far = x[b - a :] * gamma
            parts = [jnp.where(same(b, c) & upper, far[: c - b], 0.0)]
            if c < length:
                parts.append(jnp.where(same(c, length), far[c - b :], 0.0))
            dl = jnp.concatenate(parts, axis=0).astype(BF16)
            dkf = 0.0
            for p in pairs:
                dqf_ref[b:, full(p)] += dot_nn(dl[:, half(p)], tile[2])
                dkf += fold_pair(dot_tn(dl[:, half(p)], qf_ref[b:, full(p)]), HEAD)
            if t:
                dkf_ref[at, :] = dkf
            else:
                rim_ref[WINDOW:, :] = dkf.astype(BF16)
        else:
            dkf_ref[at, :] = jnp.zeros((WINDOW, FEAT), F32)
    for p in pairs:
        grads = []
        for h in (2 * p, 2 * p + 1):
            f = qf_ref[:, h * FEAT : (h + 1) * FEAT].astype(F32)
            gu, t = halves_softmax_back(f, dqf_ref[:, h * FEAT : (h + 1) * FEAT])
            grads.append(gu.astype(BF16))
            total = jnp.sum(jnp.sum(t, axis=0, keepdims=True), axis=1, keepdims=True)
            logit_ref[0, h : h + 1, :] = jnp.zeros((1, FEAT), F32) + total
        gu = jnp.concatenate(grads, axis=1)
        dq_ref[:, half(p)] += 0.5 * dot_nt(gu, maps_ref[p])
        dmap = dot_tn(q_ref[:, half(p)], gu)
        dmap_ref[2 * p] = dmap[:HEAD, :FEAT]
        dmap_ref[2 * p + 1] = dmap[HEAD:, FEAT:]
    raw_ref[...] = turn(dq_ref[...], cos_ref[...], -sin_ref[...]).astype(BF16)


def attend_back(half, q, qf, kv, kf, rim, carry, g, gd, masks, maps):
    length = q.shape[0]
    s = group_specs(length, half)
    column = lambda rows: pl.BlockSpec((rows, FEAT), lambda g: (0, g))
    return pl.pallas_call(
        attend_back_kernel,
        grid=(PER_HALF,),
        in_specs=[
            s["q"], s["qf"], s["k"], s["k"], s["rim_kv"], s["rim_kf"], s["state"], s["q"], s["q"],
            s["qdoc"], s["kdoc"], s["qdoc"], s["gamma"], s["maps"], s["wide"], s["wide"],
        ],
        out_specs=[
            s["q"], column(length), column(length), column(2 * WINDOW),
            pl.BlockSpec((GROUPS, HEAD, FEAT), lambda g: (g, 0, 0)),
            pl.BlockSpec((1, 8, FEAT), lambda g: (g, 0, 0)),
        ],
        out_shape=[
            jax.ShapeDtypeStruct((length, HALF), BF16),
            jax.ShapeDtypeStruct((length, PER_HALF * FEAT), F32),
            jax.ShapeDtypeStruct((length, PER_HALF * FEAT), F32),
            jax.ShapeDtypeStruct((2 * WINDOW, PER_HALF * FEAT), BF16),
            jax.ShapeDtypeStruct((HEADS // HALVES, HEAD, FEAT), F32),
            jax.ShapeDtypeStruct((PER_HALF, 8, FEAT), F32),
        ],
        scratch_shapes=[pltpu.VMEM((length, WIDE), F32), pltpu.VMEM((length, 2 * WIDE), F32)],
        compiler_params=pltpu.CompilerParams(vmem_limit_bytes=VMEM_LIMIT),
        cost_estimate=pl.CostEstimate(
            flops=15_000_000_000, bytes_accessed=8 * length * D, transcendentals=0
        ),
        name="attend_back",
    )(
        q, qf, kv, kf, rim, rim, carry, g, gd,
        masks["qdoc"], masks["kdoc"], masks["fresh"], masks["gamma"],
        maps, masks["cos"], masks["sin"],
    )


def keys_back_kernel(
    kv_ref, kf_ref, dkv_ref, dkf_ref, rim_kv_ref, rim_kf_ref, near_ref, far_ref, survive_ref,
    maps_ref, cos_ref, sin_ref, rk_ref, rv_ref, dmap_ref,
):
    length = kv_ref.shape[0]
    cut = length - WINDOW
    lo = low_half((length, FEAT))
    survive = survive_ref[...]
    dkv, grads = [], []
    for h in range(2):
        at = slice(h * FEAT, (h + 1) * FEAT)
        kv = kv_ref[:, at].astype(F32)
        kf = kf_ref[:, at]
        v_low = pltpu.roll(kv, HEAD, 1)
        ones = jnp.where(lane((length, FEAT)) == HEAD, 1.0, 0.0)
        v_one = jnp.where(lo, v_low, ones).astype(BF16)[:, :STATE]
        dkf, dv = [], []
        for back, part in ((near_ref, slice(0, cut)), (far_ref, slice(cut, length))):
            state = back[:, at]
            twice = jnp.concatenate([state[:HEAD], state[:HEAD]], axis=0)
            dkf.append(dot_nn(v_one[part], state))
            dv.append(dot_nt(kf[part], twice))
        rim = jnp.zeros((cut, FEAT), F32)
        dkf = (
            jnp.concatenate(dkf, axis=0) * survive
            + dkf_ref[:, at]
            + jnp.concatenate([rim, rim_kf_ref[:, at].astype(F32)], axis=0)
        )
        dv = jnp.concatenate(dv, axis=0) * survive
        total = (
            dkv_ref[:, at]
            + jnp.concatenate([rim, rim_kv_ref[:, at].astype(F32)], axis=0)
            + jnp.where(lo, 0.0, dv)
        )
        gu, _ = halves_softmax_back(kf.astype(F32), dkf)
        grads.append(gu.astype(BF16))
        dkv.append(total)
    gu = jnp.concatenate(grads, axis=1)
    keys = jnp.where(lo, kv_ref[:, :FEAT].astype(F32), pltpu.roll(kv_ref[:, FEAT:].astype(F32), HEAD, 1))
    dmap = dot_tn(keys.astype(BF16), gu)
    dmap_ref[0] = dmap[:HEAD, :FEAT]
    dmap_ref[1] = dmap[HEAD:, FEAT:]
    dk = jnp.where(lo, dkv[0], pltpu.roll(dkv[1], HEAD, 1)) + 0.5 * dot_nt(gu, maps_ref[0])
    rk_ref[...] = turn(dk, cos_ref[...], -sin_ref[...]).astype(BF16)
    rv_ref[...] = jnp.where(lo, pltpu.roll(dkv[0], HEAD, 1), dkv[1]).astype(BF16)


def keys_back(half, kv, kf, dkv, dkf, rim, near, far, masks, maps):
    length = kv.shape[0]
    pairs = PER_HALF // 2
    first = half * pairs
    column = lambda rows: pl.BlockSpec((rows, 2 * FEAT), lambda g: (0, g))
    shared = pl.BlockSpec((length, 2 * FEAT), lambda g: (0, first + g))
    state = pl.BlockSpec((STATE, 2 * FEAT), lambda g: (0, first + g))
    narrow = pl.BlockSpec((length, FEAT), lambda g: (0, 0))
    out = pl.BlockSpec((length, FEAT), lambda g: (0, g))
    return pl.pallas_call(
        keys_back_kernel,
        grid=(pairs,),
        in_specs=[
            shared, shared, column(length), column(length),
            column(WINDOW), pl.BlockSpec((WINDOW, 2 * FEAT), lambda g: (1, g)),
            state, state, pl.BlockSpec((length, 1), lambda g: (0, 0)),
            pl.BlockSpec((1, FEAT, 2 * FEAT), lambda g: (first + g, 0, 0)), narrow, narrow,
        ],
        out_specs=[out, out, pl.BlockSpec((2, HEAD, FEAT), lambda g: (g, 0, 0))],
        out_shape=[
            jax.ShapeDtypeStruct((length, KVD // HALVES), BF16),
            jax.ShapeDtypeStruct((length, KVD // HALVES), BF16),
            jax.ShapeDtypeStruct((PER_HALF, HEAD, FEAT), F32),
        ],
        compiler_params=pltpu.CompilerParams(vmem_limit_bytes=VMEM_LIMIT),
        name="keys_back",
    )(
        kv, kf, dkv, dkf, rim, rim, near, far, masks["survive"], maps, masks["cos"], masks["sin"]
    )


def out_project_kernel(*refs, counts, size):
    n = len(counts)
    places, blocks, refs = refs[0], refs[1 : 1 + n], refs[1 + n :]
    m0, m1, hidden, proj_in, proj_out, gain = refs[:6]
    residual, second, low, inverse, w, sem = refs[6:]
    start_rows(places, blocks, counts, size, w, sem)
    reduced = dot_nn(m0[...], proj_in[:HALF, :]) + dot_nn(m1[...], proj_in[HALF:, :])
    reduced = reduced.astype(BF16)
    low[...] = reduced
    wait_rows(w, sem)
    squares = 0.0
    for j in range(D // WIDE):
        at = slice(j * WIDE, (j + 1) * WIDE)
        sums = (
            hidden[:, at].astype(F32)
            + dot_nn(m0[...], w[:HALF, at])
            + dot_nn(m1[...], w[HALF:, at])
            + dot_nn(reduced, proj_out[:, at])
        )
        residual[:, at] = sums
        squares = squares + jnp.sum(sums * sums, axis=1, keepdims=True)
    inv = lax.rsqrt(squares * (1.0 / D) + EPSILON)
    inverse[...] = jnp.zeros(inverse.shape, F32) + inv
    second[...] = (residual[...] * inv * gain[...]).astype(BF16)


def out_project(w, merged, hidden, proj_in, proj_out, gain):
    length = hidden.shape[0]
    shapes = (
        jax.ShapeDtypeStruct((length, D), F32),
        jax.ShapeDtypeStruct((length, D), BF16),
        jax.ShapeDtypeStruct((length, LOW), BF16),
        jax.ShapeDtypeStruct((length, LOW), F32),
    )
    rest = (*merged, hidden, proj_in, proj_out, gain)
    return pl.pallas_call(
        functools.partial(out_project_kernel, counts=w.shapes(), size=w.size),
        grid=(1,),
        in_specs=[SCALARS] + [ANYWHERE] * len(w.blocks) + [whole(a) for a in rest],
        out_specs=[whole(v) for v in shapes],
        out_shape=shapes,
        scratch_shapes=[pltpu.VMEM((D, D), BF16), pltpu.SemaphoreType.DMA],
        compiler_params=pltpu.CompilerParams(vmem_limit_bytes=VMEM_LIMIT),
        cost_estimate=pl.CostEstimate(
            flops=2 * length * D * D, bytes_accessed=2 * D * D, transcendentals=0
        ),
        name="out_project",
    )(w.places, *w.blocks, *rest)


def branch_back_kernel(*refs, counts, size, extra):
    n = len(counts)
    places, blocks, refs = refs[0], refs[1 : 1 + n], refs[1 + n :]
    sums, refs = refs[:extra], refs[extra:]
    cot, residual, inverse, gain, proj_in, proj_out, m0, m1, low = refs[:9]
    grad_residual, g0, g1, grad_gain, grad_in, grad_out, w, sem = refs[9:]
    start_rows(places, blocks, counts, size, w, sem)
    total = sums[0][...].astype(F32)
    for v in sums[1:]:
        total = total + v[...].astype(F32)
    inv = inverse[:, :1]
    normed = residual[...] * inv
    product = total * normed
    grad_gain[...] = jnp.sum(product, axis=0, keepdims=True)
    scaled = total * gain[...]
    mean = jnp.sum(scaled * normed, axis=1, keepdims=True) * (1.0 / D)
    grad = cot[...].astype(F32) + inv * (scaled - normed * mean)
    grad_residual[...] = grad
    branch = grad.astype(BF16)
    grad_low = dot_nt(branch, proj_out[...]).astype(BF16)
    grad_out[...] = dot_tn(low[...], branch)
    for i, m in enumerate((m0, m1)):
        grad_in[:, i * HALF : (i + 1) * HALF] = dot_tn(grad_low, m[...])
    wait_rows(w, sem)
    for j in range(D // WIDE):
        at = slice(j * WIDE, (j + 1) * WIDE)
        i, col = j // (HALF // WIDE), (j % (HALF // WIDE)) * WIDE
        back = dot_nt(grad_low, proj_in[at, :]) + dot_nt(branch, w[at, :])
        (g0, g1)[i][:, col : col + WIDE] = back.astype(BF16)


def branch_back(w, sums, cot, residual, inverse, gain, proj_in, proj_out, merged, low):
    length = cot.shape[0]
    shapes = (
        jax.ShapeDtypeStruct((length, D), F32),
        jax.ShapeDtypeStruct((length, HALF), BF16),
        jax.ShapeDtypeStruct((length, HALF), BF16),
        jax.ShapeDtypeStruct((1, D), F32),
        jax.ShapeDtypeStruct((LOW, D), F32),
        jax.ShapeDtypeStruct((LOW, D), F32),
    )
    rest = (*sums, cot, residual, inverse, gain, proj_in, proj_out, *merged, low)
    return pl.pallas_call(
        functools.partial(
            branch_back_kernel, counts=w.shapes(), size=w.size, extra=len(sums)
        ),
        grid=(1,),
        in_specs=[SCALARS] + [ANYWHERE] * len(w.blocks) + [whole(a) for a in rest],
        out_specs=[whole(v) for v in shapes],
        out_shape=shapes,
        scratch_shapes=[pltpu.VMEM((D, D), BF16), pltpu.SemaphoreType.DMA],
        compiler_params=pltpu.CompilerParams(vmem_limit_bytes=VMEM_LIMIT),
        cost_estimate=pl.CostEstimate(
            flops=2 * length * D * D, bytes_accessed=2 * D * D, transcendentals=0
        ),
        name="branch_back",
    )(w.places, *w.blocks, *rest)


def inputs_back_kernel(*refs, counts, size):
    n = len(counts)
    places, blocks, refs = refs[0], refs[1 : 1 + n], refs[1 + n :]
    raws, refs = refs[:6], refs[6:]
    p_in, p_out, low, x, hidden, gain, grad_residual = refs[:7]
    grad_tokens, grad_gain, grad_in, grad_out, w, raw, back, sem = refs[7:]
    start_rows(places, blocks, counts, size, w, sem)
    at = 0
    for r in raws:
        raw[:, at : at + r.shape[1]] = r[...]
        at += r.shape[1]
    grad_low = dot_nt(raw[...], p_out[...]).astype(BF16)
    grad_out[...] = dot_tn(low[...], raw[...])
    grad_in[...] = dot_tn(grad_low, x[...])
    wait_rows(w, sem)
    values = hidden[...].astype(F32)
    inv = lax.rsqrt(jnp.sum(values * values, axis=1, keepdims=True) * (1.0 / D) + EPSILON)
    mean = 0.0
    for j in range(D // WIDE):
        at = slice(j * WIDE, (j + 1) * WIDE)
        part = dot_nt(grad_low, p_in[at, :]) + dot_nt(raw[...], w[at, :])
        normed = hidden[:, at].astype(F32) * inv
        product = part * normed
        grad_gain[:, at] = jnp.sum(product, axis=0, keepdims=True)
        mean = mean + jnp.sum(product * gain[:, at], axis=1, keepdims=True)
        back[:, at] = part
    mean = mean * (1.0 / D)
    grad_tokens[...] = grad_residual[...] + inv * (
        back[...] * gain[...] - values * inv * mean
    )


def inputs_back(w, raws, p_in, p_out, low, x, hidden, gain, grad_residual):
    length = x.shape[0]
    shapes = (
        jax.ShapeDtypeStruct((length, D), F32),
        jax.ShapeDtypeStruct((1, D), F32),
        jax.ShapeDtypeStruct((LOW, D), F32),
        jax.ShapeDtypeStruct((LOW, QKV), F32),
    )
    rest = (*raws, p_in, p_out, low, x, hidden, gain, grad_residual)
    return pl.pallas_call(
        functools.partial(inputs_back_kernel, counts=w.shapes(), size=w.size),
        grid=(1,),
        in_specs=[SCALARS] + [ANYWHERE] * len(w.blocks) + [whole(a) for a in rest],
        out_specs=[whole(v) for v in shapes],
        out_shape=shapes,
        scratch_shapes=[
            pltpu.VMEM((D, QKV), BF16),
            pltpu.VMEM((length, QKV), BF16),
            pltpu.VMEM((length, D), F32),
            pltpu.SemaphoreType.DMA,
        ],
        compiler_params=pltpu.CompilerParams(vmem_limit_bytes=VMEM_LIMIT),
        cost_estimate=pl.CostEstimate(
            flops=2 * length * D * QKV, bytes_accessed=2 * D * QKV, transcendentals=0
        ),
        name="inputs_back",
    )(w.places, *w.blocks, *rest)


def mlp_kernel(place_ref, *refs, rows, paired, tile, own, carried_in):
    n = len(rows[0]) + len(rows[1])
    tokens, refs = refs[:n], refs[n:]
    own_gu, own_dn = refs[:2]
    pair, refs = (refs[2], refs[3:]) if paired else (None, refs[2:])
    sums, refs = (refs[:2], refs[2:]) if carried_in else (None, refs)
    out_ref, back_ref, h, c, gu, dn, out, back, row_sem, gu_sem, dn_sem = refs
    step, steps = pl.program_id(0), pl.num_programs(0)
    own_tiles = own_gu.shape[2] // tile if own else 0

    def fetch(n, slot):
        @pl.when(n < own_tiles)
        def _():
            at = pl.ds(pl.multiple_of(n * tile, tile), tile)
            pltpu.make_async_copy(own_gu.at[:, :, at], gu.at[slot], gu_sem.at[slot]).start()
            pltpu.make_async_copy(own_dn.at[at, :], dn.at[slot], dn_sem.at[slot]).start()

        if not paired:
            return

        @pl.when(n >= own_tiles)
        def _():
            first = (n - own_tiles) * tile
            at = pl.ds(pl.multiple_of(first, tile), tile)
            width = pair.shape[1] // 3
            row = pl.ds(pl.multiple_of(2 * width + first % width, tile), tile)
            column = pl.ds(pl.multiple_of(first // width * width, width), width)
            for k in range(D // width):
                part = pair.at[2 * k + place_ref[0]]
                there = slice(k * width, (k + 1) * width)
                for i in range(2):
                    pltpu.make_async_copy(
                        part.at[i * width : (i + 1) * width, at],
                        gu.at[slot, i, there, :],
                        gu_sem.at[slot],
                    ).start()
                pltpu.make_async_copy(
                    part.at[row, column], dn.at[slot, :, there], dn_sem.at[slot]
                ).start()

    @pl.when(step == 0)
    def _():
        fetch(step, 0)
        copies = []
        for target, sizes in zip((h, c), rows):
            at = 0
            for size in sizes:
                i = len(copies)
                there = target.at[at : at + size]
                copies.append(pltpu.make_async_copy(tokens[i], there, row_sem.at[i]))
                at += size
        for copy in copies:
            copy.start()
        if carried_in:
            for i, target in enumerate((out, back)):
                copies.append(pltpu.make_async_copy(sums[i], target, row_sem.at[len(copies)]))
                copies[-1].start()
        else:
            out[...] = jnp.zeros_like(out)
            back[...] = jnp.zeros_like(back)
        for copy in copies:
            copy.wait()

    slot = step % 2

    @pl.when(step + 1 < steps)
    def _():
        fetch(step + 1, 1 - slot)

    pltpu.make_async_copy(own_gu.at[:, :, pl.ds(0, tile)], gu.at[slot], gu_sem.at[slot]).wait()
    pltpu.make_async_copy(own_dn.at[pl.ds(0, tile), :], dn.at[slot], dn_sem.at[slot]).wait()
    w_gate, w_up, w_down = gu.at[slot, 0], gu.at[slot, 1], dn.at[slot]
    gate = dot_nn(h[...], w_gate[...])
    up = dot_nn(h[...], w_up[...])
    grad = dot_nt(c[...], w_down[...])
    sig = jax.nn.sigmoid(gate)
    silu = gate * sig
    act = (silu * up).astype(BF16)
    grad_gate = (grad * up * sig * (1.0 + gate * (1.0 - sig))).astype(BF16)
    grad_up = (grad * silu).astype(BF16)
    out[...] += dot_nn(act, w_down[...])
    back[...] += dot_nt(grad_gate, w_gate[...]) + dot_nt(grad_up, w_up[...])

    @pl.when(step == steps - 1)
    def _():
        out_ref[...] = out[...].astype(out_ref.dtype)
        back_ref[...] = back[...].astype(back_ref.dtype)


def mlp(second, cot, own_gu, own_dn, pair=None, place=None, own=True, sums=()):
    rows = tuple(v.shape[0] for v in second), tuple(v.shape[0] for v in cot)
    total = sum(rows[0])
    hidden = own_gu.shape[2]
    tile = min(256, hidden)
    shards = own + (pair is not None)
    kind = F32 if pair is None else BF16
    if pair is None:
        place = jnp.zeros((1,), jnp.int32)
    block = pl.BlockSpec((total, D), lambda i, p: (0, 0))
    arrays = (*second, *cot, own_gu, own_dn, *(() if pair is None else (pair,)), *sums)
    return pl.pallas_call(
        functools.partial(
            mlp_kernel,
            rows=rows,
            paired=pair is not None,
            tile=tile,
            own=own,
            carried_in=bool(sums),
        ),
        grid_spec=pltpu.PrefetchScalarGridSpec(
            num_scalar_prefetch=1,
            grid=(shards * hidden // tile,),
            in_specs=[ANYWHERE] * len(arrays),
            out_specs=[block, block],
            scratch_shapes=[
                pltpu.VMEM((total, D), BF16),
                pltpu.VMEM((total, D), BF16),
                pltpu.VMEM((2, 2, D, tile), BF16),
                pltpu.VMEM((2, tile, D), BF16),
                pltpu.VMEM((total, D), F32),
                pltpu.VMEM((total, D), F32),
                pltpu.SemaphoreType.DMA((len(second) + len(cot) + len(sums),)),
                pltpu.SemaphoreType.DMA((2,)),
                pltpu.SemaphoreType.DMA((2,)),
            ],
        ),
        out_shape=[jax.ShapeDtypeStruct((total, D), kind)] * 2,
        compiler_params=pltpu.CompilerParams(vmem_limit_bytes=VMEM_LIMIT),
        cost_estimate=pl.CostEstimate(
            flops=12 * total * D * hidden * shards,
            bytes_accessed=6 * D * hidden * shards,
            transcendentals=0,
        ),
        name="mlp",
    )(place, *arrays)


class Grid:
    def __init__(self):
        self.seq = lax.axis_size("seq")
        self.rows = lax.axis_size("rows")
        self.zs = Z_SIZE
        self.xs = self.rows // Z_SIZE
        self.ys = self.seq // CORES
        s = lax.axis_index("seq")
        r = lax.axis_index("rows")
        self.y, self.c = s // CORES, s % CORES
        self.z, self.x = r // self.xs, r % self.xs
        self.s, self.r = s, r

    def send(self, value, move):
        route = []
        for s in range(self.seq):
            for r in range(self.rows):
                there = move(s // CORES, s % CORES, r // self.xs, r % self.xs)
                if there is not None:
                    y, c, z, x = there
                    target = (y * CORES + c) * self.rows + z * self.xs + x
                    route.append((s * self.rows + r, target))
        return jax.tree.map(lambda v: lax.ppermute(v, ("seq", "rows"), route), value)

    def along_z(self, value, k):
        return self.send(value, lambda y, c, z, x: (y, c, (z + k) % self.zs, x))

    def along_x(self, value, k):
        return self.send(value, lambda y, c, z, x: (y, c, z, (x + k) % self.xs))

    def along_y(self, value, k):
        return self.send(value, lambda y, c, z, x: ((y + k) % self.ys, c, z, x))

    def flip_z(self, value, bit):
        return self.send(value, lambda y, c, z, x: (y, c, z ^ bit, x))

    def flip_core(self, value):
        return self.send(value, lambda y, c, z, x: (y, 1 - c, z, x))

    def flip_x(self, value, bit):
        return self.send(value, lambda y, c, z, x: (y, c, z, x ^ bit))

    def flip_seq(self, value, bit):
        def move(y, c, z, x):
            s = (y * CORES + c) ^ bit
            return (s // CORES, s % CORES, z, x)

        return self.send(value, move)

    def along_seq(self, value, k):
        def move(y, c, z, x):
            s = y * CORES + c + k
            return (s // CORES, s % CORES, z, x) if 0 <= s < self.seq else None

        return self.send(value, move)


def after(values, *events):
    return lax.optimization_barrier((values, *events))[0]


class Gather:
    def __init__(self, grid, *shards):
        self.grid = grid
        self.size = shards[0].shape[0] // grid.seq
        at = grid.s * self.size
        own = [lax.dynamic_slice_in_dim(v, at, self.size, 0) for v in shards]
        self.own = jnp.concatenate(own, axis=1) if len(own) > 1 else own[0]

    def over_z(self):
        grid = self.grid
        pieces = [self.own] + [grid.along_z(self.own, k) for k in range(1, grid.zs)]
        half = grid.zs // 2
        self.halves = [jnp.concatenate(pieces[:half]), jnp.concatenate(pieces[half:])]

    def first(self):
        grid = self.grid
        a, b = self.halves
        self.moved = [
            [grid.along_x(a, k) for k in range(1, grid.xs)],
            [grid.along_y(b, k) for k in range(1, grid.ys)],
        ]

    def second(self):
        grid = self.grid
        a, b = (jnp.concatenate([h, *m]) for h, m in zip(self.halves, self.moved))
        self.blocks = [a, b]
        self.last = [grid.along_y(a, k) for k in range(1, grid.ys)]
        self.last += [grid.along_x(b, k) for k in range(1, grid.xs)]

    def cores(self):
        self.over = [self.grid.flip_core(b) for b in self.blocks]

    def result(self):
        grid = self.grid
        blocks = self.blocks + self.last
        blocks = blocks + self.over + [grid.flip_core(b) for b in self.last]
        places = []
        kzs = range(grid.zs // 2), range(grid.zs // 2, grid.zs)
        a = [(kx, 0, kz) for kx in range(grid.xs) for kz in kzs[0]]
        b = [(0, ky, kz) for ky in range(grid.ys) for kz in kzs[1]]
        moves = a + b
        for k in range(1, grid.ys):
            moves = moves + [(kx, k, kz) for kx, _, kz in a]
        for k in range(1, grid.xs):
            moves = moves + [(k, ky, kz) for _, ky, kz in b]
        for core in range(CORES):
            c = (grid.c + core) % CORES
            for kx, ky, kz in moves:
                z, x, y = (grid.z - kz) % grid.zs, (grid.x - kx) % grid.xs, (grid.y - ky) % grid.ys
                places.append((z * grid.xs + x) * grid.seq + y * CORES + c)
        return Gathered(blocks, jnp.stack(places).astype(jnp.int32), self.size)


def pair_part(grid, gate_up, down):
    part = D // grid.seq
    hidden = down.shape[0]
    size = (1, part, hidden)
    gu = [lax.dynamic_slice(gate_up, (i, grid.s * part, 0), size)[0] for i in range(2)]
    dn = lax.dynamic_slice_in_dim(down, grid.s * part, part, 1)
    dn = jnp.concatenate([dn[i : i + part] for i in range(0, hidden, part)], axis=1)
    return jnp.concatenate([*gu, dn], axis=0)


def gather_pair(grid, part):
    groups = []
    for z in range(0, grid.zs, 2):
        for x in range(grid.xs):
            rows = [(z + i) * grid.xs + x for i in range(2)]
            groups.append([s * grid.rows + r for s in range(grid.seq) for r in rows])
    parts = lax.all_gather(part, ("seq", "rows"), axis_index_groups=groups)
    return parts, (1 - grid.z % 2).reshape(1).astype(jnp.int32)


def spread_near(grid, block):
    return [block] + [grid.along_x(block, k) for k in range(1, grid.xs)]


def spread_far(grid, block, parts):
    size = block.shape[0] // parts
    return [grid.flip_z(block[p * size : (p + 1) * size], NEAR_BIT) for p in range(parts)]


def relay(grid, pieces):
    moved = [grid.along_x(piece, k) for k in range(1, grid.xs) for piece in pieces]
    return list(pieces) + moved


def collect_near(grid, near, length):
    blocks = [near[k * length : (k + 1) * length] for k in range(grid.xs)]
    return [blocks[0]] + [grid.along_x(blocks[k], -k) for k in range(1, grid.xs)]


def collect_far(grid, far, length, parts):
    size = length // parts
    send, total = [], None
    for p in range(parts):
        lo = p * size
        far = after(far, total)
        total = far[lo : lo + size]
        for k in range(1, grid.xs):
            other = grid.along_x(far[k * length + lo : k * length + lo + size], -k)
            total = (total.astype(F32) + other.astype(F32)).astype(BF16)
        send.append(total)
    return send


def total_over_all(grid, values):
    widths = [v.shape[2] for v in values]
    packed = jnp.concatenate([v.astype(BF16) for v in values], axis=2)
    packed = jnp.pad(packed, ((0, 0), (0, 0), (0, -packed.shape[2] % FEAT)))
    chunk = lambda i: lax.dynamic_index_in_dim(packed, i, 0, False)
    total = chunk(grid.s).astype(F32)
    for k in range(1, grid.seq):
        total = total + grid.flip_seq(chunk(grid.s ^ k), k).astype(F32)
    for flip, count in ((grid.flip_z, grid.zs), (grid.flip_x, grid.xs)):
        mine = total.astype(BF16)
        terms = [mine.astype(F32)] + [flip(mine, k).astype(F32) for k in range(1, count)]
        while len(terms) > 1:
            terms = [a + b for a, b in zip(terms[::2], terms[1::2])]
        total = terms[0]
    out, at = [], 0
    for w in widths:
        out.append(total[:, at : at + w])
        at += w
    return out


def pair_maps(maps):
    both = jnp.concatenate([maps, -maps], axis=-1)
    both = both.reshape(-1, 2, HEAD, FEAT)
    none = jnp.zeros_like(both[:, 0])
    return jnp.concatenate(
        [
            jnp.concatenate([both[:, 0], none], axis=-1),
            jnp.concatenate([none, both[:, 1]], axis=-1),
        ],
        axis=1,
    )


def adapters(query, key, value, axis):
    if axis == 1:
        joined = jnp.concatenate([query, key, value], axis=1)
        return jnp.pad(joined, ((0, 0), (0, LOW - joined.shape[1])))
    rank = query.shape[0]
    joined = jnp.zeros((LOW, QKV), query.dtype)
    joined = joined.at[:rank, :D].set(query)
    joined = joined.at[rank : 2 * rank, D : D + KVD].set(key)
    return joined.at[2 * rank : 3 * rank, D + KVD :].set(value)


def documents(grid, starts, length):
    own = starts.astype(BF16)
    other = grid.flip_core(own)
    chip = jnp.where(grid.c == 0, jnp.concatenate([own, other]), jnp.concatenate([other, own]))
    resets = jnp.zeros((grid.ys, chip.shape[0]), BF16)
    resets = lax.dynamic_update_slice(resets, chip[None], (grid.y, 0))
    for k in range(1, grid.ys):
        got = grid.along_y(chip, k)
        resets = lax.dynamic_update_slice(resets, got[None], ((grid.y - k) % grid.ys, 0))
    heard = resets
    resets = resets.reshape(-1).astype(jnp.int32)
    places = jnp.arange(resets.shape[0], dtype=jnp.int32)
    docs = jnp.cumsum(jnp.where(places == 0, 1, resets))
    padded = jnp.concatenate([jnp.full((WINDOW,), -1, jnp.int32), docs])
    extended = lax.dynamic_slice_in_dim(padded, grid.s * length, length + WINDOW, 0)
    own = extended[WINDOW:]
    before = extended[WINDOW - 1]
    last = own[-1]
    ends = docs[length - 1 :: length]
    places = jnp.arange(grid.seq, dtype=jnp.int32)
    tiles = jnp.tile(extended.reshape(-1, 1, WINDOW), (1, GROUPS, 1)).reshape(-1, WIDE)
    masks = dict(
        qdoc=own[:, None],
        kdoc=jnp.pad(tiles, ((0, 8 - tiles.shape[0]), (0, 0))),
        fresh=(own == before).astype(F32)[:, None],
        survive=(own == last).astype(F32)[:, None],
    )
    earlier = ((ends == before) & (places < grid.s)).astype(F32)
    entered = jnp.concatenate([jnp.full((1,), -1, jnp.int32), ends[:-1]])
    later = ((entered == last) & (places > grid.s)).astype(F32)
    pick = lambda v, k: lax.dynamic_index_in_dim(v, jnp.clip(grid.s + k, 0, grid.seq - 1), 0, False)
    former = [pick(earlier, -k) * (grid.s - k >= 0) for k in range(1, grid.seq)]
    latter = [pick(later, k) * (grid.s + k < grid.seq) for k in range(1, grid.seq)]
    return masks, former, latter, heard


def local(
    tokens, doc_starts, cotangent, norm_first, norm_second,
    w_query, w_key, w_value, w_out, w_gate_up, w_down,
    query_in, query_out, key_in, key_out, value_in, value_out, proj_in, proj_out,
    map_query, map_key, window_logit,
):
    grid = Grid()
    length = tokens.shape[1]
    rank = query_in.shape[1]
    hidden = tokens[0]
    grad_out = cotangent[0]
    gain_first = norm_first.astype(F32)[None, :]
    gain_second = norm_second.astype(F32)[None, :]

    masks, former, latter, heard = documents(grid, doc_starts[0], length)
    qkv = Gather(grid, w_query, w_key, w_value)
    out = Gather(grid, w_out)
    cot_near = spread_near(grid, grad_out)
    qkv.over_z()

    values = hidden.astype(F32)
    inverse_first = lax.rsqrt(jnp.mean(values * values, axis=-1, keepdims=True) + EPSILON)
    inputs = (values * inverse_first * gain_first).astype(BF16)
    gamma = jax.nn.sigmoid(window_logit)
    masks["gamma"] = jnp.repeat(gamma, HEAD)[None, :]
    half = HEAD // 2
    inverse_freq = jnp.power(THETA, -(jnp.arange(half, dtype=F32) * 2.0 / HEAD))
    places = (grid.s * length + jnp.arange(length, dtype=jnp.int32)).astype(F32)
    angles = places[:, None] * inverse_freq[None, :]
    sine = jnp.sin(angles)
    masks["cos"] = jnp.tile(jnp.cos(angles), (1, WIDE // half))
    masks["sin"] = jnp.tile(jnp.concatenate([-sine, sine], axis=1), (1, WIDE // HEAD))
    maps_q, maps_k = pair_maps(map_query), pair_maps(map_key)
    qkv_in = adapters(query_in, key_in, value_in, 1)
    qkv_out = adapters(query_out, key_out, value_out, 0)
    o_in = jnp.pad(proj_in, ((0, 0), (0, LOW - rank)))
    o_out = jnp.pad(proj_out, ((0, LOW - rank), (0, 0)))
    low = dot_nn(inputs, qkv_in).astype(BF16)

    cot_near, qkv.halves, heard, out.own = after((cot_near, qkv.halves, heard, out.own))
    qkv.first()
    out.over_z()
    ready = (masks, former, latter, maps_q, maps_k, qkv_in, qkv_out, o_in, o_out, inputs, low)
    mine = w_gate_up, w_down
    qkv.moved, out.halves, ready, mine, grad_out = after(
        (qkv.moved, out.halves, ready, mine, grad_out)
    )
    pair = pair_part(grid, *mine)
    masks, former, latter, maps_q, maps_k, qkv_in, qkv_out, o_in, o_out, inputs, low = ready
    cosine, sine = masks["cos"], masks["sin"]
    qkv.second()
    qkv.cores()
    half = length // 2
    cot_far = spread_far(grid, grad_out[:half], 1)
    late = grad_out[half:]
    qkv.last, qkv.over, out.halves, cot_far, late, pair = after(
        (qkv.last, qkv.over, out.halves, cot_far, late, pair)
    )
    pair = gather_pair(grid, pair)
    w_qkv = qkv.result()
    out.first()
    kv, kf, pack, full = project_kv(
        w_qkv, inputs, low, qkv_out[:, D:], cosine, sine, maps_k, masks["survive"]
    )
    kv, kf, pack, full, out.moved, late = after((kv, kf, pack, full, out.moved, late))
    cot_far += spread_far(grid, late, 1)
    rim = grid.along_seq(pack, 1)
    fulls = [grid.along_seq(full, k) for k in range(2, grid.seq)]
    queries = [project_q(0, w_qkv, inputs, low, qkv_out, cosine, sine, maps_q)]
    rim, fulls, out.moved, queries = after((rim, fulls, out.moved, queries))
    out.second()
    queries.append(project_q(1, w_qkv, inputs, low, qkv_out, cosine, sine, maps_q))
    carry = former[0] * rim[2 * WINDOW :].astype(F32)
    for w, full in zip(former[1:], fulls):
        carry = carry + w * full.astype(F32)
    carry = carry.astype(BF16)
    merged, attended, inverse = [], [], []
    for i in range(HALVES):
        block = attend(i, *queries[i], kv, kf, rim, carry, masks)
        merged.append(block[0])
        attended.append(block[1])
        inverse.append(block[2])
        if i == 0:
            out.blocks, out.last, merged, queries, cot_far = after(
                (out.blocks, out.last, merged, queries, cot_far)
            )
            out.cores()
            w_o = out.result()
    merged, w_o.blocks, cot_far[0] = after((merged, w_o.blocks, cot_far[0]))
    moved = relay(grid, cot_far[:1])[1:]
    residual, second_in, out_low, inverse_second = out_project(
        w_o, merged, hidden, o_in, o_out, gain_second
    )
    second_in, moved = after((second_in, moved))
    near = spread_near(grid, second_in)
    far = spread_far(grid, second_in[:half], 1)
    near, far, late, cot_far = after((near, far, second_in[half:], cot_far))
    others = relay(grid, cot_far[1:])[1:]
    cot_far = cot_far + [v for pieces in zip(moved, others) for v in pieces]
    far += spread_far(grid, late, 1)
    moved = relay(grid, far[:1])[1:]
    sums = mlp(near, cot_near, w_gate_up, w_down)
    sums, far, moved = after((sums, far, moved))
    others = relay(grid, far[1:])[1:]
    far = far + [v for pieces in zip(moved, others) for v in pieces]
    shard = w_gate_up, w_down, *pair
    near_out, near_grad = mlp(near, cot_near, *shard, own=False, sums=sums)
    far, near_out, near_grad = after((far, near_out, near_grad))
    far_out, far_grad = mlp(far, cot_far, *shard)
    terms = collect_near(grid, near_grad, length)
    far_grad, terms = after((far_grad, terms))
    send = collect_far(grid, far_grad, length, 2)
    near_out, far_out = after((near_out, far_out), send)
    terms.append(jnp.concatenate([grid.flip_z(v, NEAR_BIT) for v in send], axis=0))

    grad_residual, *grad_merged, grad_gain_two, grad_proj_in, grad_proj_out = branch_back(
        w_o, terms, grad_out, residual, inverse_second, gain_second, o_in, o_out, merged, out_low
    )
    scaled = [
        scaled_grads(i, grad_merged[i], attended[i], inverse[i], queries[i][1], masks)
        for i in range(HALVES)
    ]
    back = jnp.concatenate([v[2] for v in scaled], axis=1)
    out_terms = collect_near(grid, near_out, length)
    send = collect_far(grid, far_out, length, 1)
    back, scaled, out_terms, send = after((back, scaled, out_terms, send))
    out_terms += [grid.flip_z(v, NEAR_BIT) for v in send]
    returned = [grid.along_seq(back, -k) for k in range(1, grid.seq)]
    backs = []
    for i in range(HALVES):
        backs.append(
            attend_back(i, *queries[i], kv, kf, rim, carry, *scaled[i][:2], masks, maps_q)
        )
        scaled, returned, backs = after((scaled, returned, backs))
    far_back = jnp.zeros(back.shape, F32)
    for w, v in zip(latter[1:], returned[1:]):
        far_back = far_back + w * v.astype(F32)
    near_back = far_back + latter[0] * returned[0].astype(F32)
    near_back, far_back = near_back.astype(BF16), far_back.astype(BF16)
    raw_query = [v[0] for v in backs]
    rim_back = [grid.along_seq(v[3], -1) for v in backs]
    raw_key, raw_value, dmap_key = [], [], []
    for i, (_, dkv, dkf, *_) in enumerate(backs):
        k, v, m = keys_back(
            i, kv, kf, dkv, dkf, rim_back[i], near_back, far_back, masks, maps_k
        )
        raw_key.append(k)
        raw_value.append(v)
        dmap_key.append(m)
    raw_key, out_terms = after((raw_key, out_terms))
    block_out = residual
    for term in out_terms:
        block_out = block_out + term.astype(F32)
    block_out = block_out.astype(BF16)
    dmap_query = jnp.concatenate([v[4] for v in backs], axis=0)
    dmap_key = jnp.concatenate(dmap_key, axis=0)
    dlogit = jnp.concatenate([v[5] for v in backs], axis=0)
    grad_tokens, grad_gain_one, grad_qkv_in, grad_qkv_out = inputs_back(
        w_qkv, [*raw_query, *raw_key, *raw_value], qkv_in, qkv_out, low, inputs,
        hidden, gain_first, grad_residual,
    )
    grad_logit = dlogit[:, :GROUPS, 0].reshape(HEADS) * (1.0 - gamma)
    grad_proj_in, grad_proj_out = grad_proj_in[:rank], grad_proj_out[:rank]

    blocks = lambda v: v.reshape(8, grid.seq, -1).swapaxes(0, 1)
    plain = lambda v: v.reshape(grid.seq, 8, -1)
    outs = (
        blocks(grad_qkv_out[:rank, :D]),
        blocks(grad_qkv_out[rank : 2 * rank, D : D + KVD]),
        blocks(grad_qkv_out[2 * rank : 3 * rank, D + KVD :]),
        blocks(grad_proj_out),
    )
    ins = [blocks(grad_qkv_in[i * rank : (i + 1) * rank]) for i in range(3)]
    ins.append(blocks(grad_proj_in))
    map_q = plain(dmap_query[:, :, :HEAD].reshape(HEADS, -1))
    map_k = dmap_key[:, :, :HEAD].reshape(KV_HEADS, grid.seq, -1).swapaxes(0, 1)
    logit = jnp.pad(grad_logit.reshape(grid.seq, -1, 1), ((0, 0), (0, 8 - HEADS // grid.seq), (0, 0)))
    sums = total_over_all(
        grid, [*outs, *ins, map_q, map_k, plain(grad_gain_one), plain(grad_gain_two), logit]
    )
    outs, ins, (map_q, map_k, gain_one, gain_two, logit) = sums[:4], sums[4:8], sums[8:]
    width = D // grid.seq
    return (
        block_out[None],
        grad_tokens[None],
        gain_one.reshape(width),
        gain_two.reshape(width),
        ins[0].T,
        outs[0],
        ins[1].T,
        outs[1],
        ins[2].T,
        outs[2],
        ins[3].T,
        outs[3],
        map_q.reshape(-1, HEAD, HEAD),
        map_k.reshape(KV_HEADS, -1, HEAD),
        logit[: HEADS // grid.seq, 0],
    )


def solution(mesh):
    placed = (
        P("rows", "seq", None),
        P("rows", "seq"),
        P("rows", "seq", None),
        P(),
        P(),
        P("rows", None),
        P("rows", None),
        P("rows", None),
        P("rows", None),
        P(None, None, "rows"),
        P("rows", None),
        P(),
        P(),
        P(),
        P(),
        P(),
        P(),
        P(),
        P(),
        P(),
        P(),
        P(),
    )
    return jax.shard_map(
        local,
        mesh=mesh,
        in_specs=placed,
        out_specs=(
            P("rows", "seq", None),
            P("rows", "seq", None),
            P("seq"),
            P("seq"),
            P("seq", None),
            P(None, "seq"),
            P("seq", None),
            P(None, "seq"),
            P("seq", None),
            P(None, "seq"),
            P("seq", None),
            P(None, "seq"),
            P("seq", None, None),
            P(None, "seq", None),
            P("seq"),
        ),
        check_vma=False,
    )
```

```python
import functools

import jax
import jax.numpy as jnp
from jax import lax
from jax.experimental import pallas as pl
from jax.experimental.pallas import tpu as pltpu
from jax.sharding import PartitionSpec as P

D = 2048
HEADS = 32
KV_HEADS = 8
HEAD = 64
WINDOW = 64
KVD = KV_HEADS * HEAD
GROUPS = HEADS // KV_HEADS
QKV = D + 2 * KVD
WIDE = GROUPS * HEAD
FEAT = 2 * HEAD
LOW = 128
STATE = 80
HALVES = 2
VMEM_LIMIT = 58 << 20
HALF = D // HALVES
PER_HALF = KV_HEADS // HALVES
SCALE = HEAD ** (-0.5)

EPSILON = 1e-05
THETA = 500000.0

Z_SIZE = 4
NEAR_BIT = 2
FAR_BIT = 1
CORES = 2
F32 = jnp.float32
BF16 = jnp.bfloat16


def dot_nn(a, b):
    return jnp.dot(a, b, preferred_element_type=F32)


def dot_nt(a, b):
    return lax.dot_general(a, b, (((1,), (1,)), ((), ())), preferred_element_type=F32)


def dot_tn(a, b):
    return lax.dot_general(a, b, (((0,), (0,)), ((), ())), preferred_element_type=F32)


def lane(shape):
    return lax.broadcasted_iota(jnp.int32, shape, 1)


def row(shape):
    return lax.broadcasted_iota(jnp.int32, shape, 0)


def low_half(shape):
    return lane(shape) % FEAT < HEAD


def turn(x, cosine, sine):
    width = x.shape[1]
    first = lane(x.shape) % HEAD < HEAD // 2
    swapped = jnp.where(
        first, pltpu.roll(x, width - HEAD // 2, 1), pltpu.roll(x, HEAD // 2, 1)
    )
    return x * cosine + swapped * sine


def halves_softmax(u):
    lo = low_half(u.shape)
    top = jnp.where(
        lo,
        jnp.max(jnp.where(lo, u, -jnp.inf), axis=1, keepdims=True),
        jnp.max(jnp.where(lo, -jnp.inf, u), axis=1, keepdims=True),
    )
    e = jnp.exp(u - top)
    total = jnp.where(
        lo,
        jnp.sum(jnp.where(lo, e, 0.0), axis=1, keepdims=True),
        jnp.sum(jnp.where(lo, 0.0, e), axis=1, keepdims=True),
    )
    return e / total


def halves_softmax_back(f, g):
    lo = low_half(f.shape)
    t = f * g
    total = jnp.where(
        lo,
        jnp.sum(jnp.where(lo, t, 0.0), axis=1, keepdims=True),
        jnp.sum(jnp.where(lo, 0.0, t), axis=1, keepdims=True),
    )
    v = f * (g - total)
    return v - pltpu.roll(v, HEAD, 1), t


def pair_features(x, maps):
    u = dot_nn(x, maps)
    return jnp.concatenate(
        [halves_softmax(u[:, :FEAT]), halves_softmax(u[:, FEAT:])], axis=1
    )


def same_head(size):
    shape = (GROUPS * size, WIDE)
    return (row(shape) // size == lane(shape) // HEAD).astype(F32)


def diagonal(tile, mask):
    wide = jnp.concatenate([tile, tile], axis=1)
    return (jnp.concatenate([wide] * GROUPS, axis=0) * mask).astype(BF16)


def diagonal_pair(tile):
    none = jnp.zeros_like(tile)
    return jnp.concatenate(
        [jnp.concatenate([tile, none], axis=1), jnp.concatenate([none, tile], axis=1)], axis=0
    )


def both_halves(kv):
    kv = kv.astype(F32)
    lo = low_half(kv.shape)
    other = pltpu.roll(kv, HEAD, 1)
    return jnp.where(lo, kv, other), jnp.where(lo, other, kv)


def fold_heads(r, mask):
    r = r * mask
    r = r[:64] + r[64:128] + r[128:192] + r[192:]
    r = r[:, :FEAT] + r[:, FEAT:]
    return r + pltpu.roll(r, HEAD, 1)


def fold_pair(r, size):
    return r[:size, :FEAT] + r[size:, FEAT:]


def whole(a):
    return pl.BlockSpec(a.shape, lambda *_: (0,) * len(a.shape))


ANYWHERE = pl.BlockSpec(memory_space=pl.ANY)
SCALARS = pl.BlockSpec(memory_space=pltpu.SMEM)


class Gathered:
    def __init__(self, blocks, places, size):
        self.blocks, self.places, self.size = blocks, places, size

    def shapes(self):
        return tuple(b.shape[0] // self.size for b in self.blocks)


def start_rows(places, refs, counts, size, target, sem, column=0):
    n = 0
    columns = slice(column, column + target.shape[1])
    for ref, count in zip(refs, counts):
        for i in range(count):
            to = pl.ds(pl.multiple_of(places[n] * size, size), size)
            part = ref.at[i * size : (i + 1) * size, columns]
            pltpu.make_async_copy(part, target.at[to], sem).start()
            n += 1


def wait_rows(target, sem):
    pltpu.make_async_copy(target, target, sem).wait()


def project_kv_kernel(*refs, counts, size):
    n = len(counts)
    places_ref, blocks = refs[0], refs[1 : 1 + n]
    x_ref, low_ref, p_ref, cos_ref, sin_ref, maps_ref, survive_ref = refs[1 + n : 8 + n]
    kv_ref, kf_ref, pack_ref, full_ref, w_ref, sem = refs[8 + n :]
    length = x_ref.shape[0]
    start_rows(places_ref, blocks, counts, size, w_ref, sem, D)
    wait_rows(w_ref, sem)
    survive = survive_ref[...]
    lo = low_half((length, FEAT))
    cut = length - WINDOW
    steps = KVD // WIDE
    part = lambda j: slice(j * WIDE, (j + 1) * WIDE)
    for i in range(steps):
        raw_k, raw_v = (
            dot_nn(x_ref[...], w_ref[:, part(j)]) + dot_nn(low_ref[...], p_ref[:, part(j)])
            for j in (i, steps + i)
        )
        keys = turn(raw_k, cos_ref[...], sin_ref[...]).astype(BF16)
        values = raw_v.astype(BF16).astype(F32)
        for p in range(WIDE // FEAT):
            at = (i * GROUPS + 2 * p) * FEAT
            k2 = keys[:, p * FEAT : (p + 1) * FEAT]
            v2 = values[:, p * FEAT : (p + 1) * FEAT]
            feats = pair_features(k2, maps_ref[2 * i + p])
            kf_ref[:, at : at + 2 * FEAT] = feats.astype(BF16)
            k2 = k2.astype(F32)
            k_other, v_other = pltpu.roll(k2, HEAD, 1), pltpu.roll(v2, HEAD, 1)
            ones = jnp.where(lane((length, FEAT)) < HEAD + 8, 1.0, 0.0)
            for h, kv, v in (
                (0, jnp.where(lo, k2, v_other), v2),
                (1, jnp.where(lo, k_other, v2), v_other),
            ):
                at_h = at + h * FEAT
                kv_ref[:, at_h : at_h + FEAT] = kv.astype(BF16)
                v_one = jnp.where(lo, v, ones).astype(BF16)
                kept = (feats[:, h * FEAT : (h + 1) * FEAT].astype(BF16).astype(F32) * survive)
                kept = kept.astype(BF16)
                head = dot_tn(v_one[:cut], kept[:cut])
                tail = dot_tn(v_one[cut:], kept[cut:])
                at_h = slice(at_h, at_h + FEAT)
                pack_ref[2 * WINDOW :, at_h] = head[:STATE].astype(BF16)
                full_ref[:, at_h] = (head + tail)[:STATE].astype(BF16)
    pack_ref[:WINDOW, :] = kv_ref[cut:, :]
    pack_ref[WINDOW : 2 * WINDOW, :] = kf_ref[cut:, :]


def project_kv(w, x, low, p, cosine, sine, maps, survive):
    length = x.shape[0]
    shapes = (
        jax.ShapeDtypeStruct((length, KV_HEADS * FEAT), BF16),
        jax.ShapeDtypeStruct((length, KV_HEADS * FEAT), BF16),
        jax.ShapeDtypeStruct((2 * WINDOW + STATE, KV_HEADS * FEAT), BF16),
        jax.ShapeDtypeStruct((STATE, KV_HEADS * FEAT), BF16),
    )
    rest = (x, low, p, cosine, sine, maps, survive)
    return pl.pallas_call(
        functools.partial(project_kv_kernel, counts=w.shapes(), size=w.size),
        grid=(1,),
        in_specs=[SCALARS] + [ANYWHERE] * len(w.blocks) + [whole(a) for a in rest],
        out_specs=[whole(v) for v in shapes],
        out_shape=shapes,
        scratch_shapes=[pltpu.VMEM((D, 2 * KVD), BF16), pltpu.SemaphoreType.DMA],
        compiler_params=pltpu.CompilerParams(vmem_limit_bytes=VMEM_LIMIT),
        cost_estimate=pl.CostEstimate(
            flops=4 * length * D * KVD, bytes_accessed=4 * D * KVD, transcendentals=0
        ),
        name="project_kv",
    )(w.places, *w.blocks, *rest)


def project_q_kernel(*refs, counts, size, column):
    n = len(counts)
    places_ref, blocks = refs[0], refs[1 : 1 + n]
    x_ref, low_ref, p_ref, cos_ref, sin_ref, maps_ref = refs[1 + n : 7 + n]
    q_ref, qf_ref, w_ref, sem = refs[-4:]
    step = pl.program_id(0)

    @pl.when(step == 0)
    def _():
        start_rows(places_ref, blocks, counts, size, w_ref, sem, column)
        wait_rows(w_ref, sem)

    at = pl.ds(pl.multiple_of(step * WIDE, WIDE), WIDE)
    raw = dot_nn(x_ref[...], w_ref[:, at]) + dot_nn(low_ref[...], p_ref[...])
    q = turn(raw, cos_ref[...], sin_ref[...]).astype(BF16)
    q_ref[...] = q
    for p in range(WIDE // FEAT):
        feats = pair_features(q[:, p * FEAT : (p + 1) * FEAT], maps_ref[p])
        qf_ref[:, 2 * p * FEAT : 2 * (p + 1) * FEAT] = feats.astype(BF16)


def project_q(half, w, x, low, p, cosine, sine, maps, former=()):
    length = x.shape[0]
    first = half * PER_HALF
    pairs = WIDE // FEAT
    arrays = (w.places, *w.blocks, x, low, p, cosine, sine, maps, *former)
    return pl.pallas_call(
        functools.partial(
            project_q_kernel, counts=w.shapes(), size=w.size, column=half * HALF
        ),
        grid=(HALF // WIDE,),
        in_specs=[SCALARS] + [ANYWHERE] * len(w.blocks) + [
            whole(x), whole(low),
            pl.BlockSpec((LOW, WIDE), lambda g: (0, first + g)),
            whole(cosine), whole(sine),
            pl.BlockSpec((pairs, FEAT, 2 * FEAT), lambda g: (first + g, 0, 0)),
        ] + [ANYWHERE] * len(former),
        out_specs=[
            pl.BlockSpec((length, WIDE), lambda g: (0, first + g)),
            pl.BlockSpec((length, 2 * WIDE), lambda g: (0, first + g)),
        ],
        out_shape=[
            jax.ShapeDtypeStruct((length, D), BF16),
            jax.ShapeDtypeStruct((length, 2 * D), BF16),
        ],
        input_output_aliases={len(arrays) - len(former) + i: i for i in range(len(former))},
        scratch_shapes=[pltpu.VMEM((D, HALF), BF16), pltpu.SemaphoreType.DMA],
        compiler_params=pltpu.CompilerParams(vmem_limit_bytes=VMEM_LIMIT),
        cost_estimate=pl.CostEstimate(
            flops=2 * length * D * HALF, bytes_accessed=2 * D * HALF, transcendentals=0
        ),
        name="project_q",
    )(*arrays)


def key_tiles(kv_ref, kf_ref, rim_kv_ref, rim_kf_ref, mask):
    tiles = []
    for t in range(1 + kv_ref.shape[0] // WINDOW):
        if t == 0:
            kv, kf = rim_kv_ref[...], rim_kf_ref[...]
        else:
            at = (t - 1) * WINDOW
            kv, kf = kv_ref[at : at + WINDOW, :], kf_ref[at : at + WINDOW, :]
        kk, vv = both_halves(kv)
        tiles.append((diagonal(kk, mask * SCALE), diagonal(vv, mask), diagonal_pair(kf)))
    return tiles


def spans(t, length):
    edge = lambda v: min(max(v, 0), length)
    a, b, c = edge((t - 1) * WINDOW), edge(t * WINDOW), edge((t + 1) * WINDOW)
    return (a, b), (b, c), (c, length)


def weights_of(t, tile, q_ref, qf_ref, same, upper, gamma):
    length = q_ref.shape[0]
    (a, b), (_, c), _ = spans(t, length)
    e = jnp.exp(dot_nt(q_ref[a:c, :], tile[0]))
    linear = None
    if b < length:
        linear = gamma * jnp.concatenate(
            [
                dot_nt(qf_ref[b:, 2 * p * FEAT : 2 * (p + 1) * FEAT], tile[2])
                for p in range(GROUPS // 2)
            ],
            axis=1,
        )
    parts = []
    if b > a:
        parts.append(jnp.where(same(a, b) & upper, e[: b - a], 0.0))
    if c > b:
        mixed = jnp.where(upper, linear[: c - b], e[b - a :])
        parts.append(jnp.where(same(b, c), mixed, 0.0))
    if length > c:
        parts.append(jnp.where(same(c, length), linear[c - b :], 0.0))
    return e, jnp.concatenate(parts, axis=0).astype(BF16)


def carried(carry_ref):
    state = carry_ref[...]
    ones = jnp.zeros((HEAD, FEAT), BF16) + state[HEAD : HEAD + 1, :]
    return diagonal_pair(state[:HEAD, :]), diagonal_pair(ones)


def attend_kernel(
    q_ref, qf_ref, kv_ref, kf_ref, rim_kv_ref, rim_kf_ref, carry_ref,
    qdoc_ref, kdoc_ref, fresh_ref, gamma_ref, *refs,
):
    out_ref, att_ref, inv_ref, num_ref, den_ref = refs[-5:]
    length = q_ref.shape[0]
    mask = same_head(WINDOW)
    ones = mask.astype(BF16)
    gamma = gamma_ref[...]
    shape = (WINDOW, WIDE)
    upper = row(shape) >= lane(shape) % HEAD
    state, state_sum = carried(carry_ref)
    fresh = fresh_ref[...] * gamma
    for p in range(GROUPS // 2):
        feats = qf_ref[:, 2 * p * FEAT : 2 * (p + 1) * FEAT]
        at = slice(p * FEAT, (p + 1) * FEAT)
        num_ref[:, at] = dot_nt(feats, state) * fresh[:, at]
        den_ref[:, at] = dot_nt(feats, state_sum) * fresh[:, at]
    for t, tile in enumerate(key_tiles(kv_ref, kf_ref, rim_kv_ref, rim_kf_ref, mask)):
        a = spans(t, length)[0][0]
        same = lambda i, j, t=t: qdoc_ref[i:j, :] == kdoc_ref[t : t + 1, :]
        _, w = weights_of(t, tile, q_ref, qf_ref, same, upper, gamma)
        num_ref[a:, :] += dot_nn(w, tile[1])
        den_ref[a:, :] += dot_nn(w, ones)
    inv = 1.0 / den_ref[...]
    att = num_ref[...] * inv
    inv_ref[...] = inv
    att_ref[...] = att
    out_ref[...] = att.astype(BF16)


def group_specs(length, first=0):
    column = lambda rows, width: pl.BlockSpec((rows, width), lambda g: (0, first + g))
    fixed = lambda rows, width: pl.BlockSpec((rows, width), lambda g: (0, 0))
    return dict(
        q=column(length, WIDE),
        qf=column(length, 2 * WIDE),
        k=column(length, FEAT),
        rim_kv=column(WINDOW, FEAT),
        rim_kf=pl.BlockSpec((WINDOW, FEAT), lambda g: (1, first + g)),
        state=column(STATE, FEAT),
        qdoc=fixed(length, 1),
        kdoc=fixed(8, WIDE),
        gamma=column(1, WIDE),
        wide=fixed(length, WIDE),
        maps=pl.BlockSpec((GROUPS // 2, FEAT, 2 * FEAT), lambda g: (first + g, 0, 0)),
    )


def attend(half, q, qf, kv, kf, rim, carry, masks, former=()):
    length = q.shape[0]
    s = group_specs(length, half * PER_HALF)
    arrays = (
        q, qf, kv, kf, rim, rim, carry,
        masks["qdoc"], masks["kdoc"], masks["fresh"], masks["gamma"], *former,
    )
    return pl.pallas_call(
        attend_kernel,
        grid=(PER_HALF,),
        in_specs=[
            s["q"], s["qf"], s["k"], s["k"], s["rim_kv"], s["rim_kf"], s["state"],
            s["qdoc"], s["kdoc"], s["qdoc"], s["gamma"],
        ] + [ANYWHERE] * len(former),
        out_specs=[s["q"]] * 3,
        out_shape=[
            jax.ShapeDtypeStruct((length, D), BF16),
            jax.ShapeDtypeStruct((length, D), F32),
            jax.ShapeDtypeStruct((length, D), F32),
        ],
        input_output_aliases={len(arrays) - len(former) + i: i for i in range(len(former))},
        scratch_shapes=[pltpu.VMEM((length, WIDE), F32)] * 2,
        compiler_params=pltpu.CompilerParams(vmem_limit_bytes=VMEM_LIMIT),
        cost_estimate=pl.CostEstimate(
            flops=5_000_000_000, bytes_accessed=8 * length * D, transcendentals=0
        ),
        name="attend",
    )(*arrays)


def scaled_grads_kernel(
    ga_ref, att_ref, inv_ref, qf_ref, fresh_ref, gamma_ref, g_ref, gd_ref, back_ref
):
    mask = same_head(HEAD)
    ga = ga_ref[...].astype(F32)
    inv = inv_ref[...]
    product = ga * att_ref[...]
    high = product.astype(BF16)
    rest = (product - high.astype(F32)).astype(BF16)
    ones = mask.astype(BF16)
    gd = -(dot_nn(high, ones) + dot_nn(rest, ones)) * inv
    g = ga * inv
    g_ref[...] = g.astype(BF16)
    gd_ref[...] = gd
    fresh = fresh_ref[...] * gamma_ref[...]
    fresh_g = (g * fresh).astype(BF16)
    fresh_gd = (gd * fresh).astype(BF16)
    kv = sums = 0.0
    for p in range(GROUPS // 2):
        feats = qf_ref[:, 2 * p * FEAT : 2 * (p + 1) * FEAT]
        at = slice(p * FEAT, (p + 1) * FEAT)
        kv += fold_pair(dot_tn(fresh_g[:, at], feats), HEAD)
        sums += fold_pair(dot_tn(fresh_gd[:, at], feats), HEAD)
    back_ref[:HEAD, :] = kv.astype(BF16)
    back_ref[HEAD:, :] = sums[: STATE - HEAD].astype(BF16)


def scaled_grads(ga, att, inv, qf, masks):
    length = ga.shape[0]
    s = group_specs(length)
    return pl.pallas_call(
        scaled_grads_kernel,
        grid=(KV_HEADS,),
        in_specs=[s["q"], s["q"], s["q"], s["qf"], s["qdoc"], s["gamma"]],
        out_specs=[s["q"], s["q"], s["state"]],
        out_shape=[
            jax.ShapeDtypeStruct((length, D), BF16),
            jax.ShapeDtypeStruct((length, D), F32),
            jax.ShapeDtypeStruct((STATE, KV_HEADS * FEAT), BF16),
        ],
        compiler_params=pltpu.CompilerParams(vmem_limit_bytes=VMEM_LIMIT),
        name="scaled_grads",
    )(ga, att, inv, qf, masks["fresh"], masks["gamma"])


def attend_back_kernel(
    q_ref, qf_ref, kv_ref, kf_ref, rim_kv_ref, rim_kf_ref, carry_ref, g_ref, gd_ref,
    qdoc_ref, kdoc_ref, fresh_ref, gamma_ref, maps_ref, cos_ref, sin_ref,
    raw_ref, dkv_ref, dkf_ref, rim_ref, dmap_ref, logit_ref, dq_ref, dqf_ref,
):
    length = q_ref.shape[0]
    mask = same_head(WINDOW)
    gamma = gamma_ref[...]
    shape = (WINDOW, WIDE)
    upper = row(shape) >= lane(shape) % HEAD
    state, state_sum = carried(carry_ref)
    fresh = fresh_ref[...] * gamma
    pairs = range(GROUPS // 2)
    half = lambda p: slice(p * FEAT, (p + 1) * FEAT)
    full = lambda p: slice(2 * p * FEAT, 2 * (p + 1) * FEAT)
    fresh_g = (g_ref[...].astype(F32) * fresh).astype(BF16)
    fresh_gd = (gd_ref[...] * fresh * (1.0 / HEAD)).astype(BF16)
    for p in pairs:
        dqf_ref[:, full(p)] = dot_nn(fresh_g[:, half(p)], state) + dot_nn(
            fresh_gd[:, half(p)], state_sum
        )
    dq_ref[...] = jnp.zeros_like(dq_ref)
    lo = low_half((WINDOW, FEAT))
    for t, tile in enumerate(key_tiles(kv_ref, kf_ref, rim_kv_ref, rim_kf_ref, mask)):
        (a, b), (_, c), _ = spans(t, length)
        same = lambda i, j, t=t: qdoc_ref[i:j, :] == kdoc_ref[t : t + 1, :]
        e, w = weights_of(t, tile, q_ref, qf_ref, same, upper, gamma)
        g = g_ref[a:, :]
        x = dot_nt(g, tile[1]) + gd_ref[a:, :]
        near = x[: c - a] * e
        parts = []
        if b > a:
            parts.append(jnp.where(same(a, b) & upper, near[: b - a], 0.0))
        if c > b:
            parts.append(jnp.where(same(b, c), jnp.where(upper, 0.0, near[b - a :]), 0.0))
        ds = jnp.concatenate(parts, axis=0).astype(BF16)
        dq_ref[a:c, :] += dot_nn(ds, tile[0])
        dk = fold_heads(dot_tn(ds, q_ref[a:c, :]), mask) * SCALE
        dv = fold_heads(dot_tn(w, g), mask)
        at = slice((t - 1) * WINDOW, t * WINDOW)
        dkv = jnp.where(lo, dk, dv)
        if t:
            dkv_ref[at, :] = dkv
        else:
            rim_ref[:WINDOW, :] = dkv.astype(BF16)
        if b < length:
            far = x[b - a :] * gamma
            parts = [jnp.where(same(b, c) & upper, far[: c - b], 0.0)]
            if c < length:
                parts.append(jnp.where(same(c, length), far[c - b :], 0.0))
            dl = jnp.concatenate(parts, axis=0).astype(BF16)
            dkf = 0.0
            for p in pairs:
                dqf_ref[b:, full(p)] += dot_nn(dl[:, half(p)], tile[2])
                dkf += fold_pair(dot_tn(dl[:, half(p)], qf_ref[b:, full(p)]), HEAD)
            if t:
                dkf_ref[at, :] = dkf
            else:
                rim_ref[WINDOW:, :] = dkf.astype(BF16)
        else:
            dkf_ref[at, :] = jnp.zeros((WINDOW, FEAT), F32)
    for p in pairs:
        grads = []
        for h in (2 * p, 2 * p + 1):
            f = qf_ref[:, h * FEAT : (h + 1) * FEAT].astype(F32)
            gu, t = halves_softmax_back(f, dqf_ref[:, h * FEAT : (h + 1) * FEAT])
            grads.append(gu.astype(BF16))
            total = jnp.sum(jnp.sum(t, axis=0, keepdims=True), axis=1, keepdims=True)
            logit_ref[0, h : h + 1, :] = jnp.zeros((1, FEAT), F32) + total
        gu = jnp.concatenate(grads, axis=1)
        dq_ref[:, half(p)] += 0.5 * dot_nt(gu, maps_ref[p])
        dmap = dot_tn(q_ref[:, half(p)], gu)
        dmap_ref[2 * p] = dmap[:HEAD, :FEAT]
        dmap_ref[2 * p + 1] = dmap[HEAD:, FEAT:]
    raw_ref[...] = turn(dq_ref[...], cos_ref[...], -sin_ref[...]).astype(BF16)


def attend_back(q, qf, kv, kf, rim, carry, g, gd, masks, maps):
    length = q.shape[0]
    s = group_specs(length)
    column = lambda rows: pl.BlockSpec((rows, FEAT), lambda g: (0, g))
    return pl.pallas_call(
        attend_back_kernel,
        grid=(KV_HEADS,),
        in_specs=[
            s["q"], s["qf"], s["k"], s["k"], s["rim_kv"], s["rim_kf"], s["state"], s["q"], s["q"],
            s["qdoc"], s["kdoc"], s["qdoc"], s["gamma"], s["maps"], s["wide"], s["wide"],
        ],
        out_specs=[
            s["q"], column(length), column(length), column(2 * WINDOW),
            pl.BlockSpec((GROUPS, HEAD, FEAT), lambda g: (g, 0, 0)),
            pl.BlockSpec((1, 8, FEAT), lambda g: (g, 0, 0)),
        ],
        out_shape=[
            jax.ShapeDtypeStruct((length, D), BF16),
            jax.ShapeDtypeStruct((length, KV_HEADS * FEAT), F32),
            jax.ShapeDtypeStruct((length, KV_HEADS * FEAT), F32),
            jax.ShapeDtypeStruct((2 * WINDOW, KV_HEADS * FEAT), BF16),
            jax.ShapeDtypeStruct((HEADS, HEAD, FEAT), F32),
            jax.ShapeDtypeStruct((KV_HEADS, 8, FEAT), F32),
        ],
        scratch_shapes=[pltpu.VMEM((length, WIDE), F32), pltpu.VMEM((length, 2 * WIDE), F32)],
        compiler_params=pltpu.CompilerParams(vmem_limit_bytes=VMEM_LIMIT),
        cost_estimate=pl.CostEstimate(
            flops=15_000_000_000, bytes_accessed=8 * length * D, transcendentals=0
        ),
        name="attend_back",
    )(
        q, qf, kv, kf, rim, rim, carry, g, gd,
        masks["qdoc"], masks["kdoc"], masks["fresh"], masks["gamma"],
        maps, masks["cos"], masks["sin"],
    )


def keys_back_kernel(
    kv_ref, kf_ref, dkv_ref, dkf_ref, rim_kv_ref, rim_kf_ref, near_ref, far_ref, survive_ref,
    maps_ref, cos_ref, sin_ref, rk_ref, rv_ref, dmap_ref,
):
    length = kv_ref.shape[0]
    cut = length - WINDOW
    lo = low_half((length, FEAT))
    survive = survive_ref[...]
    dkv, grads = [], []
    for h in range(2):
        at = slice(h * FEAT, (h + 1) * FEAT)
        kv = kv_ref[:, at].astype(F32)
        kf = kf_ref[:, at]
        v_low = pltpu.roll(kv, HEAD, 1)
        ones = jnp.where(lane((length, FEAT)) == HEAD, 1.0, 0.0)
        v_one = jnp.where(lo, v_low, ones).astype(BF16)[:, :STATE]
        dkf, dv = [], []
        for back, part in ((near_ref, slice(0, cut)), (far_ref, slice(cut, length))):
            state = back[:, at]
            twice = jnp.concatenate([state[:HEAD], state[:HEAD]], axis=0)
            dkf.append(dot_nn(v_one[part], state))
            dv.append(dot_nt(kf[part], twice))
        rim = jnp.zeros((cut, FEAT), F32)
        dkf = (
            jnp.concatenate(dkf, axis=0) * survive
            + dkf_ref[:, at]
            + jnp.concatenate([rim, rim_kf_ref[:, at].astype(F32)], axis=0)
        )
        dv = jnp.concatenate(dv, axis=0) * survive
        total = (
            dkv_ref[:, at]
            + jnp.concatenate([rim, rim_kv_ref[:, at].astype(F32)], axis=0)
            + jnp.where(lo, 0.0, dv)
        )
        gu, _ = halves_softmax_back(kf.astype(F32), dkf)
        grads.append(gu.astype(BF16))
        dkv.append(total)
    gu = jnp.concatenate(grads, axis=1)
    keys = jnp.where(lo, kv_ref[:, :FEAT].astype(F32), pltpu.roll(kv_ref[:, FEAT:].astype(F32), HEAD, 1))
    dmap = dot_tn(keys.astype(BF16), gu)
    dmap_ref[0] = dmap[:HEAD, :FEAT]
    dmap_ref[1] = dmap[HEAD:, FEAT:]
    dk = jnp.where(lo, dkv[0], pltpu.roll(dkv[1], HEAD, 1)) + 0.5 * dot_nt(gu, maps_ref[0])
    rk_ref[...] = turn(dk, cos_ref[...], -sin_ref[...]).astype(BF16)
    rv_ref[...] = jnp.where(lo, pltpu.roll(dkv[0], HEAD, 1), dkv[1]).astype(BF16)


def keys_back(kv, kf, dkv, dkf, rim, near, far, masks, maps):
    length = kv.shape[0]
    pairs = KV_HEADS // 2
    column = lambda rows: pl.BlockSpec((rows, 2 * FEAT), lambda g: (0, g))
    state = pl.BlockSpec((STATE, 2 * FEAT), lambda g: (0, g))
    narrow = pl.BlockSpec((length, FEAT), lambda g: (0, 0))
    out = pl.BlockSpec((length, FEAT), lambda g: (0, g))
    return pl.pallas_call(
        keys_back_kernel,
        grid=(pairs,),
        in_specs=[
            column(length), column(length), column(length), column(length),
            column(WINDOW), pl.BlockSpec((WINDOW, 2 * FEAT), lambda g: (1, g)),
            state, state, pl.BlockSpec((length, 1), lambda g: (0, 0)),
            pl.BlockSpec((1, FEAT, 2 * FEAT), lambda g: (g, 0, 0)), narrow, narrow,
        ],
        out_specs=[out, out, pl.BlockSpec((2, HEAD, FEAT), lambda g: (g, 0, 0))],
        out_shape=[
            jax.ShapeDtypeStruct((length, KVD), BF16),
            jax.ShapeDtypeStruct((length, KVD), BF16),
            jax.ShapeDtypeStruct((KV_HEADS, HEAD, FEAT), F32),
        ],
        compiler_params=pltpu.CompilerParams(vmem_limit_bytes=VMEM_LIMIT),
        name="keys_back",
    )(
        kv, kf, dkv, dkf, rim, rim, near, far, masks["survive"], maps, masks["cos"], masks["sin"]
    )


def out_project_kernel(*refs, counts, size):
    n = len(counts)
    places, blocks, refs = refs[0], refs[1 : 1 + n], refs[1 + n :]
    m, hidden, proj_in, proj_out, gain = refs[:5]
    residual, second, low, inverse, w, sem = refs[5:]
    start_rows(places, blocks, counts, size, w, sem)
    reduced = dot_nn(m[...], proj_in[...]).astype(BF16)
    low[...] = reduced
    wait_rows(w, sem)
    squares = 0.0
    for j in range(D // WIDE):
        at = slice(j * WIDE, (j + 1) * WIDE)
        sums = (
            hidden[:, at].astype(F32)
            + dot_nn(m[...], w[:, at])
            + dot_nn(reduced, proj_out[:, at])
        )
        residual[:, at] = sums
        squares = squares + jnp.sum(sums * sums, axis=1, keepdims=True)
    inv = lax.rsqrt(squares * (1.0 / D) + EPSILON)
    inverse[...] = jnp.zeros(inverse.shape, F32) + inv
    second[...] = (residual[...] * inv * gain[...]).astype(BF16)


def out_project(w, merged, hidden, proj_in, proj_out, gain):
    length = hidden.shape[0]
    shapes = (
        jax.ShapeDtypeStruct((length, D), F32),
        jax.ShapeDtypeStruct((length, D), BF16),
        jax.ShapeDtypeStruct((length, LOW), BF16),
        jax.ShapeDtypeStruct((length, LOW), F32),
    )
    rest = (merged, hidden, proj_in, proj_out, gain)
    return pl.pallas_call(
        functools.partial(out_project_kernel, counts=w.shapes(), size=w.size),
        grid=(1,),
        in_specs=[SCALARS] + [ANYWHERE] * len(w.blocks) + [whole(a) for a in rest],
        out_specs=[whole(v) for v in shapes],
        out_shape=shapes,
        scratch_shapes=[pltpu.VMEM((D, D), BF16), pltpu.SemaphoreType.DMA],
        compiler_params=pltpu.CompilerParams(vmem_limit_bytes=VMEM_LIMIT),
        cost_estimate=pl.CostEstimate(
            flops=2 * length * D * D, bytes_accessed=2 * D * D, transcendentals=0
        ),
        name="out_project",
    )(w.places, *w.blocks, *rest)


def branch_back_kernel(*refs, counts, size, extra):
    n = len(counts)
    places, blocks, refs = refs[0], refs[1 : 1 + n], refs[1 + n :]
    sums, refs = refs[:extra], refs[extra:]
    cot, residual, inverse, gain, proj_in, proj_out, m, low = refs[:8]
    grad_residual, back_ref, grad_gain, grad_in, grad_out, w, sem = refs[8:]
    start_rows(places, blocks, counts, size, w, sem)
    total = sums[0][...].astype(F32)
    for v in sums[1:]:
        total = total + v[...].astype(F32)
    inv = inverse[:, :1]
    normed = residual[...] * inv
    product = total * normed
    grad_gain[...] = jnp.sum(product, axis=0, keepdims=True)
    scaled = total * gain[...]
    mean = jnp.sum(scaled * normed, axis=1, keepdims=True) * (1.0 / D)
    grad = cot[...].astype(F32) + inv * (scaled - normed * mean)
    grad_residual[...] = grad
    branch = grad.astype(BF16)
    grad_low = dot_nt(branch, proj_out[...]).astype(BF16)
    grad_out[...] = dot_tn(low[...], branch)
    grad_in[...] = dot_tn(grad_low, m[...])
    wait_rows(w, sem)
    for j in range(D // WIDE):
        at = slice(j * WIDE, (j + 1) * WIDE)
        back = dot_nt(grad_low, proj_in[at, :]) + dot_nt(branch, w[at, :])
        back_ref[:, at] = back.astype(BF16)


def branch_back(w, sums, cot, residual, inverse, gain, proj_in, proj_out, merged, low):
    length = cot.shape[0]
    shapes = (
        jax.ShapeDtypeStruct((length, D), F32),
        jax.ShapeDtypeStruct((length, D), BF16),
        jax.ShapeDtypeStruct((1, D), F32),
        jax.ShapeDtypeStruct((LOW, D), F32),
        jax.ShapeDtypeStruct((LOW, D), F32),
    )
    rest = (*sums, cot, residual, inverse, gain, proj_in, proj_out, merged, low)
    return pl.pallas_call(
        functools.partial(
            branch_back_kernel, counts=w.shapes(), size=w.size, extra=len(sums)
        ),
        grid=(1,),
        in_specs=[SCALARS] + [ANYWHERE] * len(w.blocks) + [whole(a) for a in rest],
        out_specs=[whole(v) for v in shapes],
        out_shape=shapes,
        scratch_shapes=[pltpu.VMEM((D, D), BF16), pltpu.SemaphoreType.DMA],
        compiler_params=pltpu.CompilerParams(vmem_limit_bytes=VMEM_LIMIT),
        cost_estimate=pl.CostEstimate(
            flops=2 * length * D * D, bytes_accessed=2 * D * D, transcendentals=0
        ),
        name="branch_back",
    )(w.places, *w.blocks, *rest)


def inputs_back_kernel(*refs, counts, size):
    n = len(counts)
    places, blocks, refs = refs[0], refs[1 : 1 + n], refs[1 + n :]
    raws, refs = refs[:3], refs[3:]
    p_in, p_out, low, x, hidden, gain, grad_residual = refs[:7]
    grad_tokens, grad_gain, grad_in, grad_out, w, raw, back, sem = refs[7:]
    start_rows(places, blocks, counts, size, w, sem)
    at = 0
    for r in raws:
        raw[:, at : at + r.shape[1]] = r[...]
        at += r.shape[1]
    grad_low = dot_nt(raw[...], p_out[...]).astype(BF16)
    grad_out[...] = dot_tn(low[...], raw[...])
    grad_in[...] = dot_tn(grad_low, x[...])
    wait_rows(w, sem)
    values = hidden[...].astype(F32)
    inv = lax.rsqrt(jnp.sum(values * values, axis=1, keepdims=True) * (1.0 / D) + EPSILON)
    mean = 0.0
    for j in range(D // WIDE):
        at = slice(j * WIDE, (j + 1) * WIDE)
        part = dot_nt(grad_low, p_in[at, :]) + dot_nt(raw[...], w[at, :])
        normed = hidden[:, at].astype(F32) * inv
        product = part * normed
        grad_gain[:, at] = jnp.sum(product, axis=0, keepdims=True)
        mean = mean + jnp.sum(product * gain[:, at], axis=1, keepdims=True)
        back[:, at] = part
    mean = mean * (1.0 / D)
    grad_tokens[...] = grad_residual[...] + inv * (
        back[...] * gain[...] - values * inv * mean
    )


def inputs_back(w, raws, p_in, p_out, low, x, hidden, gain, grad_residual):
    length = x.shape[0]
    shapes = (
        jax.ShapeDtypeStruct((length, D), F32),
        jax.ShapeDtypeStruct((1, D), F32),
        jax.ShapeDtypeStruct((LOW, D), F32),
        jax.ShapeDtypeStruct((LOW, QKV), F32),
    )
    rest = (*raws, p_in, p_out, low, x, hidden, gain, grad_residual)
    return pl.pallas_call(
        functools.partial(inputs_back_kernel, counts=w.shapes(), size=w.size),
        grid=(1,),
        in_specs=[SCALARS] + [ANYWHERE] * len(w.blocks) + [whole(a) for a in rest],
        out_specs=[whole(v) for v in shapes],
        out_shape=shapes,
        scratch_shapes=[
            pltpu.VMEM((D, QKV), BF16),
            pltpu.VMEM((length, QKV), BF16),
            pltpu.VMEM((length, D), F32),
            pltpu.SemaphoreType.DMA,
        ],
        compiler_params=pltpu.CompilerParams(vmem_limit_bytes=VMEM_LIMIT),
        cost_estimate=pl.CostEstimate(
            flops=2 * length * D * QKV, bytes_accessed=2 * D * QKV, transcendentals=0
        ),
        name="inputs_back",
    )(w.places, *w.blocks, *rest)


def mlp_kernel(place_ref, *refs, rows, paired, tile, own, carried_in):
    n = len(rows[0]) + len(rows[1])
    tokens, refs = refs[:n], refs[n:]
    own_gu, own_dn = refs[:2]
    pair, refs = (refs[2], refs[3:]) if paired else (None, refs[2:])
    sums, refs = (refs[:2], refs[2:]) if carried_in else (None, refs)
    out_ref, back_ref, h, c, gu, dn, out, back, row_sem, gu_sem, dn_sem = refs
    step, steps = pl.program_id(0), pl.num_programs(0)
    own_tiles = own_gu.shape[2] // tile if own else 0

    def fetch(n, slot):
        @pl.when(n < own_tiles)
        def _():
            at = pl.ds(pl.multiple_of(n * tile, tile), tile)
            pltpu.make_async_copy(own_gu.at[:, :, at], gu.at[slot], gu_sem.at[slot]).start()
            pltpu.make_async_copy(own_dn.at[at, :], dn.at[slot], dn_sem.at[slot]).start()

        if not paired:
            return

        @pl.when(n >= own_tiles)
        def _():
            first = (n - own_tiles) * tile
            at = pl.ds(pl.multiple_of(first, tile), tile)
            width = pair.shape[1] // 3
            row = pl.ds(pl.multiple_of(2 * width + first % width, tile), tile)
            column = pl.ds(pl.multiple_of(first // width * width, width), width)
            for k in range(D // width):
                part = pair.at[2 * k + place_ref[0]]
                there = slice(k * width, (k + 1) * width)
                for i in range(2):
                    pltpu.make_async_copy(
                        part.at[i * width : (i + 1) * width, at],
                        gu.at[slot, i, there, :],
                        gu_sem.at[slot],
                    ).start()
                pltpu.make_async_copy(
                    part.at[row, column], dn.at[slot, :, there], dn_sem.at[slot]
                ).start()

    @pl.when(step == 0)
    def _():
        fetch(step, 0)
        copies = []
        for target, sizes in zip((h, c), rows):
            at = 0
            for size in sizes:
                i = len(copies)
                there = target.at[at : at + size]
                copies.append(pltpu.make_async_copy(tokens[i], there, row_sem.at[i]))
                at += size
        for copy in copies:
            copy.start()
        if carried_in:
            for i, target in enumerate((out, back)):
                copies.append(pltpu.make_async_copy(sums[i], target, row_sem.at[len(copies)]))
                copies[-1].start()
        else:
            out[...] = jnp.zeros_like(out)
            back[...] = jnp.zeros_like(back)
        for copy in copies:
            copy.wait()

    slot = step % 2

    @pl.when(step + 1 < steps)
    def _():
        fetch(step + 1, 1 - slot)

    pltpu.make_async_copy(own_gu.at[:, :, pl.ds(0, tile)], gu.at[slot], gu_sem.at[slot]).wait()
    pltpu.make_async_copy(own_dn.at[pl.ds(0, tile), :], dn.at[slot], dn_sem.at[slot]).wait()
    w_gate, w_up, w_down = gu.at[slot, 0], gu.at[slot, 1], dn.at[slot]
    gate = dot_nn(h[...], w_gate[...])
    up = dot_nn(h[...], w_up[...])
    grad = dot_nt(c[...], w_down[...])
    sig = jax.nn.sigmoid(gate)
    silu = gate * sig
    act = (silu * up).astype(BF16)
    grad_gate = (grad * up * sig * (1.0 + gate * (1.0 - sig))).astype(BF16)
    grad_up = (grad * silu).astype(BF16)
    out[...] += dot_nn(act, w_down[...])
    back[...] += dot_nt(grad_gate, w_gate[...]) + dot_nt(grad_up, w_up[...])

    @pl.when(step == steps - 1)
    def _():
        out_ref[...] = out[...].astype(out_ref.dtype)
        back_ref[...] = back[...].astype(back_ref.dtype)


def mlp(second, cot, own_gu, own_dn, pair=None, place=None, own=True, sums=()):
    rows = tuple(v.shape[0] for v in second), tuple(v.shape[0] for v in cot)
    total = sum(rows[0])
    hidden = own_gu.shape[2]
    tile = min(256, hidden)
    shards = own + (pair is not None)
    kind = F32 if pair is None else BF16
    if pair is None:
        place = jnp.zeros((1,), jnp.int32)
    block = pl.BlockSpec((total, D), lambda i, p: (0, 0))
    arrays = (*second, *cot, own_gu, own_dn, *(() if pair is None else (pair,)), *sums)
    return pl.pallas_call(
        functools.partial(
            mlp_kernel,
            rows=rows,
            paired=pair is not None,
            tile=tile,
            own=own,
            carried_in=bool(sums),
        ),
        grid_spec=pltpu.PrefetchScalarGridSpec(
            num_scalar_prefetch=1,
            grid=(shards * hidden // tile,),
            in_specs=[ANYWHERE] * len(arrays),
            out_specs=[block, block],
            scratch_shapes=[
                pltpu.VMEM((total, D), BF16),
                pltpu.VMEM((total, D), BF16),
                pltpu.VMEM((2, 2, D, tile), BF16),
                pltpu.VMEM((2, tile, D), BF16),
                pltpu.VMEM((total, D), F32),
                pltpu.VMEM((total, D), F32),
                pltpu.SemaphoreType.DMA((len(second) + len(cot) + len(sums),)),
                pltpu.SemaphoreType.DMA((2,)),
                pltpu.SemaphoreType.DMA((2,)),
            ],
        ),
        out_shape=[jax.ShapeDtypeStruct((total, D), kind)] * 2,
        compiler_params=pltpu.CompilerParams(vmem_limit_bytes=VMEM_LIMIT),
        cost_estimate=pl.CostEstimate(
            flops=12 * total * D * hidden * shards,
            bytes_accessed=6 * D * hidden * shards,
            transcendentals=0,
        ),
        name="mlp",
    )(place, *arrays)


class Grid:
    def __init__(self):
        self.seq = lax.axis_size("seq")
        self.rows = lax.axis_size("rows")
        self.zs = Z_SIZE
        self.xs = self.rows // Z_SIZE
        self.ys = self.seq // CORES
        s = lax.axis_index("seq")
        r = lax.axis_index("rows")
        self.y, self.c = s // CORES, s % CORES
        self.z, self.x = r // self.xs, r % self.xs
        self.s, self.r = s, r

    def send(self, value, move):
        route = []
        for s in range(self.seq):
            for r in range(self.rows):
                there = move(s // CORES, s % CORES, r // self.xs, r % self.xs)
                if there is not None:
                    y, c, z, x = there
                    target = (y * CORES + c) * self.rows + z * self.xs + x
                    route.append((s * self.rows + r, target))
        return jax.tree.map(lambda v: lax.ppermute(v, ("seq", "rows"), route), value)

    def along_z(self, value, k):
        return self.send(value, lambda y, c, z, x: (y, c, (z + k) % self.zs, x))

    def along_x(self, value, k):
        return self.send(value, lambda y, c, z, x: (y, c, z, (x + k) % self.xs))

    def along_y(self, value, k):
        return self.send(value, lambda y, c, z, x: ((y + k) % self.ys, c, z, x))

    def flip_z(self, value, bit):
        return self.send(value, lambda y, c, z, x: (y, c, z ^ bit, x))

    def flip_core(self, value):
        return self.send(value, lambda y, c, z, x: (y, 1 - c, z, x))

    def flip_x(self, value, bit):
        return self.send(value, lambda y, c, z, x: (y, c, z, x ^ bit))

    def flip_seq(self, value, bit):
        def move(y, c, z, x):
            s = (y * CORES + c) ^ bit
            return (s // CORES, s % CORES, z, x)

        return self.send(value, move)

    def along_seq(self, value, k):
        def move(y, c, z, x):
            s = y * CORES + c + k
            return (s // CORES, s % CORES, z, x) if 0 <= s < self.seq else None

        return self.send(value, move)


def after(values, *events):
    return lax.optimization_barrier((values, *events))[0]


class Gather:
    def __init__(self, grid, *shards):
        self.grid = grid
        self.size = shards[0].shape[0] // grid.seq
        at = grid.s * self.size
        own = [lax.dynamic_slice_in_dim(v, at, self.size, 0) for v in shards]
        self.own = jnp.concatenate(own, axis=1) if len(own) > 1 else own[0]

    def over_z(self):
        grid = self.grid
        pieces = [self.own] + [grid.along_z(self.own, k) for k in range(1, grid.zs)]
        half = grid.zs // 2
        self.halves = [jnp.concatenate(pieces[:half]), jnp.concatenate(pieces[half:])]

    def first(self):
        grid = self.grid
        a, b = self.halves
        self.moved = [
            [grid.along_x(a, k) for k in range(1, grid.xs)],
            [grid.along_y(b, k) for k in range(1, grid.ys)],
        ]

    def second(self):
        grid = self.grid
        a, b = (jnp.concatenate([h, *m]) for h, m in zip(self.halves, self.moved))
        self.blocks = [a, b]
        self.last = [grid.along_y(a, k) for k in range(1, grid.ys)]
        self.last += [grid.along_x(b, k) for k in range(1, grid.xs)]

    def cores(self):
        self.over = [self.grid.flip_core(b) for b in self.blocks]

    def result(self):
        grid = self.grid
        blocks = self.blocks + self.last
        blocks = blocks + self.over + [grid.flip_core(b) for b in self.last]
        places = []
        kzs = range(grid.zs // 2), range(grid.zs // 2, grid.zs)
        a = [(kx, 0, kz) for kx in range(grid.xs) for kz in kzs[0]]
        b = [(0, ky, kz) for ky in range(grid.ys) for kz in kzs[1]]
        moves = a + b
        for k in range(1, grid.ys):
            moves = moves + [(kx, k, kz) for kx, _, kz in a]
        for k in range(1, grid.xs):
            moves = moves + [(k, ky, kz) for _, ky, kz in b]
        for core in range(CORES):
            c = (grid.c + core) % CORES
            for kx, ky, kz in moves:
                z, x, y = (grid.z - kz) % grid.zs, (grid.x - kx) % grid.xs, (grid.y - ky) % grid.ys
                places.append((z * grid.xs + x) * grid.seq + y * CORES + c)
        return Gathered(blocks, jnp.stack(places).astype(jnp.int32), self.size)


def pair_part(grid, gate_up, down):
    part = D // grid.seq
    hidden = down.shape[0]
    size = (1, part, hidden)
    gu = [lax.dynamic_slice(gate_up, (i, grid.s * part, 0), size)[0] for i in range(2)]
    dn = lax.dynamic_slice_in_dim(down, grid.s * part, part, 1)
    dn = jnp.concatenate([dn[i : i + part] for i in range(0, hidden, part)], axis=1)
    return jnp.concatenate([*gu, dn], axis=0)


def gather_pair(grid, part):
    groups = []
    for z in range(0, grid.zs, 2):
        for x in range(grid.xs):
            rows = [(z + i) * grid.xs + x for i in range(2)]
            groups.append([s * grid.rows + r for s in range(grid.seq) for r in rows])
    parts = lax.all_gather(part, ("seq", "rows"), axis_index_groups=groups)
    return parts, (1 - grid.z % 2).reshape(1).astype(jnp.int32)


def spread_near(grid, block):
    return [block] + [grid.along_x(block, k) for k in range(1, grid.xs)]


def spread_far(grid, block, parts):
    size = block.shape[0] // parts
    return [grid.flip_z(block[p * size : (p + 1) * size], NEAR_BIT) for p in range(parts)]


def relay(grid, pieces):
    moved = [grid.along_x(piece, k) for k in range(1, grid.xs) for piece in pieces]
    return list(pieces) + moved


def collect_near(grid, near, length):
    blocks = [near[k * length : (k + 1) * length] for k in range(grid.xs)]
    return [blocks[0]] + [grid.along_x(blocks[k], -k) for k in range(1, grid.xs)]


def collect_far(grid, far, length, parts):
    size = length // parts
    send, total = [], None
    for p in range(parts):
        lo = p * size
        far = after(far, total)
        total = far[lo : lo + size]
        for k in range(1, grid.xs):
            other = grid.along_x(far[k * length + lo : k * length + lo + size], -k)
            total = (total.astype(F32) + other.astype(F32)).astype(BF16)
        send.append(total)
    return send


def total_over_all(grid, values):
    widths = [v.shape[2] for v in values]
    packed = jnp.concatenate([v.astype(BF16) for v in values], axis=2)
    packed = jnp.pad(packed, ((0, 0), (0, 0), (0, -packed.shape[2] % FEAT)))
    chunk = lambda i: lax.dynamic_index_in_dim(packed, i, 0, False)
    total = chunk(grid.s).astype(F32)
    for k in range(1, grid.seq):
        total = total + grid.flip_seq(chunk(grid.s ^ k), k).astype(F32)
    for flip, count in ((grid.flip_z, grid.zs), (grid.flip_x, grid.xs)):
        mine = total.astype(BF16)
        terms = [mine.astype(F32)] + [flip(mine, k).astype(F32) for k in range(1, count)]
        while len(terms) > 1:
            terms = [a + b for a, b in zip(terms[::2], terms[1::2])]
        total = terms[0]
    out, at = [], 0
    for w in widths:
        out.append(total[:, at : at + w])
        at += w
    return out


def pair_maps(maps):
    both = jnp.concatenate([maps, -maps], axis=-1)
    both = both.reshape(-1, 2, HEAD, FEAT)
    none = jnp.zeros_like(both[:, 0])
    return jnp.concatenate(
        [
            jnp.concatenate([both[:, 0], none], axis=-1),
            jnp.concatenate([none, both[:, 1]], axis=-1),
        ],
        axis=1,
    )


def adapters(query, key, value, axis):
    if axis == 1:
        joined = jnp.concatenate([query, key, value], axis=1)
        return jnp.pad(joined, ((0, 0), (0, LOW - joined.shape[1])))
    rank = query.shape[0]
    joined = jnp.zeros((LOW, QKV), query.dtype)
    joined = joined.at[:rank, :D].set(query)
    joined = joined.at[rank : 2 * rank, D : D + KVD].set(key)
    return joined.at[2 * rank : 3 * rank, D + KVD :].set(value)


def documents(grid, starts, length):
    own = starts.astype(BF16)
    other = grid.flip_core(own)
    chip = jnp.where(grid.c == 0, jnp.concatenate([own, other]), jnp.concatenate([other, own]))
    resets = jnp.zeros((grid.ys, chip.shape[0]), BF16)
    resets = lax.dynamic_update_slice(resets, chip[None], (grid.y, 0))
    for k in range(1, grid.ys):
        got = grid.along_y(chip, k)
        resets = lax.dynamic_update_slice(resets, got[None], ((grid.y - k) % grid.ys, 0))
    heard = resets
    resets = resets.reshape(-1).astype(jnp.int32)
    places = jnp.arange(resets.shape[0], dtype=jnp.int32)
    docs = jnp.cumsum(jnp.where(places == 0, 1, resets))
    padded = jnp.concatenate([jnp.full((WINDOW,), -1, jnp.int32), docs])
    extended = lax.dynamic_slice_in_dim(padded, grid.s * length, length + WINDOW, 0)
    own = extended[WINDOW:]
    before = extended[WINDOW - 1]
    last = own[-1]
    ends = docs[length - 1 :: length]
    places = jnp.arange(grid.seq, dtype=jnp.int32)
    tiles = jnp.tile(extended.reshape(-1, 1, WINDOW), (1, GROUPS, 1)).reshape(-1, WIDE)
    masks = dict(
        qdoc=own[:, None],
        kdoc=jnp.pad(tiles, ((0, 8 - tiles.shape[0]), (0, 0))),
        fresh=(own == before).astype(F32)[:, None],
        survive=(own == last).astype(F32)[:, None],
    )
    earlier = ((ends == before) & (places < grid.s)).astype(F32)
    entered = jnp.concatenate([jnp.full((1,), -1, jnp.int32), ends[:-1]])
    later = ((entered == last) & (places > grid.s)).astype(F32)
    pick = lambda v, k: lax.dynamic_index_in_dim(v, jnp.clip(grid.s + k, 0, grid.seq - 1), 0, False)
    former = [pick(earlier, -k) * (grid.s - k >= 0) for k in range(1, grid.seq)]
    latter = [pick(later, k) * (grid.s + k < grid.seq) for k in range(1, grid.seq)]
    return masks, former, latter, heard


def local(
    tokens, doc_starts, cotangent, norm_first, norm_second,
    w_query, w_key, w_value, w_out, w_gate_up, w_down,
    query_in, query_out, key_in, key_out, value_in, value_out, proj_in, proj_out,
    map_query, map_key, window_logit,
):
    grid = Grid()
    length = tokens.shape[1]
    rank = query_in.shape[1]
    hidden = tokens[0]
    grad_out = cotangent[0]
    gain_first = norm_first.astype(F32)[None, :]
    gain_second = norm_second.astype(F32)[None, :]

    masks, former, latter, heard = documents(grid, doc_starts[0], length)
    qkv = Gather(grid, w_query, w_key, w_value)
    out = Gather(grid, w_out)
    cot_near = spread_near(grid, grad_out)
    qkv.over_z()

    values = hidden.astype(F32)
    inverse_first = lax.rsqrt(jnp.mean(values * values, axis=-1, keepdims=True) + EPSILON)
    inputs = (values * inverse_first * gain_first).astype(BF16)
    gamma = jax.nn.sigmoid(window_logit)
    masks["gamma"] = jnp.repeat(gamma, HEAD)[None, :]
    half = HEAD // 2
    inverse_freq = jnp.power(THETA, -(jnp.arange(half, dtype=F32) * 2.0 / HEAD))
    places = (grid.s * length + jnp.arange(length, dtype=jnp.int32)).astype(F32)
    angles = places[:, None] * inverse_freq[None, :]
    sine = jnp.sin(angles)
    masks["cos"] = jnp.tile(jnp.cos(angles), (1, WIDE // half))
    masks["sin"] = jnp.tile(jnp.concatenate([-sine, sine], axis=1), (1, WIDE // HEAD))
    maps_q, maps_k = pair_maps(map_query), pair_maps(map_key)
    qkv_in = adapters(query_in, key_in, value_in, 1)
    qkv_out = adapters(query_out, key_out, value_out, 0)
    o_in = jnp.pad(proj_in, ((0, 0), (0, LOW - rank)))
    o_out = jnp.pad(proj_out, ((0, LOW - rank), (0, 0)))
    low = dot_nn(inputs, qkv_in).astype(BF16)

    cot_near, qkv.halves, heard, out.own = after((cot_near, qkv.halves, heard, out.own))
    qkv.first()
    out.over_z()
    ready = (masks, former, latter, maps_q, maps_k, qkv_in, qkv_out, o_in, o_out, inputs, low)
    mine = w_gate_up, w_down
    qkv.moved, out.halves, ready, mine, grad_out = after(
        (qkv.moved, out.halves, ready, mine, grad_out)
    )
    pair = pair_part(grid, *mine)
    masks, former, latter, maps_q, maps_k, qkv_in, qkv_out, o_in, o_out, inputs, low = ready
    cosine, sine = masks["cos"], masks["sin"]
    qkv.second()
    qkv.cores()
    half = length // 2
    cot_far = spread_far(grid, grad_out[:half], 1)
    late = grad_out[half:]
    qkv.last, qkv.over, out.halves, cot_far, late, pair = after(
        (qkv.last, qkv.over, out.halves, cot_far, late, pair)
    )
    pair = gather_pair(grid, pair)
    w_qkv = qkv.result()
    out.first()
    kv, kf, pack, full = project_kv(
        w_qkv, inputs, low, qkv_out[:, D:], cosine, sine, maps_k, masks["survive"]
    )
    kv, kf, pack, full, out.moved, late = after((kv, kf, pack, full, out.moved, late))
    cot_far += spread_far(grid, late, 1)
    rim = grid.along_seq(pack, 1)
    fulls = [grid.along_seq(full, k) for k in range(2, grid.seq)]
    queries = project_q(0, w_qkv, inputs, low, qkv_out, cosine, sine, maps_q)
    rim, fulls, out.moved, queries = after((rim, fulls, out.moved, queries))
    out.second()
    queries = project_q(1, w_qkv, inputs, low, qkv_out, cosine, sine, maps_q, queries)
    carry = former[0] * rim[2 * WINDOW :].astype(F32)
    for w, full in zip(former[1:], fulls):
        carry = carry + w * full.astype(F32)
    carry = carry.astype(BF16)
    block = attend(0, *queries, kv, kf, rim, carry, masks)
    out.blocks, out.last, block, queries, cot_far = after(
        (out.blocks, out.last, block, queries, cot_far)
    )
    out.cores()
    w_o = out.result()
    merged, attended, inverse = attend(1, *queries, kv, kf, rim, carry, masks, block)
    merged, w_o.blocks, cot_far[0] = after((merged, w_o.blocks, cot_far[0]))
    moved = relay(grid, cot_far[:1])[1:]
    residual, second_in, out_low, inverse_second = out_project(
        w_o, merged, hidden, o_in, o_out, gain_second
    )
    second_in, moved = after((second_in, moved))
    near = spread_near(grid, second_in)
    far = spread_far(grid, second_in[:half], 1)
    near, far, late, cot_far = after((near, far, second_in[half:], cot_far))
    others = relay(grid, cot_far[1:])[1:]
    cot_far = cot_far + [v for pieces in zip(moved, others) for v in pieces]
    far += spread_far(grid, late, 1)
    moved = relay(grid, far[:1])[1:]
    sums = mlp(near, cot_near, w_gate_up, w_down)
    sums, far, moved = after((sums, far, moved))
    others = relay(grid, far[1:])[1:]
    far = far + [v for pieces in zip(moved, others) for v in pieces]
    shard = w_gate_up, w_down, *pair
    near_out, near_grad = mlp(near, cot_near, *shard, own=False, sums=sums)
    far, near_out, near_grad = after((far, near_out, near_grad))
    far_out, far_grad = mlp(far, cot_far, *shard)
    terms = collect_near(grid, near_grad, length)
    far_grad, terms = after((far_grad, terms))
    send = collect_far(grid, far_grad, length, 2)
    near_out, far_out = after((near_out, far_out), send)
    terms.append(jnp.concatenate([grid.flip_z(v, NEAR_BIT) for v in send], axis=0))

    grad_residual, grad_merged, grad_gain_two, grad_proj_in, grad_proj_out = branch_back(
        w_o, terms, grad_out, residual, inverse_second, gain_second, o_in, o_out, merged, out_low
    )
    *scaled, back = scaled_grads(grad_merged, attended, inverse, queries[1], masks)
    out_terms = collect_near(grid, near_out, length)
    send = collect_far(grid, far_out, length, 1)
    back, scaled, out_terms, send = after((back, scaled, out_terms, send))
    out_terms += [grid.flip_z(v, NEAR_BIT) for v in send]
    returned = [grid.along_seq(back, -k) for k in range(1, grid.seq)]
    raw_query, dkv, dkf, rim_back, dmap_query, dlogit = attend_back(
        *queries, kv, kf, rim, carry, *scaled, masks, maps_q
    )
    rim_back = grid.along_seq(rim_back, -1)
    returned, dkv = after((returned, dkv))
    far_back = jnp.zeros(back.shape, F32)
    for w, v in zip(latter[1:], returned[1:]):
        far_back = far_back + w * v.astype(F32)
    near_back = far_back + latter[0] * returned[0].astype(F32)
    near_back, far_back = near_back.astype(BF16), far_back.astype(BF16)
    raw_key, raw_value, dmap_key = keys_back(
        kv, kf, dkv, dkf, rim_back, near_back, far_back, masks, maps_k
    )
    raw_key, out_terms = after((raw_key, out_terms))
    block_out = residual
    for term in out_terms:
        block_out = block_out + term.astype(F32)
    block_out = block_out.astype(BF16)
    grad_tokens, grad_gain_one, grad_qkv_in, grad_qkv_out = inputs_back(
        w_qkv, [raw_query, raw_key, raw_value], qkv_in, qkv_out, low, inputs,
        hidden, gain_first, grad_residual,
    )
    grad_logit = dlogit[:, :GROUPS, 0].reshape(HEADS) * (1.0 - gamma)
    grad_proj_in, grad_proj_out = grad_proj_in[:rank], grad_proj_out[:rank]

    blocks = lambda v: v.reshape(8, grid.seq, -1).swapaxes(0, 1)
    plain = lambda v: v.reshape(grid.seq, 8, -1)
    outs = (
        blocks(grad_qkv_out[:rank, :D]),
        blocks(grad_qkv_out[rank : 2 * rank, D : D + KVD]),
        blocks(grad_qkv_out[2 * rank : 3 * rank, D + KVD :]),
        blocks(grad_proj_out),
    )
    ins = [blocks(grad_qkv_in[i * rank : (i + 1) * rank]) for i in range(3)]
    ins.append(blocks(grad_proj_in))
    map_q = plain(dmap_query[:, :, :HEAD].reshape(HEADS, -1))
    map_k = dmap_key[:, :, :HEAD].reshape(KV_HEADS, grid.seq, -1).swapaxes(0, 1)
    logit = jnp.pad(grad_logit.reshape(grid.seq, -1, 1), ((0, 0), (0, 8 - HEADS // grid.seq), (0, 0)))
    sums = total_over_all(
        grid, [*outs, *ins, map_q, map_k, plain(grad_gain_one), plain(grad_gain_two), logit]
    )
    outs, ins, (map_q, map_k, gain_one, gain_two, logit) = sums[:4], sums[4:8], sums[8:]
    width = D // grid.seq
    return (
        block_out[None],
        grad_tokens[None],
        gain_one.reshape(width),
        gain_two.reshape(width),
        ins[0].T,
        outs[0],
        ins[1].T,
        outs[1],
        ins[2].T,
        outs[2],
        ins[3].T,
        outs[3],
        map_q.reshape(-1, HEAD, HEAD),
        map_k.reshape(KV_HEADS, -1, HEAD),
        logit[: HEADS // grid.seq, 0],
    )


def solution(mesh):
    placed = (
        P("rows", "seq", None),
        P("rows", "seq"),
        P("rows", "seq", None),
        P(),
        P(),
        P("rows", None),
        P("rows", None),
        P("rows", None),
        P("rows", None),
        P(None, None, "rows"),
        P("rows", None),
        P(),
        P(),
        P(),
        P(),
        P(),
        P(),
        P(),
        P(),
        P(),
        P(),
        P(),
    )
    return jax.shard_map(
        local,
        mesh=mesh,
        in_specs=placed,
        out_specs=(
            P("rows", "seq", None),
            P("rows", "seq", None),
            P("seq"),
            P("seq"),
            P("seq", None),
            P(None, "seq"),
            P("seq", None),
            P(None, "seq"),
            P("seq", None),
            P(None, "seq"),
            P("seq", None),
            P(None, "seq"),
            P("seq", None, None),
            P(None, "seq", None),
            P("seq"),
        ),
        check_vma=False,
    )
```

```python
import functools

import jax
import jax.numpy as jnp
from jax import lax
from jax.experimental import pallas as pl
from jax.experimental.pallas import tpu as pltpu
from jax.sharding import PartitionSpec as P

D = 2048
HEADS = 32
KV_HEADS = 8
HEAD = 64
WINDOW = 64
KVD = KV_HEADS * HEAD
GROUPS = HEADS // KV_HEADS
QKV = D + 2 * KVD
WIDE = GROUPS * HEAD
FEAT = 2 * HEAD
LOW = 128
STATE = 80
HALVES = 2
VMEM_LIMIT = 58 << 20
HALF = D // HALVES
PER_HALF = KV_HEADS // HALVES
SCALE = HEAD ** (-0.5)

EPSILON = 1e-05
THETA = 500000.0

Z_SIZE = 4
NEAR_BIT = 2
FAR_BIT = 1
CORES = 2
F32 = jnp.float32
BF16 = jnp.bfloat16


def dot_nn(a, b):
    return jnp.dot(a, b, preferred_element_type=F32)


def dot_nt(a, b):
    return lax.dot_general(a, b, (((1,), (1,)), ((), ())), preferred_element_type=F32)


def dot_tn(a, b):
    return lax.dot_general(a, b, (((0,), (0,)), ((), ())), preferred_element_type=F32)


def lane(shape):
    return lax.broadcasted_iota(jnp.int32, shape, 1)


def row(shape):
    return lax.broadcasted_iota(jnp.int32, shape, 0)


def low_half(shape):
    return lane(shape) % FEAT < HEAD


def turn(x, cosine, sine):
    width = x.shape[1]
    first = lane(x.shape) % HEAD < HEAD // 2
    swapped = jnp.where(
        first, pltpu.roll(x, width - HEAD // 2, 1), pltpu.roll(x, HEAD // 2, 1)
    )
    return x * cosine + swapped * sine


def halves_softmax(u):
    lo = low_half(u.shape)
    top = jnp.where(
        lo,
        jnp.max(jnp.where(lo, u, -jnp.inf), axis=1, keepdims=True),
        jnp.max(jnp.where(lo, -jnp.inf, u), axis=1, keepdims=True),
    )
    e = jnp.exp(u - top)
    total = jnp.where(
        lo,
        jnp.sum(jnp.where(lo, e, 0.0), axis=1, keepdims=True),
        jnp.sum(jnp.where(lo, 0.0, e), axis=1, keepdims=True),
    )
    return e / total


def halves_softmax_back(f, g):
    lo = low_half(f.shape)
    t = f * g
    total = jnp.where(
        lo,
        jnp.sum(jnp.where(lo, t, 0.0), axis=1, keepdims=True),
        jnp.sum(jnp.where(lo, 0.0, t), axis=1, keepdims=True),
    )
    v = f * (g - total)
    return v - pltpu.roll(v, HEAD, 1), t


def pair_features(x, maps):
    u = dot_nn(x, maps)
    return jnp.concatenate(
        [halves_softmax(u[:, :FEAT]), halves_softmax(u[:, FEAT:])], axis=1
    )


def same_head(size):
    shape = (GROUPS * size, WIDE)
    return (row(shape) // size == lane(shape) // HEAD).astype(F32)


def diagonal(tile, mask):
    wide = jnp.concatenate([tile, tile], axis=1)
    return (jnp.concatenate([wide] * GROUPS, axis=0) * mask).astype(BF16)


def diagonal_pair(tile):
    none = jnp.zeros_like(tile)
    return jnp.concatenate(
        [jnp.concatenate([tile, none], axis=1), jnp.concatenate([none, tile], axis=1)], axis=0
    )


def both_halves(kv):
    kv = kv.astype(F32)
    lo = low_half(kv.shape)
    other = pltpu.roll(kv, HEAD, 1)
    return jnp.where(lo, kv, other), jnp.where(lo, other, kv)


def fold_heads(r, mask):
    r = r * mask
    r = r[:64] + r[64:128] + r[128:192] + r[192:]
    r = r[:, :FEAT] + r[:, FEAT:]
    return r + pltpu.roll(r, HEAD, 1)


def fold_pair(r, size):
    return r[:size, :FEAT] + r[size:, FEAT:]


def whole(a):
    return pl.BlockSpec(a.shape, lambda *_: (0,) * len(a.shape))


ANYWHERE = pl.BlockSpec(memory_space=pl.ANY)
SCALARS = pl.BlockSpec(memory_space=pltpu.SMEM)


class Gathered:
    def __init__(self, blocks, places, size):
        self.blocks, self.places, self.size = blocks, places, size

    def shapes(self):
        return tuple(b.shape[0] // self.size for b in self.blocks)


def start_rows(places, refs, counts, size, target, sem, column=0):
    n = 0
    columns = slice(column, column + target.shape[1])
    for ref, count in zip(refs, counts):
        for i in range(count):
            to = pl.ds(pl.multiple_of(places[n] * size, size), size)
            part = ref.at[i * size : (i + 1) * size, columns]
            pltpu.make_async_copy(part, target.at[to], sem).start()
            n += 1


def wait_rows(target, sem):
    pltpu.make_async_copy(target, target, sem).wait()


def project_kv_kernel(*refs, counts, size):
    n = len(counts)
    places_ref, blocks = refs[0], refs[1 : 1 + n]
    x_ref, low_ref, p_ref, cos_ref, sin_ref, maps_ref, survive_ref = refs[1 + n : 8 + n]
    kv_ref, kf_ref, pack_ref, full_ref, w_ref, sem = refs[8 + n :]
    length = x_ref.shape[0]
    start_rows(places_ref, blocks, counts, size, w_ref, sem, D)
    wait_rows(w_ref, sem)
    survive = survive_ref[...]
    lo = low_half((length, FEAT))
    cut = length - WINDOW
    steps = KVD // WIDE
    part = lambda j: slice(j * WIDE, (j + 1) * WIDE)
    for i in range(steps):
        raw_k, raw_v = (
            dot_nn(x_ref[...], w_ref[:, part(j)]) + dot_nn(low_ref[...], p_ref[:, part(j)])
            for j in (i, steps + i)
        )
        keys = turn(raw_k, cos_ref[...], sin_ref[...]).astype(BF16)
        values = raw_v.astype(BF16).astype(F32)
        for p in range(WIDE // FEAT):
            at = (i * GROUPS + 2 * p) * FEAT
            k2 = keys[:, p * FEAT : (p + 1) * FEAT]
            v2 = values[:, p * FEAT : (p + 1) * FEAT]
            feats = pair_features(k2, maps_ref[2 * i + p])
            kf_ref[:, at : at + 2 * FEAT] = feats.astype(BF16)
            k2 = k2.astype(F32)
            k_other, v_other = pltpu.roll(k2, HEAD, 1), pltpu.roll(v2, HEAD, 1)
            ones = jnp.where(lane((length, FEAT)) < HEAD + 8, 1.0, 0.0)
            for h, kv, v in (
                (0, jnp.where(lo, k2, v_other), v2),
                (1, jnp.where(lo, k_other, v2), v_other),
            ):
                at_h = at + h * FEAT
                kv_ref[:, at_h : at_h + FEAT] = kv.astype(BF16)
                v_one = jnp.where(lo, v, ones).astype(BF16)
                kept = (feats[:, h * FEAT : (h + 1) * FEAT].astype(BF16).astype(F32) * survive)
                kept = kept.astype(BF16)
                head = dot_tn(v_one[:cut], kept[:cut])
                tail = dot_tn(v_one[cut:], kept[cut:])
                at_h = slice(at_h, at_h + FEAT)
                pack_ref[2 * WINDOW :, at_h] = head[:STATE].astype(BF16)
                full_ref[:, at_h] = (head + tail)[:STATE].astype(BF16)
    pack_ref[:WINDOW, :] = kv_ref[cut:, :]
    pack_ref[WINDOW : 2 * WINDOW, :] = kf_ref[cut:, :]


def project_kv(w, x, low, p, cosine, sine, maps, survive):
    length = x.shape[0]
    shapes = (
        jax.ShapeDtypeStruct((length, KV_HEADS * FEAT), BF16),
        jax.ShapeDtypeStruct((length, KV_HEADS * FEAT), BF16),
        jax.ShapeDtypeStruct((2 * WINDOW + STATE, KV_HEADS * FEAT), BF16),
        jax.ShapeDtypeStruct((STATE, KV_HEADS * FEAT), BF16),
    )
    rest = (x, low, p, cosine, sine, maps, survive)
    return pl.pallas_call(
        functools.partial(project_kv_kernel, counts=w.shapes(), size=w.size),
        grid=(1,),
        in_specs=[SCALARS] + [ANYWHERE] * len(w.blocks) + [whole(a) for a in rest],
        out_specs=[whole(v) for v in shapes],
        out_shape=shapes,
        scratch_shapes=[pltpu.VMEM((D, 2 * KVD), BF16), pltpu.SemaphoreType.DMA],
        compiler_params=pltpu.CompilerParams(vmem_limit_bytes=VMEM_LIMIT),
        cost_estimate=pl.CostEstimate(
            flops=4 * length * D * KVD, bytes_accessed=4 * D * KVD, transcendentals=0
        ),
        name="project_kv",
    )(w.places, *w.blocks, *rest)


def project_q_kernel(*refs, counts, size, column):
    n = len(counts)
    places_ref, blocks = refs[0], refs[1 : 1 + n]
    x_ref, low_ref, p_ref, cos_ref, sin_ref, maps_ref = refs[1 + n : 7 + n]
    q_ref, qf_ref, w_ref, sem = refs[-4:]
    step = pl.program_id(0)

    @pl.when(step == 0)
    def _():
        start_rows(places_ref, blocks, counts, size, w_ref, sem, column)
        wait_rows(w_ref, sem)

    at = pl.ds(pl.multiple_of(step * WIDE, WIDE), WIDE)
    raw = dot_nn(x_ref[...], w_ref[:, at]) + dot_nn(low_ref[...], p_ref[...])
    q = turn(raw, cos_ref[...], sin_ref[...]).astype(BF16)
    q_ref[...] = q
    for p in range(WIDE // FEAT):
        feats = pair_features(q[:, p * FEAT : (p + 1) * FEAT], maps_ref[p])
        qf_ref[:, 2 * p * FEAT : 2 * (p + 1) * FEAT] = feats.astype(BF16)


def project_q(half, w, x, low, p, cosine, sine, maps, former=()):
    length = x.shape[0]
    first = half * PER_HALF
    pairs = WIDE // FEAT
    arrays = (w.places, *w.blocks, x, low, p, cosine, sine, maps, *former)
    return pl.pallas_call(
        functools.partial(
            project_q_kernel, counts=w.shapes(), size=w.size, column=half * HALF
        ),
        grid=(HALF // WIDE,),
        in_specs=[SCALARS] + [ANYWHERE] * len(w.blocks) + [
            whole(x), whole(low),
            pl.BlockSpec((LOW, WIDE), lambda g: (0, first + g)),
            whole(cosine), whole(sine),
            pl.BlockSpec((pairs, FEAT, 2 * FEAT), lambda g: (first + g, 0, 0)),
        ] + [ANYWHERE] * len(former),
        out_specs=[
            pl.BlockSpec((length, WIDE), lambda g: (0, first + g)),
            pl.BlockSpec((length, 2 * WIDE), lambda g: (0, first + g)),
        ],
        out_shape=[
            jax.ShapeDtypeStruct((length, D), BF16),
            jax.ShapeDtypeStruct((length, 2 * D), BF16),
        ],
        input_output_aliases={len(arrays) - len(former) + i: i for i in range(len(former))},
        scratch_shapes=[pltpu.VMEM((D, HALF), BF16), pltpu.SemaphoreType.DMA],
        compiler_params=pltpu.CompilerParams(vmem_limit_bytes=VMEM_LIMIT),
        cost_estimate=pl.CostEstimate(
            flops=2 * length * D * HALF, bytes_accessed=2 * D * HALF, transcendentals=0
        ),
        name="project_q",
    )(*arrays)


def key_tiles(kv_ref, kf_ref, rim_kv_ref, rim_kf_ref, mask):
    tiles = []
    for t in range(1 + kv_ref.shape[0] // WINDOW):
        if t == 0:
            kv, kf = rim_kv_ref[...], rim_kf_ref[...]
        else:
            at = (t - 1) * WINDOW
            kv, kf = kv_ref[at : at + WINDOW, :], kf_ref[at : at + WINDOW, :]
        kk, vv = both_halves(kv)
        tiles.append((diagonal(kk, mask * SCALE), diagonal(vv, mask), diagonal_pair(kf)))
    return tiles


def spans(t, length):
    edge = lambda v: min(max(v, 0), length)
    a, b, c = edge((t - 1) * WINDOW), edge(t * WINDOW), edge((t + 1) * WINDOW)
    return (a, b), (b, c), (c, length)


def weights_of(t, tile, q_ref, qf_ref, same, upper, gamma):
    length = q_ref.shape[0]
    (a, b), (_, c), _ = spans(t, length)
    e = jnp.exp(dot_nt(q_ref[a:c, :], tile[0]))
    linear = None
    if b < length:
        linear = gamma * jnp.concatenate(
            [
                dot_nt(qf_ref[b:, 2 * p * FEAT : 2 * (p + 1) * FEAT], tile[2])
                for p in range(GROUPS // 2)
            ],
            axis=1,
        )
    parts = []
    if b > a:
        parts.append(jnp.where(same(a, b) & upper, e[: b - a], 0.0))
    if c > b:
        mixed = jnp.where(upper, linear[: c - b], e[b - a :])
        parts.append(jnp.where(same(b, c), mixed, 0.0))
    if length > c:
        parts.append(jnp.where(same(c, length), linear[c - b :], 0.0))
    return e, jnp.concatenate(parts, axis=0).astype(BF16)


def carried(carry_ref):
    state = carry_ref[...]
    ones = jnp.zeros((HEAD, FEAT), BF16) + state[HEAD : HEAD + 1, :]
    return diagonal_pair(state[:HEAD, :]), diagonal_pair(ones)


def attend_kernel(
    q_ref, qf_ref, kv_ref, kf_ref, rim_kv_ref, rim_kf_ref, carry_ref,
    qdoc_ref, kdoc_ref, fresh_ref, gamma_ref, *refs,
):
    out_ref, att_ref, inv_ref, num_ref, den_ref = refs[-5:]
    length = q_ref.shape[0]
    mask = same_head(WINDOW)
    ones = mask.astype(BF16)
    gamma = gamma_ref[...]
    shape = (WINDOW, WIDE)
    upper = row(shape) >= lane(shape) % HEAD
    state, state_sum = carried(carry_ref)
    fresh = fresh_ref[...] * gamma
    for p in range(GROUPS // 2):
        feats = qf_ref[:, 2 * p * FEAT : 2 * (p + 1) * FEAT]
        at = slice(p * FEAT, (p + 1) * FEAT)
        num_ref[:, at] = dot_nt(feats, state) * fresh[:, at]
        den_ref[:, at] = dot_nt(feats, state_sum) * fresh[:, at]
    for t, tile in enumerate(key_tiles(kv_ref, kf_ref, rim_kv_ref, rim_kf_ref, mask)):
        a = spans(t, length)[0][0]
        same = lambda i, j, t=t: qdoc_ref[i:j, :] == kdoc_ref[t : t + 1, :]
        _, w = weights_of(t, tile, q_ref, qf_ref, same, upper, gamma)
        num_ref[a:, :] += dot_nn(w, tile[1])
        den_ref[a:, :] += dot_nn(w, ones)
    inv = 1.0 / den_ref[...]
    att = num_ref[...] * inv
    inv_ref[...] = inv
    att_ref[...] = att
    out_ref[...] = att.astype(BF16)


def group_specs(length, first=0):
    column = lambda rows, width: pl.BlockSpec((rows, width), lambda g: (0, first + g))
    fixed = lambda rows, width: pl.BlockSpec((rows, width), lambda g: (0, 0))
    return dict(
        q=column(length, WIDE),
        qf=column(length, 2 * WIDE),
        k=column(length, FEAT),
        rim_kv=column(WINDOW, FEAT),
        rim_kf=pl.BlockSpec((WINDOW, FEAT), lambda g: (1, first + g)),
        state=column(STATE, FEAT),
        qdoc=fixed(length, 1),
        kdoc=fixed(8, WIDE),
        gamma=column(1, WIDE),
        wide=fixed(length, WIDE),
        maps=pl.BlockSpec((GROUPS // 2, FEAT, 2 * FEAT), lambda g: (first + g, 0, 0)),
    )


def attend(half, q, qf, kv, kf, rim, carry, masks, former=()):
    length = q.shape[0]
    s = group_specs(length, half * PER_HALF)
    arrays = (
        q, qf, kv, kf, rim, rim, carry,
        masks["qdoc"], masks["kdoc"], masks["fresh"], masks["gamma"], *former,
    )
    return pl.pallas_call(
        attend_kernel,
        grid=(PER_HALF,),
        in_specs=[
            s["q"], s["qf"], s["k"], s["k"], s["rim_kv"], s["rim_kf"], s["state"],
            s["qdoc"], s["kdoc"], s["qdoc"], s["gamma"],
        ] + [ANYWHERE] * len(former),
        out_specs=[s["q"]] * 3,
        out_shape=[
            jax.ShapeDtypeStruct((length, D), BF16),
            jax.ShapeDtypeStruct((length, D), F32),
            jax.ShapeDtypeStruct((length, D), F32),
        ],
        input_output_aliases={len(arrays) - len(former) + i: i for i in range(len(former))},
        scratch_shapes=[pltpu.VMEM((length, WIDE), F32)] * 2,
        compiler_params=pltpu.CompilerParams(vmem_limit_bytes=VMEM_LIMIT),
        cost_estimate=pl.CostEstimate(
            flops=5_000_000_000, bytes_accessed=8 * length * D, transcendentals=0
        ),
        name="attend",
    )(*arrays)


def scaled_grads_kernel(
    ga_ref, att_ref, inv_ref, qf_ref, fresh_ref, gamma_ref, g_ref, gd_ref, back_ref
):
    mask = same_head(HEAD)
    ga = ga_ref[...].astype(F32)
    inv = inv_ref[...]
    product = ga * att_ref[...]
    high = product.astype(BF16)
    rest = (product - high.astype(F32)).astype(BF16)
    ones = mask.astype(BF16)
    gd = -(dot_nn(high, ones) + dot_nn(rest, ones)) * inv
    g = ga * inv
    g_ref[...] = g.astype(BF16)
    gd_ref[...] = gd
    fresh = fresh_ref[...] * gamma_ref[...]
    fresh_g = (g * fresh).astype(BF16)
    fresh_gd = (gd * fresh).astype(BF16)
    kv = sums = 0.0
    for p in range(GROUPS // 2):
        feats = qf_ref[:, 2 * p * FEAT : 2 * (p + 1) * FEAT]
        at = slice(p * FEAT, (p + 1) * FEAT)
        kv += fold_pair(dot_tn(fresh_g[:, at], feats), HEAD)
        sums += fold_pair(dot_tn(fresh_gd[:, at], feats), HEAD)
    back_ref[:HEAD, :] = kv.astype(BF16)
    back_ref[HEAD:, :] = sums[: STATE - HEAD].astype(BF16)


def scaled_grads(ga, att, inv, qf, masks):
    length = ga.shape[0]
    s = group_specs(length)
    return pl.pallas_call(
        scaled_grads_kernel,
        grid=(KV_HEADS,),
        in_specs=[s["q"], s["q"], s["q"], s["qf"], s["qdoc"], s["gamma"]],
        out_specs=[s["q"], s["q"], s["state"]],
        out_shape=[
            jax.ShapeDtypeStruct((length, D), BF16),
            jax.ShapeDtypeStruct((length, D), F32),
            jax.ShapeDtypeStruct((STATE, KV_HEADS * FEAT), BF16),
        ],
        compiler_params=pltpu.CompilerParams(vmem_limit_bytes=VMEM_LIMIT),
        name="scaled_grads",
    )(ga, att, inv, qf, masks["fresh"], masks["gamma"])


def attend_back_kernel(
    q_ref, qf_ref, kv_ref, kf_ref, rim_kv_ref, rim_kf_ref, carry_ref, g_ref, gd_ref,
    qdoc_ref, kdoc_ref, fresh_ref, gamma_ref, maps_ref, cos_ref, sin_ref,
    raw_ref, dkv_ref, dkf_ref, rim_ref, dmap_ref, logit_ref, dq_ref, dqf_ref,
):
    length = q_ref.shape[0]
    mask = same_head(WINDOW)
    gamma = gamma_ref[...]
    shape = (WINDOW, WIDE)
    upper = row(shape) >= lane(shape) % HEAD
    state, state_sum = carried(carry_ref)
    fresh = fresh_ref[...] * gamma
    pairs = range(GROUPS // 2)
    half = lambda p: slice(p * FEAT, (p + 1) * FEAT)
    full = lambda p: slice(2 * p * FEAT, 2 * (p + 1) * FEAT)
    fresh_g = (g_ref[...].astype(F32) * fresh).astype(BF16)
    fresh_gd = (gd_ref[...] * fresh * (1.0 / HEAD)).astype(BF16)
    for p in pairs:
        dqf_ref[:, full(p)] = dot_nn(fresh_g[:, half(p)], state) + dot_nn(
            fresh_gd[:, half(p)], state_sum
        )
    dq_ref[...] = jnp.zeros_like(dq_ref)
    lo = low_half((WINDOW, FEAT))
    for t, tile in enumerate(key_tiles(kv_ref, kf_ref, rim_kv_ref, rim_kf_ref, mask)):
        (a, b), (_, c), _ = spans(t, length)
        same = lambda i, j, t=t: qdoc_ref[i:j, :] == kdoc_ref[t : t + 1, :]
        e, w = weights_of(t, tile, q_ref, qf_ref, same, upper, gamma)
        g = g_ref[a:, :]
        x = dot_nt(g, tile[1]) + gd_ref[a:, :]
        near = x[: c - a] * e
        parts = []
        if b > a:
            parts.append(jnp.where(same(a, b) & upper, near[: b - a], 0.0))
        if c > b:
            parts.append(jnp.where(same(b, c), jnp.where(upper, 0.0, near[b - a :]), 0.0))
        ds = jnp.concatenate(parts, axis=0).astype(BF16)
        dq_ref[a:c, :] += dot_nn(ds, tile[0])
        dk = fold_heads(dot_tn(ds, q_ref[a:c, :]), mask) * SCALE
        dv = fold_heads(dot_tn(w, g), mask)
        at = slice((t - 1) * WINDOW, t * WINDOW)
        dkv = jnp.where(lo, dk, dv)
        if t:
            dkv_ref[at, :] = dkv
        else:
            rim_ref[:WINDOW, :] = dkv.astype(BF16)
        if b < length:
            far = x[b - a :] * gamma
            parts = [jnp.where(same(b, c) & upper, far[: c - b], 0.0)]
            if c < length:
                parts.append(jnp.where(same(c, length), far[c - b :], 0.0))
            dl = jnp.concatenate(parts, axis=0).astype(BF16)
            dkf = 0.0
            for p in pairs:
                dqf_ref[b:, full(p)] += dot_nn(dl[:, half(p)], tile[2])
                dkf += fold_pair(dot_tn(dl[:, half(p)], qf_ref[b:, full(p)]), HEAD)
            if t:
                dkf_ref[at, :] = dkf
            else:
                rim_ref[WINDOW:, :] = dkf.astype(BF16)
        else:
            dkf_ref[at, :] = jnp.zeros((WINDOW, FEAT), F32)
    for p in pairs:
        grads = []
        for h in (2 * p, 2 * p + 1):
            f = qf_ref[:, h * FEAT : (h + 1) * FEAT].astype(F32)
            gu, t = halves_softmax_back(f, dqf_ref[:, h * FEAT : (h + 1) * FEAT])
            grads.append(gu.astype(BF16))
            total = jnp.sum(jnp.sum(t, axis=0, keepdims=True), axis=1, keepdims=True)
            logit_ref[0, h : h + 1, :] = jnp.zeros((1, FEAT), F32) + total
        gu = jnp.concatenate(grads, axis=1)
        dq_ref[:, half(p)] += 0.5 * dot_nt(gu, maps_ref[p])
        dmap = dot_tn(q_ref[:, half(p)], gu)
        dmap_ref[2 * p] = dmap[:HEAD, :FEAT]
        dmap_ref[2 * p + 1] = dmap[HEAD:, FEAT:]
    raw_ref[...] = turn(dq_ref[...], cos_ref[...], -sin_ref[...]).astype(BF16)


def attend_back(q, qf, kv, kf, rim, carry, g, gd, masks, maps):
    length = q.shape[0]
    s = group_specs(length)
    column = lambda rows: pl.BlockSpec((rows, FEAT), lambda g: (0, g))
    return pl.pallas_call(
        attend_back_kernel,
        grid=(KV_HEADS,),
        in_specs=[
            s["q"], s["qf"], s["k"], s["k"], s["rim_kv"], s["rim_kf"], s["state"], s["q"], s["q"],
            s["qdoc"], s["kdoc"], s["qdoc"], s["gamma"], s["maps"], s["wide"], s["wide"],
        ],
        out_specs=[
            s["q"], column(length), column(length), column(2 * WINDOW),
            pl.BlockSpec((GROUPS, HEAD, FEAT), lambda g: (g, 0, 0)),
            pl.BlockSpec((1, 8, FEAT), lambda g: (g, 0, 0)),
        ],
        out_shape=[
            jax.ShapeDtypeStruct((length, D), BF16),
            jax.ShapeDtypeStruct((length, KV_HEADS * FEAT), F32),
            jax.ShapeDtypeStruct((length, KV_HEADS * FEAT), F32),
            jax.ShapeDtypeStruct((2 * WINDOW, KV_HEADS * FEAT), BF16),
            jax.ShapeDtypeStruct((HEADS, HEAD, FEAT), F32),
            jax.ShapeDtypeStruct((KV_HEADS, 8, FEAT), F32),
        ],
        scratch_shapes=[pltpu.VMEM((length, WIDE), F32), pltpu.VMEM((length, 2 * WIDE), F32)],
        compiler_params=pltpu.CompilerParams(vmem_limit_bytes=VMEM_LIMIT),
        cost_estimate=pl.CostEstimate(
            flops=15_000_000_000, bytes_accessed=8 * length * D, transcendentals=0
        ),
        name="attend_back",
    )(
        q, qf, kv, kf, rim, rim, carry, g, gd,
        masks["qdoc"], masks["kdoc"], masks["fresh"], masks["gamma"],
        maps, masks["cos"], masks["sin"],
    )


def keys_back_kernel(
    kv_ref, kf_ref, dkv_ref, dkf_ref, rim_kv_ref, rim_kf_ref, near_ref, far_ref, survive_ref,
    maps_ref, cos_ref, sin_ref, rk_ref, rv_ref, dmap_ref,
):
    length = kv_ref.shape[0]
    cut = length - WINDOW
    lo = low_half((length, FEAT))
    survive = survive_ref[...]
    dkv, grads = [], []
    for h in range(2):
        at = slice(h * FEAT, (h + 1) * FEAT)
        kv = kv_ref[:, at].astype(F32)
        kf = kf_ref[:, at]
        v_low = pltpu.roll(kv, HEAD, 1)
        ones = jnp.where(lane((length, FEAT)) == HEAD, 1.0, 0.0)
        v_one = jnp.where(lo, v_low, ones).astype(BF16)[:, :STATE]
        dkf, dv = [], []
        for back, part in ((near_ref, slice(0, cut)), (far_ref, slice(cut, length))):
            state = back[:, at]
            twice = jnp.concatenate([state[:HEAD], state[:HEAD]], axis=0)
            dkf.append(dot_nn(v_one[part], state))
            dv.append(dot_nt(kf[part], twice))
        rim = jnp.zeros((cut, FEAT), F32)
        dkf = (
            jnp.concatenate(dkf, axis=0) * survive
            + dkf_ref[:, at]
            + jnp.concatenate([rim, rim_kf_ref[:, at].astype(F32)], axis=0)
        )
        dv = jnp.concatenate(dv, axis=0) * survive
        total = (
            dkv_ref[:, at]
            + jnp.concatenate([rim, rim_kv_ref[:, at].astype(F32)], axis=0)
            + jnp.where(lo, 0.0, dv)
        )
        gu, _ = halves_softmax_back(kf.astype(F32), dkf)
        grads.append(gu.astype(BF16))
        dkv.append(total)
    gu = jnp.concatenate(grads, axis=1)
    keys = jnp.where(lo, kv_ref[:, :FEAT].astype(F32), pltpu.roll(kv_ref[:, FEAT:].astype(F32), HEAD, 1))
    dmap = dot_tn(keys.astype(BF16), gu)
    dmap_ref[0] = dmap[:HEAD, :FEAT]
    dmap_ref[1] = dmap[HEAD:, FEAT:]
    dk = jnp.where(lo, dkv[0], pltpu.roll(dkv[1], HEAD, 1)) + 0.5 * dot_nt(gu, maps_ref[0])
    rk_ref[...] = turn(dk, cos_ref[...], -sin_ref[...]).astype(BF16)
    rv_ref[...] = jnp.where(lo, pltpu.roll(dkv[0], HEAD, 1), dkv[1]).astype(BF16)


def keys_back(kv, kf, dkv, dkf, rim, near, far, masks, maps):
    length = kv.shape[0]
    pairs = KV_HEADS // 2
    column = lambda rows: pl.BlockSpec((rows, 2 * FEAT), lambda g: (0, g))
    state = pl.BlockSpec((STATE, 2 * FEAT), lambda g: (0, g))
    narrow = pl.BlockSpec((length, FEAT), lambda g: (0, 0))
    out = pl.BlockSpec((length, FEAT), lambda g: (0, g))
    return pl.pallas_call(
        keys_back_kernel,
        grid=(pairs,),
        in_specs=[
            column(length), column(length), column(length), column(length),
            column(WINDOW), pl.BlockSpec((WINDOW, 2 * FEAT), lambda g: (1, g)),
            state, state, pl.BlockSpec((length, 1), lambda g: (0, 0)),
            pl.BlockSpec((1, FEAT, 2 * FEAT), lambda g: (g, 0, 0)), narrow, narrow,
        ],
        out_specs=[out, out, pl.BlockSpec((2, HEAD, FEAT), lambda g: (g, 0, 0))],
        out_shape=[
            jax.ShapeDtypeStruct((length, KVD), BF16),
            jax.ShapeDtypeStruct((length, KVD), BF16),
            jax.ShapeDtypeStruct((KV_HEADS, HEAD, FEAT), F32),
        ],
        compiler_params=pltpu.CompilerParams(vmem_limit_bytes=VMEM_LIMIT),
        name="keys_back",
    )(
        kv, kf, dkv, dkf, rim, rim, near, far, masks["survive"], maps, masks["cos"], masks["sin"]
    )


def out_project_kernel(*refs, counts, size):
    n = len(counts)
    places, blocks, refs = refs[0], refs[1 : 1 + n], refs[1 + n :]
    m, hidden, proj_in, proj_out, gain = refs[:5]
    residual, second, low, inverse, w, sem = refs[5:]
    start_rows(places, blocks, counts, size, w, sem)
    reduced = dot_nn(m[...], proj_in[...]).astype(BF16)
    low[...] = reduced
    wait_rows(w, sem)
    squares = 0.0
    for j in range(D // WIDE):
        at = slice(j * WIDE, (j + 1) * WIDE)
        sums = (
            hidden[:, at].astype(F32)
            + dot_nn(m[...], w[:, at])
            + dot_nn(reduced, proj_out[:, at])
        )
        residual[:, at] = sums
        squares = squares + jnp.sum(sums * sums, axis=1, keepdims=True)
    inv = lax.rsqrt(squares * (1.0 / D) + EPSILON)
    inverse[...] = jnp.zeros(inverse.shape, F32) + inv
    second[...] = (residual[...] * inv * gain[...]).astype(BF16)


def out_project(w, merged, hidden, proj_in, proj_out, gain):
    length = hidden.shape[0]
    shapes = (
        jax.ShapeDtypeStruct((length, D), F32),
        jax.ShapeDtypeStruct((length, D), BF16),
        jax.ShapeDtypeStruct((length, LOW), BF16),
        jax.ShapeDtypeStruct((length, LOW), F32),
    )
    rest = (merged, hidden, proj_in, proj_out, gain)
    return pl.pallas_call(
        functools.partial(out_project_kernel, counts=w.shapes(), size=w.size),
        grid=(1,),
        in_specs=[SCALARS] + [ANYWHERE] * len(w.blocks) + [whole(a) for a in rest],
        out_specs=[whole(v) for v in shapes],
        out_shape=shapes,
        scratch_shapes=[pltpu.VMEM((D, D), BF16), pltpu.SemaphoreType.DMA],
        compiler_params=pltpu.CompilerParams(vmem_limit_bytes=VMEM_LIMIT),
        cost_estimate=pl.CostEstimate(
            flops=2 * length * D * D, bytes_accessed=2 * D * D, transcendentals=0
        ),
        name="out_project",
    )(w.places, *w.blocks, *rest)


def branch_back_kernel(*refs, counts, size, extra):
    n = len(counts)
    places, blocks, refs = refs[0], refs[1 : 1 + n], refs[1 + n :]
    sums, refs = refs[:extra], refs[extra:]
    cot, residual, inverse, gain, proj_in, proj_out, m, low = refs[:8]
    grad_residual, back_ref, grad_gain, grad_in, grad_out, w, sem = refs[8:]
    start_rows(places, blocks, counts, size, w, sem)
    total = sums[0][...].astype(F32)
    for v in sums[1:]:
        total = total + v[...].astype(F32)
    inv = inverse[:, :1]
    normed = residual[...] * inv
    product = total * normed
    grad_gain[...] = jnp.sum(product, axis=0, keepdims=True)
    scaled = total * gain[...]
    mean = jnp.sum(scaled * normed, axis=1, keepdims=True) * (1.0 / D)
    grad = cot[...].astype(F32) + inv * (scaled - normed * mean)
    grad_residual[...] = grad
    branch = grad.astype(BF16)
    grad_low = dot_nt(branch, proj_out[...]).astype(BF16)
    grad_out[...] = dot_tn(low[...], branch)
    grad_in[...] = dot_tn(grad_low, m[...])
    wait_rows(w, sem)
    for j in range(D // WIDE):
        at = slice(j * WIDE, (j + 1) * WIDE)
        back = dot_nt(grad_low, proj_in[at, :]) + dot_nt(branch, w[at, :])
        back_ref[:, at] = back.astype(BF16)


def branch_back(w, sums, cot, residual, inverse, gain, proj_in, proj_out, merged, low):
    length = cot.shape[0]
    shapes = (
        jax.ShapeDtypeStruct((length, D), F32),
        jax.ShapeDtypeStruct((length, D), BF16),
        jax.ShapeDtypeStruct((1, D), F32),
        jax.ShapeDtypeStruct((LOW, D), F32),
        jax.ShapeDtypeStruct((LOW, D), F32),
    )
    rest = (*sums, cot, residual, inverse, gain, proj_in, proj_out, merged, low)
    return pl.pallas_call(
        functools.partial(
            branch_back_kernel, counts=w.shapes(), size=w.size, extra=len(sums)
        ),
        grid=(1,),
        in_specs=[SCALARS] + [ANYWHERE] * len(w.blocks) + [whole(a) for a in rest],
        out_specs=[whole(v) for v in shapes],
        out_shape=shapes,
        scratch_shapes=[pltpu.VMEM((D, D), BF16), pltpu.SemaphoreType.DMA],
        compiler_params=pltpu.CompilerParams(vmem_limit_bytes=VMEM_LIMIT),
        cost_estimate=pl.CostEstimate(
            flops=2 * length * D * D, bytes_accessed=2 * D * D, transcendentals=0
        ),
        name="branch_back",
    )(w.places, *w.blocks, *rest)


def inputs_back_kernel(*refs, counts, size):
    n = len(counts)
    places, blocks, refs = refs[0], refs[1 : 1 + n], refs[1 + n :]
    raws, refs = refs[:3], refs[3:]
    p_in, p_out, low, x, hidden, gain, grad_residual = refs[:7]
    grad_tokens, grad_gain, grad_in, grad_out, w, raw, back, sem = refs[7:]
    start_rows(places, blocks, counts, size, w, sem)
    at = 0
    for r in raws:
        raw[:, at : at + r.shape[1]] = r[...]
        at += r.shape[1]
    grad_low = dot_nt(raw[...], p_out[...]).astype(BF16)
    grad_out[...] = dot_tn(low[...], raw[...])
    grad_in[...] = dot_tn(grad_low, x[...])
    wait_rows(w, sem)
    values = hidden[...].astype(F32)
    inv = lax.rsqrt(jnp.sum(values * values, axis=1, keepdims=True) * (1.0 / D) + EPSILON)
    mean = 0.0
    for j in range(D // WIDE):
        at = slice(j * WIDE, (j + 1) * WIDE)
        part = dot_nt(grad_low, p_in[at, :]) + dot_nt(raw[...], w[at, :])
        normed = hidden[:, at].astype(F32) * inv
        product = part * normed
        grad_gain[:, at] = jnp.sum(product, axis=0, keepdims=True)
        mean = mean + jnp.sum(product * gain[:, at], axis=1, keepdims=True)
        back[:, at] = part
    mean = mean * (1.0 / D)
    grad_tokens[...] = grad_residual[...] + inv * (
        back[...] * gain[...] - values * inv * mean
    )


def inputs_back(w, raws, p_in, p_out, low, x, hidden, gain, grad_residual):
    length = x.shape[0]
    shapes = (
        jax.ShapeDtypeStruct((length, D), F32),
        jax.ShapeDtypeStruct((1, D), F32),
        jax.ShapeDtypeStruct((LOW, D), F32),
        jax.ShapeDtypeStruct((LOW, QKV), F32),
    )
    rest = (*raws, p_in, p_out, low, x, hidden, gain, grad_residual)
    return pl.pallas_call(
        functools.partial(inputs_back_kernel, counts=w.shapes(), size=w.size),
        grid=(1,),
        in_specs=[SCALARS] + [ANYWHERE] * len(w.blocks) + [whole(a) for a in rest],
        out_specs=[whole(v) for v in shapes],
        out_shape=shapes,
        scratch_shapes=[
            pltpu.VMEM((D, QKV), BF16),
            pltpu.VMEM((length, QKV), BF16),
            pltpu.VMEM((length, D), F32),
            pltpu.SemaphoreType.DMA,
        ],
        compiler_params=pltpu.CompilerParams(vmem_limit_bytes=VMEM_LIMIT),
        cost_estimate=pl.CostEstimate(
            flops=2 * length * D * QKV, bytes_accessed=2 * D * QKV, transcendentals=0
        ),
        name="inputs_back",
    )(w.places, *w.blocks, *rest)


def mlp_kernel(place_ref, *refs, rows, paired, tile, own, carried_in):
    n = len(rows[0]) + len(rows[1])
    tokens, refs = refs[:n], refs[n:]
    own_gu, own_dn = refs[:2]
    pair, refs = (refs[2], refs[3:]) if paired else (None, refs[2:])
    sums, refs = (refs[:2], refs[2:]) if carried_in else (None, refs)
    results, (h, c, gu, dn, out, back, row_sem, gu_sem, dn_sem) = refs[:-9], refs[-9:]
    n_out = h.shape[0] // results[0].shape[0]
    step, steps = pl.program_id(0), pl.num_programs(0)
    own_tiles = own_gu.shape[2] // tile if own else 0

    def fetch(n, slot):
        @pl.when(n < own_tiles)
        def _():
            at = pl.ds(pl.multiple_of(n * tile, tile), tile)
            pltpu.make_async_copy(own_gu.at[:, :, at], gu.at[slot], gu_sem.at[slot]).start()
            pltpu.make_async_copy(own_dn.at[at, :], dn.at[slot], dn_sem.at[slot]).start()

        if not paired:
            return

        @pl.when(n >= own_tiles)
        def _():
            first = (n - own_tiles) * tile
            at = pl.ds(pl.multiple_of(first, tile), tile)
            width = pair.shape[1] // 3
            row = pl.ds(pl.multiple_of(2 * width + first % width, tile), tile)
            column = pl.ds(pl.multiple_of(first // width * width, width), width)
            for k in range(D // width):
                part = pair.at[2 * k + place_ref[0]]
                there = slice(k * width, (k + 1) * width)
                for i in range(2):
                    pltpu.make_async_copy(
                        part.at[i * width : (i + 1) * width, at],
                        gu.at[slot, i, there, :],
                        gu_sem.at[slot],
                    ).start()
                pltpu.make_async_copy(
                    part.at[row, column], dn.at[slot, :, there], dn_sem.at[slot]
                ).start()

    @pl.when(step == 0)
    def _():
        fetch(step, 0)
        copies = []
        for target, sizes in zip((h, c), rows):
            at = 0
            for size in sizes:
                i = len(copies)
                there = target.at[at : at + size]
                copies.append(pltpu.make_async_copy(tokens[i], there, row_sem.at[i]))
                at += size
        for copy in copies:
            copy.start()
        if carried_in:
            for i, target in enumerate((out, back)):
                copies.append(pltpu.make_async_copy(sums[i], target, row_sem.at[len(copies)]))
                copies[-1].start()
        else:
            out[...] = jnp.zeros_like(out)
            back[...] = jnp.zeros_like(back)
        for copy in copies:
            copy.wait()

    slot = step % 2

    @pl.when(step + 1 < steps)
    def _():
        fetch(step + 1, 1 - slot)

    pltpu.make_async_copy(own_gu.at[:, :, pl.ds(0, tile)], gu.at[slot], gu_sem.at[slot]).wait()
    pltpu.make_async_copy(own_dn.at[pl.ds(0, tile), :], dn.at[slot], dn_sem.at[slot]).wait()
    w_gate, w_up, w_down = gu.at[slot, 0], gu.at[slot, 1], dn.at[slot]
    gate = dot_nn(h[...], w_gate[...])
    up = dot_nn(h[...], w_up[...])
    grad = dot_nt(c[...], w_down[...])
    sig = jax.nn.sigmoid(gate)
    silu = gate * sig
    act = (silu * up).astype(BF16)
    grad_gate = (grad * up * sig * (1.0 + gate * (1.0 - sig))).astype(BF16)
    grad_up = (grad * silu).astype(BF16)
    out[...] += dot_nn(act, w_down[...])
    back[...] += dot_nt(grad_gate, w_gate[...]) + dot_nt(grad_up, w_up[...])

    @pl.when(step == steps - 1)
    def _():
        for total, blocks in ((out, results[:n_out]), (back, results[n_out:])):
            size = blocks[0].shape[0]
            for i, ref in enumerate(blocks):
                ref[...] = total[i * size : (i + 1) * size].astype(ref.dtype)


def mlp(second, cot, own_gu, own_dn, pair=None, place=None, own=True, sums=(), split=None):
    rows = tuple(v.shape[0] for v in second), tuple(v.shape[0] for v in cot)
    total = sum(rows[0])
    hidden = own_gu.shape[2]
    tile = min(256, hidden)
    shards = own + (pair is not None)
    kind = F32 if pair is None else BF16
    if pair is None:
        place = jnp.zeros((1,), jnp.int32)
    blocks = [n for n in split or (total, total) for _ in range(total // n)]
    arrays = (*second, *cot, own_gu, own_dn, *(() if pair is None else (pair,)), *sums)
    return pl.pallas_call(
        functools.partial(
            mlp_kernel,
            rows=rows,
            paired=pair is not None,
            tile=tile,
            own=own,
            carried_in=bool(sums),
        ),
        grid_spec=pltpu.PrefetchScalarGridSpec(
            num_scalar_prefetch=1,
            grid=(shards * hidden // tile,),
            in_specs=[ANYWHERE] * len(arrays),
            out_specs=[pl.BlockSpec((n, D), lambda i, p: (0, 0)) for n in blocks],
            scratch_shapes=[
                pltpu.VMEM((total, D), BF16),
                pltpu.VMEM((total, D), BF16),
                pltpu.VMEM((2, 2, D, tile), BF16),
                pltpu.VMEM((2, tile, D), BF16),
                pltpu.VMEM((total, D), F32),
                pltpu.VMEM((total, D), F32),
                pltpu.SemaphoreType.DMA((len(second) + len(cot) + len(sums),)),
                pltpu.SemaphoreType.DMA((2,)),
                pltpu.SemaphoreType.DMA((2,)),
            ],
        ),
        out_shape=[jax.ShapeDtypeStruct((n, D), kind) for n in blocks],
        compiler_params=pltpu.CompilerParams(vmem_limit_bytes=VMEM_LIMIT),
        cost_estimate=pl.CostEstimate(
            flops=12 * total * D * hidden * shards,
            bytes_accessed=6 * D * hidden * shards,
            transcendentals=0,
        ),
        name="mlp",
    )(place, *arrays)


class Grid:
    def __init__(self):
        self.seq = lax.axis_size("seq")
        self.rows = lax.axis_size("rows")
        self.zs = Z_SIZE
        self.xs = self.rows // Z_SIZE
        self.ys = self.seq // CORES
        s = lax.axis_index("seq")
        r = lax.axis_index("rows")
        self.y, self.c = s // CORES, s % CORES
        self.z, self.x = r // self.xs, r % self.xs
        self.s, self.r = s, r

    def send(self, value, move):
        route = []
        for s in range(self.seq):
            for r in range(self.rows):
                there = move(s // CORES, s % CORES, r // self.xs, r % self.xs)
                if there is not None:
                    y, c, z, x = there
                    target = (y * CORES + c) * self.rows + z * self.xs + x
                    route.append((s * self.rows + r, target))
        return jax.tree.map(lambda v: lax.ppermute(v, ("seq", "rows"), route), value)

    def along_z(self, value, k):
        return self.send(value, lambda y, c, z, x: (y, c, (z + k) % self.zs, x))

    def along_x(self, value, k):
        return self.send(value, lambda y, c, z, x: (y, c, z, (x + k) % self.xs))

    def along_y(self, value, k):
        return self.send(value, lambda y, c, z, x: ((y + k) % self.ys, c, z, x))

    def flip_z(self, value, bit):
        return self.send(value, lambda y, c, z, x: (y, c, z ^ bit, x))

    def flip_core(self, value):
        return self.send(value, lambda y, c, z, x: (y, 1 - c, z, x))

    def flip_x(self, value, bit):
        return self.send(value, lambda y, c, z, x: (y, c, z, x ^ bit))

    def flip_seq(self, value, bit):
        def move(y, c, z, x):
            s = (y * CORES + c) ^ bit
            return (s // CORES, s % CORES, z, x)

        return self.send(value, move)

    def along_seq(self, value, k):
        def move(y, c, z, x):
            s = y * CORES + c + k
            return (s // CORES, s % CORES, z, x) if 0 <= s < self.seq else None

        return self.send(value, move)


def after(values, *events):
    return lax.optimization_barrier((values, *events))[0]


class Gather:
    def __init__(self, grid, *shards):
        self.grid = grid
        self.size = shards[0].shape[0] // grid.seq
        at = grid.s * self.size
        own = [lax.dynamic_slice_in_dim(v, at, self.size, 0) for v in shards]
        self.own = jnp.concatenate(own, axis=1) if len(own) > 1 else own[0]

    def over_z(self):
        grid = self.grid
        pieces = [self.own] + [grid.along_z(self.own, k) for k in range(1, grid.zs)]
        half = grid.zs // 2
        self.halves = [jnp.concatenate(pieces[:half]), jnp.concatenate(pieces[half:])]

    def first(self):
        grid = self.grid
        a, b = self.halves
        self.moved = [
            [grid.along_x(a, k) for k in range(1, grid.xs)],
            [grid.along_y(b, k) for k in range(1, grid.ys)],
        ]

    def second(self):
        grid = self.grid
        a, b = (jnp.concatenate([h, *m]) for h, m in zip(self.halves, self.moved))
        self.blocks = [a, b]
        self.last = [grid.along_y(a, k) for k in range(1, grid.ys)]
        self.last += [grid.along_x(b, k) for k in range(1, grid.xs)]

    def cores(self):
        self.over = [self.grid.flip_core(b) for b in self.blocks]

    def result(self):
        grid = self.grid
        blocks = self.blocks + self.last
        blocks = blocks + self.over + [grid.flip_core(b) for b in self.last]
        places = []
        kzs = range(grid.zs // 2), range(grid.zs // 2, grid.zs)
        a = [(kx, 0, kz) for kx in range(grid.xs) for kz in kzs[0]]
        b = [(0, ky, kz) for ky in range(grid.ys) for kz in kzs[1]]
        moves = a + b
        for k in range(1, grid.ys):
            moves = moves + [(kx, k, kz) for kx, _, kz in a]
        for k in range(1, grid.xs):
            moves = moves + [(k, ky, kz) for _, ky, kz in b]
        for core in range(CORES):
            c = (grid.c + core) % CORES
            for kx, ky, kz in moves:
                z, x, y = (grid.z - kz) % grid.zs, (grid.x - kx) % grid.xs, (grid.y - ky) % grid.ys
                places.append((z * grid.xs + x) * grid.seq + y * CORES + c)
        return Gathered(blocks, jnp.stack(places).astype(jnp.int32), self.size)


def pair_part(grid, gate_up, down):
    part = D // grid.seq
    hidden = down.shape[0]
    size = (1, part, hidden)
    gu = [lax.dynamic_slice(gate_up, (i, grid.s * part, 0), size)[0] for i in range(2)]
    dn = lax.dynamic_slice_in_dim(down, grid.s * part, part, 1)
    dn = jnp.concatenate([dn[i : i + part] for i in range(0, hidden, part)], axis=1)
    return jnp.concatenate([*gu, dn], axis=0)


def gather_pair(grid, part):
    groups = []
    for z in range(0, grid.zs, 2):
        for x in range(grid.xs):
            rows = [(z + i) * grid.xs + x for i in range(2)]
            groups.append([s * grid.rows + r for s in range(grid.seq) for r in rows])
    parts = lax.all_gather(part, ("seq", "rows"), axis_index_groups=groups)
    return parts, (1 - grid.z % 2).reshape(1).astype(jnp.int32)


def spread_near(grid, block):
    return [block] + [grid.along_x(block, k) for k in range(1, grid.xs)]


def spread_far(grid, block, parts):
    size = block.shape[0] // parts
    return [grid.flip_z(block[p * size : (p + 1) * size], NEAR_BIT) for p in range(parts)]


def relay(grid, pieces):
    moved = [grid.along_x(piece, k) for k in range(1, grid.xs) for piece in pieces]
    return list(pieces) + moved


def collect_near(grid, near, length):
    return [near[0]] + [grid.along_x(near[k], -k) for k in range(1, grid.xs)]


def collect_far(grid, far, length, parts):
    send, total = [], None
    for p in range(parts):
        far = after(far, total)
        total = far[p]
        for k in range(1, grid.xs):
            other = grid.along_x(far[k * parts + p], -k)
            total = (total.astype(F32) + other.astype(F32)).astype(BF16)
        send.append(total)
    return send


def total_over_all(grid, values):
    widths = [v.shape[2] for v in values]
    packed = jnp.concatenate([v.astype(BF16) for v in values], axis=2)
    packed = jnp.pad(packed, ((0, 0), (0, 0), (0, -packed.shape[2] % FEAT)))
    chunk = lambda i: lax.dynamic_index_in_dim(packed, i, 0, False)
    total = chunk(grid.s).astype(F32)
    for k in range(1, grid.seq):
        total = total + grid.flip_seq(chunk(grid.s ^ k), k).astype(F32)
    for flip, count in ((grid.flip_z, grid.zs), (grid.flip_x, grid.xs)):
        mine = total.astype(BF16)
        terms = [mine.astype(F32)] + [flip(mine, k).astype(F32) for k in range(1, count)]
        while len(terms) > 1:
            terms = [a + b for a, b in zip(terms[::2], terms[1::2])]
        total = terms[0]
    out, at = [], 0
    for w in widths:
        out.append(total[:, at : at + w])
        at += w
    return out


def pair_maps(maps):
    both = jnp.concatenate([maps, -maps], axis=-1)
    both = both.reshape(-1, 2, HEAD, FEAT)
    none = jnp.zeros_like(both[:, 0])
    return jnp.concatenate(
        [
            jnp.concatenate([both[:, 0], none], axis=-1),
            jnp.concatenate([none, both[:, 1]], axis=-1),
        ],
        axis=1,
    )


def adapters(query, key, value, axis):
    if axis == 1:
        joined = jnp.concatenate([query, key, value], axis=1)
        return jnp.pad(joined, ((0, 0), (0, LOW - joined.shape[1])))
    rank = query.shape[0]
    joined = jnp.zeros((LOW, QKV), query.dtype)
    joined = joined.at[:rank, :D].set(query)
    joined = joined.at[rank : 2 * rank, D : D + KVD].set(key)
    return joined.at[2 * rank : 3 * rank, D + KVD :].set(value)


def documents(grid, starts, length):
    own = starts.astype(BF16)
    other = grid.flip_core(own)
    chip = jnp.where(grid.c == 0, jnp.concatenate([own, other]), jnp.concatenate([other, own]))
    resets = jnp.zeros((grid.ys, chip.shape[0]), BF16)
    resets = lax.dynamic_update_slice(resets, chip[None], (grid.y, 0))
    for k in range(1, grid.ys):
        got = grid.along_y(chip, k)
        resets = lax.dynamic_update_slice(resets, got[None], ((grid.y - k) % grid.ys, 0))
    heard = resets
    resets = resets.reshape(-1).astype(jnp.int32)
    places = jnp.arange(resets.shape[0], dtype=jnp.int32)
    docs = jnp.cumsum(jnp.where(places == 0, 1, resets))
    padded = jnp.concatenate([jnp.full((WINDOW,), -1, jnp.int32), docs])
    extended = lax.dynamic_slice_in_dim(padded, grid.s * length, length + WINDOW, 0)
    own = extended[WINDOW:]
    before = extended[WINDOW - 1]
    last = own[-1]
    ends = docs[length - 1 :: length]
    places = jnp.arange(grid.seq, dtype=jnp.int32)
    tiles = jnp.tile(extended.reshape(-1, 1, WINDOW), (1, GROUPS, 1)).reshape(-1, WIDE)
    masks = dict(
        qdoc=own[:, None],
        kdoc=jnp.pad(tiles, ((0, 8 - tiles.shape[0]), (0, 0))),
        fresh=(own == before).astype(F32)[:, None],
        survive=(own == last).astype(F32)[:, None],
    )
    earlier = ((ends == before) & (places < grid.s)).astype(F32)
    entered = jnp.concatenate([jnp.full((1,), -1, jnp.int32), ends[:-1]])
    later = ((entered == last) & (places > grid.s)).astype(F32)
    pick = lambda v, k: lax.dynamic_index_in_dim(v, jnp.clip(grid.s + k, 0, grid.seq - 1), 0, False)
    former = [pick(earlier, -k) * (grid.s - k >= 0) for k in range(1, grid.seq)]
    latter = [pick(later, k) * (grid.s + k < grid.seq) for k in range(1, grid.seq)]
    return masks, former, latter, heard


def local(
    tokens, doc_starts, cotangent, norm_first, norm_second,
    w_query, w_key, w_value, w_out, w_gate_up, w_down,
    query_in, query_out, key_in, key_out, value_in, value_out, proj_in, proj_out,
    map_query, map_key, window_logit,
):
    grid = Grid()
    length = tokens.shape[1]
    rank = query_in.shape[1]
    hidden = tokens[0]
    grad_out = cotangent[0]
    gain_first = norm_first.astype(F32)[None, :]
    gain_second = norm_second.astype(F32)[None, :]

    masks, former, latter, heard = documents(grid, doc_starts[0], length)
    qkv = Gather(grid, w_query, w_key, w_value)
    out = Gather(grid, w_out)
    cot_near = spread_near(grid, grad_out)
    qkv.over_z()

    values = hidden.astype(F32)
    inverse_first = lax.rsqrt(jnp.mean(values * values, axis=-1, keepdims=True) + EPSILON)
    inputs = (values * inverse_first * gain_first).astype(BF16)
    gamma = jax.nn.sigmoid(window_logit)
    masks["gamma"] = jnp.repeat(gamma, HEAD)[None, :]
    half = HEAD // 2
    inverse_freq = jnp.power(THETA, -(jnp.arange(half, dtype=F32) * 2.0 / HEAD))
    places = (grid.s * length + jnp.arange(length, dtype=jnp.int32)).astype(F32)
    angles = places[:, None] * inverse_freq[None, :]
    sine = jnp.sin(angles)
    masks["cos"] = jnp.tile(jnp.cos(angles), (1, WIDE // half))
    masks["sin"] = jnp.tile(jnp.concatenate([-sine, sine], axis=1), (1, WIDE // HEAD))
    maps_q, maps_k = pair_maps(map_query), pair_maps(map_key)
    qkv_in = adapters(query_in, key_in, value_in, 1)
    qkv_out = adapters(query_out, key_out, value_out, 0)
    o_in = jnp.pad(proj_in, ((0, 0), (0, LOW - rank)))
    o_out = jnp.pad(proj_out, ((0, LOW - rank), (0, 0)))
    low = dot_nn(inputs, qkv_in).astype(BF16)

    cot_near, qkv.halves, heard, out.own = after((cot_near, qkv.halves, heard, out.own))
    qkv.first()
    out.over_z()
    ready = (masks, former, latter, maps_q, maps_k, qkv_in, qkv_out, o_in, o_out, inputs, low)
    mine = w_gate_up, w_down
    qkv.moved, out.halves, ready, mine, grad_out = after(
        (qkv.moved, out.halves, ready, mine, grad_out)
    )
    pair = pair_part(grid, *mine)
    masks, former, latter, maps_q, maps_k, qkv_in, qkv_out, o_in, o_out, inputs, low = ready
    cosine, sine = masks["cos"], masks["sin"]
    qkv.second()
    qkv.cores()
    half = length // 2
    cot_far = spread_far(grid, grad_out[:half], 1)
    late = grad_out[half:]
    qkv.last, qkv.over, out.halves, cot_far, late, pair = after(
        (qkv.last, qkv.over, out.halves, cot_far, late, pair)
    )
    pair = gather_pair(grid, pair)
    w_qkv = qkv.result()
    out.first()
    kv, kf, pack, full = project_kv(
        w_qkv, inputs, low, qkv_out[:, D:], cosine, sine, maps_k, masks["survive"]
    )
    kv, kf, pack, full, out.moved, late = after((kv, kf, pack, full, out.moved, late))
    cot_far += spread_far(grid, late, 1)
    rim = grid.along_seq(pack, 1)
    fulls = [grid.along_seq(full, k) for k in range(2, grid.seq)]
    queries = project_q(0, w_qkv, inputs, low, qkv_out, cosine, sine, maps_q)
    rim, fulls, out.moved, queries = after((rim, fulls, out.moved, queries))
    out.second()
    queries = project_q(1, w_qkv, inputs, low, qkv_out, cosine, sine, maps_q, queries)
    carry = former[0] * rim[2 * WINDOW :].astype(F32)
    for w, full in zip(former[1:], fulls):
        carry = carry + w * full.astype(F32)
    carry = carry.astype(BF16)
    block = attend(0, *queries, kv, kf, rim, carry, masks)
    out.blocks, out.last, block, queries, cot_far = after(
        (out.blocks, out.last, block, queries, cot_far)
    )
    out.cores()
    w_o = out.result()
    merged, attended, inverse = attend(1, *queries, kv, kf, rim, carry, masks, block)
    merged, w_o.blocks, cot_far[0] = after((merged, w_o.blocks, cot_far[0]))
    moved = relay(grid, cot_far[:1])[1:]
    residual, second_in, out_low, inverse_second = out_project(
        w_o, merged, hidden, o_in, o_out, gain_second
    )
    second_in, moved = after((second_in, moved))
    near = spread_near(grid, second_in)
    far = spread_far(grid, second_in[:half], 1)
    near, far, late, cot_far = after((near, far, second_in[half:], cot_far))
    others = relay(grid, cot_far[1:])[1:]
    cot_far = cot_far + [v for pieces in zip(moved, others) for v in pieces]
    far += spread_far(grid, late, 1)
    moved = relay(grid, far[:1])[1:]
    sums = mlp(near, cot_near, w_gate_up, w_down)
    sums, far, moved = after((sums, far, moved))
    others = relay(grid, far[1:])[1:]
    far = far + [v for pieces in zip(moved, others) for v in pieces]
    shard = w_gate_up, w_down, *pair
    results = mlp(near, cot_near, *shard, own=False, sums=sums, split=(length, length))
    near_out, near_grad = results[: grid.xs], results[grid.xs :]
    far, near_out, near_grad = after((far, near_out, near_grad))
    results = mlp(far, cot_far, *shard, split=(length, half))
    far_out, far_grad = results[: grid.xs], results[grid.xs :]
    terms = collect_near(grid, near_grad, length)
    far_grad, terms = after((far_grad, terms))
    send = collect_far(grid, far_grad, length, 2)
    near_out, far_out = after((near_out, far_out), send)
    terms.append(jnp.concatenate([grid.flip_z(v, NEAR_BIT) for v in send], axis=0))

    grad_residual, grad_merged, grad_gain_two, grad_proj_in, grad_proj_out = branch_back(
        w_o, terms, grad_out, residual, inverse_second, gain_second, o_in, o_out, merged, out_low
    )
    *scaled, back = scaled_grads(grad_merged, attended, inverse, queries[1], masks)
    out_terms = collect_near(grid, near_out, length)
    send = collect_far(grid, far_out, length, 1)
    back, scaled, out_terms, send = after((back, scaled, out_terms, send))
    out_terms += [grid.flip_z(v, NEAR_BIT) for v in send]
    returned = [grid.along_seq(back, -k) for k in range(1, grid.seq)]
    raw_query, dkv, dkf, rim_back, dmap_query, dlogit = attend_back(
        *queries, kv, kf, rim, carry, *scaled, masks, maps_q
    )
    rim_back = grid.along_seq(rim_back, -1)
    returned, dkv = after((returned, dkv))
    far_back = jnp.zeros(back.shape, F32)
    for w, v in zip(latter[1:], returned[1:]):
        far_back = far_back + w * v.astype(F32)
    near_back = far_back + latter[0] * returned[0].astype(F32)
    near_back, far_back = near_back.astype(BF16), far_back.astype(BF16)
    raw_key, raw_value, dmap_key = keys_back(
        kv, kf, dkv, dkf, rim_back, near_back, far_back, masks, maps_k
    )
    raw_key, out_terms = after((raw_key, out_terms))
    block_out = residual
    for term in out_terms:
        block_out = block_out + term.astype(F32)
    block_out = block_out.astype(BF16)
    grad_tokens, grad_gain_one, grad_qkv_in, grad_qkv_out = inputs_back(
        w_qkv, [raw_query, raw_key, raw_value], qkv_in, qkv_out, low, inputs,
        hidden, gain_first, grad_residual,
    )
    grad_logit = dlogit[:, :GROUPS, 0].reshape(HEADS) * (1.0 - gamma)
    grad_proj_in, grad_proj_out = grad_proj_in[:rank], grad_proj_out[:rank]

    blocks = lambda v: v.reshape(8, grid.seq, -1).swapaxes(0, 1)
    plain = lambda v: v.reshape(grid.seq, 8, -1)
    outs = (
        blocks(grad_qkv_out[:rank, :D]),
        blocks(grad_qkv_out[rank : 2 * rank, D : D + KVD]),
        blocks(grad_qkv_out[2 * rank : 3 * rank, D + KVD :]),
        blocks(grad_proj_out),
    )
    ins = [blocks(grad_qkv_in[i * rank : (i + 1) * rank]) for i in range(3)]
    ins.append(blocks(grad_proj_in))
    map_q = plain(dmap_query[:, :, :HEAD].reshape(HEADS, -1))
    map_k = dmap_key[:, :, :HEAD].reshape(KV_HEADS, grid.seq, -1).swapaxes(0, 1)
    logit = jnp.pad(grad_logit.reshape(grid.seq, -1, 1), ((0, 0), (0, 8 - HEADS // grid.seq), (0, 0)))
    sums = total_over_all(
        grid, [*outs, *ins, map_q, map_k, plain(grad_gain_one), plain(grad_gain_two), logit]
    )
    outs, ins, (map_q, map_k, gain_one, gain_two, logit) = sums[:4], sums[4:8], sums[8:]
    width = D // grid.seq
    return (
        block_out[None],
        grad_tokens[None],
        gain_one.reshape(width),
        gain_two.reshape(width),
        ins[0].T,
        outs[0],
        ins[1].T,
        outs[1],
        ins[2].T,
        outs[2],
        ins[3].T,
        outs[3],
        map_q.reshape(-1, HEAD, HEAD),
        map_k.reshape(KV_HEADS, -1, HEAD),
        logit[: HEADS // grid.seq, 0],
    )


def solution(mesh):
    placed = (
        P("rows", "seq", None),
        P("rows", "seq"),
        P("rows", "seq", None),
        P(),
        P(),
        P("rows", None),
        P("rows", None),
        P("rows", None),
        P("rows", None),
        P(None, None, "rows"),
        P("rows", None),
        P(),
        P(),
        P(),
        P(),
        P(),
        P(),
        P(),
        P(),
        P(),
        P(),
        P(),
    )
    return jax.shard_map(
        local,
        mesh=mesh,
        in_specs=placed,
        out_specs=(
            P("rows", "seq", None),
            P("rows", "seq", None),
            P("seq"),
            P("seq"),
            P("seq", None),
            P(None, "seq"),
            P("seq", None),
            P(None, "seq"),
            P("seq", None),
            P(None, "seq"),
            P("seq", None),
            P(None, "seq"),
            P("seq", None, None),
            P(None, "seq", None),
            P("seq"),
        ),
        check_vma=False,
    )
```
